32 devices in a mesh: graph: 8 (over y, x, core), tm: 4 (over z).
Axes of the slice: x: 2, y: 2, z: 4, core: 2. Of those that a mesh axis runs over, the one named last changes fastest.
Arguments:
- series: bfloat16 [16, 32, 4096], P('tm', None, 'graph'), may hold values from -6 to 6
- convolution_weight: bfloat16 [2, 2, 64, 32], replicated, may hold values from -0.75 to 0.75
- convolution_bias: float32 [2, 64], replicated, may hold values from -3 to 3
- mixing_weight: bfloat16 [2, 5, 32, 32], replicated, may hold values from -0.5 to 0.5
- mix_bias: float32 [2, 32], replicated, may hold values from -3 to 3
- tile_values: bfloat16 [32, 3, 128, 128], P('graph'), may hold values from -0.3125 to 0.3125
- tile_cols: int32 [32, 3], P('graph'), may hold values from 0 to 5
- send_index: int32 [8, 8, 32], P('graph'), may hold values from 0 to 511
- send_mask: int32 [8, 8, 32], P('graph'), may hold values 0 or 1
- cotangent: bfloat16 [16, 32, 4096], P('tm', None, 'graph'), may hold values from -6 to 6
Outputs:
- output: bfloat16 [16, 32, 4096], P('tm', None, 'graph')
- grad_series: bfloat16 [16, 32, 4096], P('tm', None, 'graph')
- grad_conv: float32 [2, 2, 64, 32], replicated
- grad_mix: float32 [2, 5, 32, 32], replicated
The draws below stay inside these ranges and needn't reach their ends.
Inputs may be any that keep to these rules, and one draw needn't show every extreme that they name: `send_index`: a local sensor number of the sending partition; a list may name a sensor more than once. `tile_cols`: blocks below 4 are the partition's own sensors, the others its boundary rows.
All inputs are finite; a program needn't handle non-finite values. No bound on the sum of `send_mask` on one device may be relied on, other than what follows from the above.
Results may differ from the reference program's by a relative error of at most 0.0079.
Values may be sent and summed in bfloat16 or wider, within the bound.
A program may use at most 64 MiB of HBM per device.

```python
import math
import jax
import jax.numpy as jnp
from jax import lax

RESIDUAL_WIDTH = 32
DILATION_WIDTH = 32
TILE = 128
TILES_ROW = 3
GATED_LAYERS = 2
HALO = 256
SENS_DEV = 512
SLOTS = 32
ROW_BLOCKS = 4
COL_BLOCKS = 6
TIMES = 16
SENSORS = 4096
N_GRAPH = 8


def plant(entries, own_key, low, largest):
    place = [jax.random.randint(jax.random.fold_in(own_key, axis), (), 0, length) for axis, length in enumerate(entries.shape)]
    widest = entries.shape.index(max(entries.shape))
    beside = place[:widest] + [(place[widest] + 1) % entries.shape[widest]] + place[widest + 1:]
    return entries.at[tuple(place)].set(low).at[tuple(beside)].set(largest)


def steps_of(own_key, extent, pieces, least, high):
    loudness = 1.0
    for axis_at, shards_of in pieces:
        draws = jax.random.uniform(jax.random.fold_in(jax.random.fold_in(own_key, 6), axis_at), (shards_of,), jnp.float32, least / len(pieces), high / len(pieces))
        loudness = loudness * jnp.repeat(jnp.exp(draws), extent[axis_at] // shards_of).reshape((-1,) + (1,) * (len(extent) - 1 - axis_at))
    return loudness


def normal_values(own_key, extent, deviation, bound, pieces=(), kind=jnp.bfloat16):
    factor_of = steps_of(own_key, extent, pieces, -0.22, 0.18) if pieces else 1.0
    values = jax.random.normal(own_key, extent, jnp.float32) * deviation * factor_of
    return jnp.minimum(jnp.maximum(values, -bound), bound).astype(kind)


def setup_inputs(seed: int = 0) -> dict:
    key_of = jax.random.split(jax.random.key(seed), 11)
    series = normal_values(key_of[0], (TIMES, RESIDUAL_WIDTH, SENSORS), 1.0, 6.0, ((0, 4), (2, 8)))
    convolution_weight = normal_values(key_of[1], (GATED_LAYERS, 2, 2 * DILATION_WIDTH, RESIDUAL_WIDTH), (2 * RESIDUAL_WIDTH) ** -0.5, 0.75)
    convolution_bias = normal_values(key_of[2], (GATED_LAYERS, 2 * DILATION_WIDTH), 0.5, 3.0, (), jnp.float32)
    mixing_weight = normal_values(key_of[3], (GATED_LAYERS, 5, RESIDUAL_WIDTH, DILATION_WIDTH), (5 * DILATION_WIDTH) ** -0.5, 0.5)
    mix_bias = normal_values(key_of[4], (GATED_LAYERS, RESIDUAL_WIDTH), 0.5, 3.0, (), jnp.float32)
    tile_values = normal_values(key_of[5], (N_GRAPH * ROW_BLOCKS, TILES_ROW, TILE, TILE), (TILES_ROW * TILE) ** -0.5, 0.3125, ((0, 8),))
    tile_cols = plant(jax.random.randint(key_of[6], (N_GRAPH * ROW_BLOCKS, TILES_ROW), 0, COL_BLOCKS), jax.random.fold_in(key_of[6], 1), 0, COL_BLOCKS - 1).astype(jnp.int32)
    send_index = plant(jax.random.randint(key_of[7], (N_GRAPH, N_GRAPH, SLOTS), 0, SENS_DEV), jax.random.fold_in(key_of[7], 1), 0, SENS_DEV - 1).astype(jnp.int32)
    send_mask = plant((jax.random.randint(key_of[8], (N_GRAPH, N_GRAPH, SLOTS), 0, 4) < 3).astype(jnp.int32), jax.random.fold_in(key_of[8], 1), 0, 1)
    cotangent = normal_values(key_of[9], (TIMES, RESIDUAL_WIDTH, SENSORS), 1.0, 6.0, ((0, 4), (2, 8)))
    return dict(series=series, convolution_weight=convolution_weight, convolution_bias=convolution_bias, mixing_weight=mixing_weight, mix_bias=mix_bias, tile_values=tile_values, tile_cols=tile_cols, send_index=send_index, send_mask=send_mask, cotangent=cotangent)


def apply_tiles(packed):
    extended, columns, values = packed
    height = extended.shape[0]
    blocks = extended.reshape(height, -1, TILE)
    picked = jnp.take(blocks, columns.reshape(-1), axis=1)
    picked = picked.reshape(height, columns.shape[0], columns.shape[1], TILE)
    result = jnp.einsum('mrkj,rkij->mri', picked.astype(jnp.float32), values.astype(jnp.float32))
    return result.reshape(height, -1)

def spread_tiles(packed):
    rows_in, columns, values = packed
    height = rows_in.shape[0]
    blocks = rows_in.reshape(height, columns.shape[0], TILE)
    contrib = jnp.einsum('mri,rkij->rkmj', blocks.astype(jnp.float32), values.astype(jnp.float32))
    contrib = contrib.reshape(-1, height, TILE)
    totals = jax.ops.segment_sum(contrib, columns.reshape(-1).astype(jnp.int32), num_segments=COL_BLOCKS)
    return totals.transpose(1, 0, 2).reshape(height, -1)

def reference(series, convolution_weight, convolution_bias, mixing_weight, mix_bias, tile_values, tile_cols, send_index, send_mask, cotangent):
    part_count = N_GRAPH
    columns = tile_cols.reshape(part_count, ROW_BLOCKS, TILES_ROW)
    values = tile_values.reshape(part_count, ROW_BLOCKS, TILES_ROW, TILE, TILE)
    indices = send_index.reshape(part_count, HALO).astype(jnp.int32)
    live_rows = send_mask.reshape(part_count, HALO).astype(jnp.float32)

    def to_parts(array):
        return array.reshape(TIMES, array.shape[1], part_count, SENS_DEV).transpose(2, 0, 1, 3)

    def from_parts(array):
        return array.transpose(1, 2, 0, 3).reshape(TIMES, array.shape[2], SENSORS)

    def pull(signal):
        height = signal.shape[1] * signal.shape[2]
        flattened = signal.reshape(part_count, height, SENS_DEV)
        picked = jax.vmap(lambda source, rows_at: jnp.take(source, rows_at, axis=1))(flattened, indices)
        outgoing = picked * live_rows[:, None, :].astype(jnp.bfloat16)
        received = outgoing.reshape(part_count, height, part_count, SLOTS).transpose(2, 1, 0, 3).reshape(part_count, height, HALO)
        extended = jnp.concatenate([flattened, received], axis=2)
        result = lax.map(apply_tiles, (extended, columns, values))
        return result.reshape(signal.shape)

    def push(signal):
        height = signal.shape[1] * signal.shape[2]
        flattened = signal.reshape(part_count, height, SENS_DEV)
        totals = lax.map(spread_tiles, (flattened, columns, values))
        local_part = totals[:, :, :SENS_DEV]
        outgoing = totals[:, :, SENS_DEV:].astype(jnp.bfloat16)
        returned = outgoing.reshape(part_count, height, part_count, SLOTS).transpose(2, 1, 0, 3).reshape(part_count, height, HALO)
        addend = returned.astype(jnp.float32) * live_rows[:, None, :]
        local_part = jax.vmap(lambda target, rows_at, extra_rows: target.at[:, rows_at].add(extra_rows))(local_part, indices, addend)
        return local_part.reshape(signal.shape)

    def delayed(signal, shift_by):
        zero_block = jnp.zeros(signal.shape[:1] + (shift_by,) + signal.shape[2:], signal.dtype)
        return jnp.concatenate([zero_block, signal[:, :signal.shape[1] - shift_by]], axis=1)

    def advanced(signal, shift_by):
        zero_block = jnp.zeros(signal.shape[:1] + (shift_by,) + signal.shape[2:], signal.dtype)
        return jnp.concatenate([signal[:, shift_by:], zero_block], axis=1)

    def channel_mix(matrix, signal):
        return jnp.einsum('oc,ptcn->pton', matrix.astype(jnp.float32), signal.astype(jnp.float32))

    def channel_back(matrix, signal):
        return jnp.einsum('oc,pton->ptcn', matrix.astype(jnp.float32), signal.astype(jnp.float32))

    def outer_sum(left_side, right_side):
        return jnp.einsum('pton,ptcn->oc', left_side.astype(jnp.float32), right_side.astype(jnp.float32))
    hidden = to_parts(series)
    saved = []
    for layer_index in range(GATED_LAYERS):
        dilation = layer_index + 1
        lagged = delayed(hidden, dilation)
        preactivation = channel_mix(convolution_weight[layer_index, 0], hidden) + channel_mix(convolution_weight[layer_index, 1], lagged)
        preactivation = preactivation + convolution_bias[layer_index][None, None, :, None]
        filter_half = jnp.tanh(preactivation[:, :, :DILATION_WIDTH])
        gate_half = jax.nn.sigmoid(preactivation[:, :, DILATION_WIDTH:])
        gated = (filter_half * gate_half).astype(jnp.bfloat16)
        fwd_one = pull(gated).astype(jnp.bfloat16)
        back_one = push(gated).astype(jnp.bfloat16)
        fwd_two = pull(fwd_one).astype(jnp.bfloat16)
        back_two = push(back_one).astype(jnp.bfloat16)
        hop_list = (gated, fwd_one, fwd_two, back_one, back_two)
        mixed_sum = mix_bias[layer_index][None, None, :, None] + jnp.zeros((), jnp.float32)
        for hop_order in range(5):
            mixed_sum = mixed_sum + channel_mix(mixing_weight[layer_index, hop_order], hop_list[hop_order])
        saved.append((hidden, lagged, filter_half, gate_half, hop_list))
        hidden = (hidden.astype(jnp.float32) + mixed_sum).astype(jnp.bfloat16)
    output = from_parts(hidden)
    grad_flow = to_parts(cotangent).astype(jnp.float32)
    conv_list = [None] * GATED_LAYERS
    mix_list = [None] * GATED_LAYERS
    for layer_index in reversed(range(GATED_LAYERS)):
        dilation = layer_index + 1
        hidden, lagged, filter_half, gate_half, hop_list = saved[layer_index]
        flow_round = grad_flow.astype(jnp.bfloat16)
        mix_list[layer_index] = jnp.stack([outer_sum(flow_round, hop_list[hop_order]) for hop_order in range(5)])
        hop_grads = [channel_back(mixing_weight[layer_index, hop_order], flow_round) for hop_order in range(5)]
        fwd_inner = push(hop_grads[2].astype(jnp.bfloat16))
        back_inner = pull(hop_grads[4].astype(jnp.bfloat16))
        fwd_outer = push((hop_grads[1] + fwd_inner).astype(jnp.bfloat16))
        back_outer = pull((hop_grads[3] + back_inner).astype(jnp.bfloat16))
        grad_gated = hop_grads[0] + fwd_outer + back_outer
        grad_filter = grad_gated * gate_half * (1.0 - filter_half * filter_half)
        grad_gate = grad_gated * filter_half * gate_half * (1.0 - gate_half)
        grad_pre = jnp.concatenate([grad_filter, grad_gate], axis=2).astype(jnp.bfloat16)
        conv_list[layer_index] = jnp.stack([outer_sum(grad_pre, hidden), outer_sum(grad_pre, lagged)])
        lag_term = channel_back(convolution_weight[layer_index, 1], grad_pre)
        grad_flow = grad_flow + channel_back(convolution_weight[layer_index, 0], grad_pre) + advanced(lag_term, dilation)
    norm_scale = 1.0 / math.sqrt(float(TIMES * SENSORS))
    grad_conv = jnp.stack(conv_list) * norm_scale
    grad_mix = jnp.stack(mix_list) * norm_scale
    return (output, from_parts(grad_flow).astype(jnp.bfloat16), grad_conv, grad_mix)
```

```python
import functools
import math

import jax
import jax.numpy as jnp
from jax import lax
from jax.experimental import pallas as pl
from jax.experimental.pallas import tpu as pltpu
from jax.sharding import PartitionSpec as P

GATED_LAYERS = 2
HOPS = 5
BF = jnp.bfloat16
F32 = jnp.float32
MESH = pl.DeviceIdType.MESH


def dot(a, b):
    return lax.dot_general(a, b, (((1,), (0,)), ((), ())), preferred_element_type=F32)


def dot_nt(a, b):
    return lax.dot_general(a, b, (((1,), (1,)), ((), ())), preferred_element_type=F32)


def dot_tn(a, b):
    return lax.dot_general(a, b, (((0,), (0,)), ((), ())), preferred_element_type=F32)


def quot(x, n):
    return x >> (n.bit_length() - 1) if n & (n - 1) == 0 else x // n


def rest_of(x, n):
    return x & (n - 1) if n & (n - 1) == 0 else lax.rem(x, n)


def peers(count, body):
    if count <= 8:
        for off in range(count - 1, 0, -1):
            body(off)
    elif count > 1:
        lax.fori_loop(1, count, lambda off, c: (body(off), c)[1], 0)


def kernel(
    n_graph, n_tm, steps, scale,
    series_h, cw_h, cb_h, mw_h, mb_h, tv_h, tcol, sidx_h, smask_h, cot_h,
    out, gser, gconv, gmix,
    wl, wlt, wh, wht, gm, gmt, band, band_h, mixall, mix_h, ext, hops, hops_h, filt, gate, flow,
    prev0, pack_s, pack_r, send, recv, send_w, recv_w, e_buf, et_buf, l_buf, lt_buf,
    e_part, eg_buf, series, cw, cb, mw, mb, tv, sidx, smask, cot, in_sem,
    r_ssem, r_rsem, w_ssem, w_rsem, t_ssem, t_rsem, e_ssem, e_rsem, et_ssem, et_rsem,
    l_ssem, l_rsem, lt_ssem, lt_rsem, eg_ssem, eg_rsem,
):
    me = lax.axis_index("graph")
    z = lax.axis_index("tm")
    tc, sensors = series.shape
    ch = tc // steps
    half = tc // 2
    half_s = sensors // 2
    slots = sidx.shape[1]
    halo = n_graph * slots
    tile = tv.shape[-1]
    rblocks, tslots = tcol.shape
    lblocks = sensors // tile
    hblocks = halo // tile
    wire = send.dtype

    def partner(off):
        if n_graph & (n_graph - 1) or n_graph > 8:
            return lax.rem(me + off, n_graph)
        p = 0
        bit = 1
        while bit < n_graph:
            p = p + lax.rem(me // bit + off // bit, 2) * bit
            bit *= 2
        return p

    er = e_part.shape[1]

    loads = [
        pltpu.make_async_copy(src, dst, in_sem.at[i])
        for i, (src, dst) in enumerate(
            ((cw_h, cw), (mw_h, mw), (cb_h, cb), (mb_h, mb), (tv_h, tv), (series_h, series),
             (sidx_h, sidx), (smask_h, smask), (cot_h, cot))
        )
    ]
    for load in loads:
        load.start()
    barrier = pltpu.get_barrier_semaphore()

    def greet_graph(off):
        pl.semaphore_signal(barrier, inc=1, device_id={"graph": partner(off)}, device_id_type=MESH)

    def greet_tm(off):
        pl.semaphore_signal(barrier, inc=1, device_id={"tm": lax.rem(z + off, n_tm)}, device_id_type=MESH)

    peers(n_graph, greet_graph)
    peers(n_tm, greet_tm)

    def shift_copy(slot, src, dst, by):
        return pltpu.make_async_remote_copy(
            src_ref=src, dst_ref=dst, send_sem=t_ssem.at[slot], recv_sem=t_rsem.at[slot],
            device_id={"tm": lax.rem(z + by + n_tm, n_tm)}, device_id_type=MESH,
        )

    up = z < n_tm - 1
    down = z > 0

    firsts = [
        shift_copy(0, series_h.at[pl.ds(tc - ch, ch)], prev0.at[pl.ds(tc - ch, ch)], 1),
        shift_copy(1, series_h.at[pl.ds(tc - 3 * ch, 2 * ch)], prev0.at[pl.ds(tc - 3 * ch, 2 * ch)], 1),
    ]
    prev0[pl.ds(0, tc - 3 * ch), :] = jnp.zeros((tc - 3 * ch, sensors), BF)

    row32 = lax.broadcasted_iota(jnp.int32, (ch, tc), 0)
    lane32 = lax.broadcasted_iota(jnp.int32, (ch, tc), 1)
    spread = jnp.where(rest_of(lane32, ch) == row32, 1.0, 0.0)
    spread_b = spread.astype(BF)
    rt = lax.broadcasted_iota(jnp.int32, (tc, tc), 0)
    lt = lax.broadcasted_iota(jnp.int32, (tc, tc), 1)
    rt, lt = quot(rt, ch), quot(lt, ch)
    same = rt == lt
    late = rt >= steps // 2

    def before(d):
        return lt == rt - d

    def before_prev(d):
        return lt == rt - d + steps

    for load in loads[:4]:
        load.wait()
    taps = 2 * GATED_LAYERS
    rs = lax.broadcasted_iota(jnp.int32, (taps * ch, taps * tc), 0)
    ls = lax.broadcasted_iota(jnp.int32, (taps * ch, taps * tc), 1)
    spread_taps = jnp.where(quot(ls, tc) * ch + rest_of(ls, ch) == rs, 1.0, 0.0).astype(BF)
    def after(d):
        return rt == lt - d

    def after_prev(d):
        return rt == lt - d + steps

    cwr = dot_tn(cw[...], spread_taps)
    mwr = dot(mw[...], spread_b)

    def stack(x, base):
        return jnp.concatenate([x[base:base + ch]] * steps, axis=0)

    for l in range(GATED_LAYERS):
        d = l + 1
        for h in range(2):
            w0 = stack(cwr[:, (l * 2) * tc:(l * 2 + 1) * tc], h * ch)
            w1 = stack(cwr[:, (l * 2 + 1) * tc:(l * 2 + 2) * tc], h * ch)
            own = (jnp.where(same, w0, 0.0) + jnp.where(before(d), w1, 0.0)).astype(BF)
            band[l, pl.ds(h * tc, tc), pl.ds(0, tc)] = own
            band[l, pl.ds(h * tc, tc), pl.ds(tc, tc)] = jnp.where(before_prev(d), w1, 0.0).astype(BF)
            if l == 0:
                band_h[pl.ds(h * tc, tc), :] = jnp.concatenate([own[half:], own[half:]], axis=0)
        for k in range(HOPS):
            mk = stack(mwr, (l * HOPS + k) * ch)
            mixall[l, :, pl.ds(k * tc, tc)] = jnp.where(same, mk, 0.0).astype(BF)
            if l == 0:
                at = (rt == lt + steps // 2) if k in (1, 2) else (same & late)
                mix_h[:, pl.ds(k * tc, tc)] = jnp.where(at, mk, 0.0).astype(BF)

    r64 = lax.broadcasted_iota(jnp.int32, (2 * ch, 2 * tc), 0)
    l64 = lax.broadcasted_iota(jnp.int32, (2 * ch, 2 * tc), 1)
    spread2 = jnp.where(rest_of(l64, ch) + quot(l64, tc) * ch == r64, 1.0, 0.0)
    cbias = lax.dot_general(cb[...], spread2, (((1,), (0,)), ((), ())), precision=lax.Precision.HIGHEST, preferred_element_type=F32)
    mbias = lax.dot_general(mb[...], spread, (((1,), (0,)), ((), ())), precision=lax.Precision.HIGHEST, preferred_element_type=F32)

    pl.semaphore_wait(barrier, n_graph - 1 + n_tm - 1)

    @pl.when(up)
    def _():
        for first in firsts:
            first.start()

    for load in loads[4:]:
        load.wait()
    for r in range(rblocks):
        tiles = [tv[r * tslots + k].astype(F32) for k in range(tslots)]
        flips = [t.T for t in tiles]
        for c in range(lblocks + hblocks):
            a = jnp.zeros((tile, tile), F32)
            b = jnp.zeros((tile, tile), F32)
            for k in range(tslots):
                on = (tcol[r, k] == c).astype(jnp.int32).astype(F32)
                a = a + tiles[k] * on
                b = b + flips[k] * on
            a = a.astype(BF)
            b = b.astype(BF)
            if c < lblocks:
                wl[pl.ds(r * tile, tile), pl.ds(c * tile, tile)] = a
                wlt[pl.ds(c * tile, tile), pl.ds(r * tile, tile)] = b
            else:
                ch_at = c - lblocks
                wh[pl.ds(r * tile, tile), pl.ds(ch_at * tile, tile)] = a
                wht[pl.ds(ch_at * tile, tile), pl.ds(r * tile, tile)] = b

    key = jnp.where(smask[...] != 0, sidx[...] + 1, 0)
    es = lax.broadcasted_iota(jnp.int32, (slots, halo), 0)
    ej = lax.broadcasted_iota(jnp.int32, (slots, halo), 1)
    pick = jnp.where(rest_of(ej, slots) == es, 1.0, 0.0).astype(BF)
    hi = dot((key >> 5).astype(F32).astype(BF), pick)
    lo = dot((key & 31).astype(F32).astype(BF), pick)
    pr = lax.broadcasted_iota(jnp.int32, (n_graph, halo), 0)
    pj = quot(lax.broadcasted_iota(jnp.int32, (n_graph, halo), 1), slots)
    keys = jnp.sum(jnp.where(pr == pj, hi * 32.0 + lo, 0.0), axis=0, keepdims=True)
    ids = lax.broadcasted_iota(jnp.int32, (sensors, halo), 0).astype(F32) + 1.0
    onehot = jnp.where(ids == keys, 1.0, 0.0)
    gm[...] = onehot.astype(BF)
    gmt[...] = onehot.T.astype(BF)

    def graph_copy(src, dst, ssem, rsem, p):
        return pltpu.make_async_remote_copy(
            src_ref=src, dst_ref=dst, send_sem=ssem, recv_sem=rsem,
            device_id={"graph": p}, device_id_type=MESH,
        )

    def tm_copy(src, dst, ssem, rsem, p):
        return pltpu.make_async_remote_copy(
            src_ref=src, dst_ref=dst, send_sem=ssem, recv_sem=rsem,
            device_id={"tm": p}, device_id_type=MESH,
        )

    lane_low = lax.broadcasted_iota(jnp.int32, (halo, tc), 1) < half

    def ship(blocks, out_buf, in_buf, ssem, rsem, r):
        for i, block in enumerate(blocks):
            out_buf[r, :, i] = block.astype(BF).reshape(n_graph, slots, tc).astype(wire)

        def go(off):
            p = partner(off)
            graph_copy(out_buf.at[r, p], in_buf.at[r, me], ssem.at[r, p], rsem.at[r], p).start()

        peers(n_graph, go)
        in_buf[r, me] = out_buf[r, me]

    def collect(in_buf, ssem, rsem, r, count):
        arrived = in_buf.at[r, pl.ds(0, n_graph - 1)]
        graph_copy(arrived, arrived, ssem.at[r, 0], rsem.at[r], partner(1)).wait_recv()
        return [in_buf[r, :, i].reshape(halo, tc).astype(BF) for i in range(count)]

    def launch(r, pull_in, push_in):
        ship((dot(gmt[...], pull_in), dot(wht[...], push_in)), send, recv, r_ssem, r_rsem, r)

    def launch_w(r, pull_in, push_in):
        sp = dot(gmt[...], pull_in)
        sb = dot(wht[...], push_in)
        packed = jnp.where(lane_low, sp[:, tc:], sb[:, tc:])
        ship((sp[:, :tc], sb[:, :tc], packed), send_w, recv_w, w_ssem, w_rsem, r)

    def local(pull_in, push_in):
        return dot(wl[...], pull_in), dot(wlt[...], push_in)

    def land(r, pulled, pushed):
        rp, rb = collect(recv, r_ssem, r_rsem, r, 2)
        return pulled + dot(wh[...], rp), pushed + dot(gm[...], rb)

    def land_w(r, pulled, pushed):
        rp, rb, both = collect(recv_w, w_ssem, w_rsem, r, 3)
        rp = jnp.concatenate([rp, both], axis=1)
        rb = jnp.concatenate([rb, both], axis=1)
        return pulled + dot(wh[...], rp), pushed + dot(gm[...], rb)

    lane_half = lax.broadcasted_iota(jnp.int32, (half_s, tc), 1) < half

    def pack(x):
        return jnp.where(lane_half, pltpu.roll(x[:half_s], half, 1), x[half_s:]).astype(BF)

    def unpack(p):
        x = p.astype(F32)
        return jnp.concatenate([pltpu.roll(x, half, 1), x], axis=0)

    lane_g = quot(lax.broadcasted_iota(jnp.int32, (ch, tc), 1), ch)

    def fold(x):
        y = x[0:ch]
        for t in range(1, steps):
            y = y + x[t * ch:(t + 1) * ch]
        sh = ch
        while sh < tc:
            y = y + pltpu.roll(y, sh, 1)
            sh *= 2
        return y

    def lanes_of(xs):
        y = jnp.zeros((ch, tc), F32)
        for g, x in enumerate(xs):
            y = jnp.where(lane_g == g, x, y)
        return y

    def gather_start(buf, ssem, rsem, count, here, copy):
        def go(off):
            p = lax.rem(here + off, count)
            copy(buf.at[here], buf.at[here], ssem.at[p], rsem.at[here], p).start()

        peers(count, go)

    def gather_sum(buf, ssem, rsem, count, here, copy):
        def take(off):
            p = lax.rem(here + off, count)
            copy(buf.at[p], buf.at[p], ssem.at[p], rsem.at[p], p).wait_recv()

        peers(count, take)
        total = buf[0]
        for p in range(1, count):
            total = total + buf[p]
        return total

    def hop_grad(fr, l, k):
        return dot(fr, mixall[l, :, pl.ds(k * tc, tc)])

    def mix_fold(fr, l):
        prod = dot_tn(fr, hops[l])
        return [fold(jnp.where(same, prod[:, k * tc:(k + 1) * tc], 0.0)) for k in range(HOPS)]

    def conv_fold(l, gp):
        d = l + 1
        prod = dot_tn(ext[l], gp)
        pieces = []
        for tap in range(2):
            for h in range(2):
                own = prod[:tc, h * tc:(h + 1) * tc]
                if tap == 0:
                    x = jnp.where(same, own, 0.0)
                else:
                    x = jnp.where(after(d), own, 0.0) + jnp.where(after_prev(d), prod[tc:, h * tc:(h + 1) * tc], 0.0)
                pieces.append(fold(x))
        return lanes_of(pieces)

    def pre_grad(l, gg):
        f = filt[l]
        g = gate[l]
        return jnp.concatenate([gg * g * (1.0 - f * f), gg * f * g * (1.0 - g)], axis=1).astype(BF)

    def lag_start(i, l, gp):
        pack_s[i] = pack(dot(gp, band[l, :, pl.ds(tc, tc)]))

        @pl.when(down)
        def _():
            shift_copy(2 + i, pack_s.at[i], pack_r.at[i], -1).start()

    lanes_late = lax.broadcasted_iota(jnp.int32, (sensors, tc), 1) >= half

    def lag_take(i):
        @pl.when(up)
        def _():
            shift_copy(2 + i, pack_s.at[i], pack_r.at[i], -1).wait_recv()

        @pl.when(jnp.logical_not(up))
        def _():
            pack_r[i] = jnp.zeros((half_s, tc), BF)

        return jnp.where(lanes_late, unpack(pack_r[i]), 0.0)

    flow[...] = cot[...].astype(F32).T
    fr1 = flow[...].astype(BF)
    h4, h2 = hop_grad(fr1, 1, 4).astype(BF), hop_grad(fr1, 1, 2).astype(BF)
    launch(0, h4, h2)
    ab = local(h4, h2)

    ext[0, :, pl.ds(0, tc)] = series[...].astype(F32).T.astype(BF)

    @pl.when(down)
    def _():
        for first in firsts:
            first.wait_recv()

    @pl.when(jnp.logical_not(down))
    def _():
        prev0[pl.ds(tc - 3 * ch, 3 * ch), :] = jnp.zeros((3 * ch, sensors), BF)

    prev_t = prev0[...].astype(F32).T
    ext[0, :, pl.ds(tc, tc)] = prev_t.astype(BF)
    pre = dot_nt(ext[0], band[0]) + cbias[0:1]
    f = jnp.tanh(pre[:, :tc])
    g = jax.nn.sigmoid(pre[:, tc:])
    filt[0] = f
    gate[0] = g
    gated = (f * g).astype(BF)
    pre = dot_nt(ext[0, :, pl.ds(tc, tc)], band_h[...]) + cbias[0:1]
    gated_h = (jnp.tanh(pre[:, :tc]) * jax.nn.sigmoid(pre[:, tc:])).astype(BF)
    both = jnp.concatenate([gated, gated_h], axis=1)
    launch_w(0, both, both)

    def keep(k, x):
        hops[0, :, pl.ds(k * tc, tc)] = x[:, :tc]
        hops_h[:, pl.ds(k * tc, tc)] = x[:, tc:]

    keep(0, both)
    af = local(both, both)

    bi, fi = land(0, *ab)
    bi = (hop_grad(fr1, 1, 3) + bi).astype(BF)
    fi = (hop_grad(fr1, 1, 1) + fi).astype(BF)
    launch(1, bi, fi)
    bb = local(bi, fi)
    gg0 = hop_grad(fr1, 1, 0)

    fo, bo = land_w(0, *af)
    fo, bo = fo.astype(BF), bo.astype(BF)
    launch_w(1, fo, bo)
    keep(1, fo)
    keep(3, bo)
    bf = local(fo, bo)

    def mix_three(mat, hop):
        m = dot_nt(hop(0, 2), mat(0, 2))
        return m + dot_nt(hop(3, 1), mat(3, 1))

    def mat_of(l):
        return lambda k, n: mixall[l, :, pl.ds(k * tc, n * tc)]

    def hop_of(l):
        return lambda k, n: hops[l, :, pl.ds(k * tc, n * tc)]

    part = mix_three(mat_of(0), hop_of(0))
    part_h = mix_three(
        lambda k, n: mix_h[:, pl.ds(k * tc, n * tc)], lambda k, n: hops_h[:, pl.ds(k * tc, n * tc)]
    )

    bi, fi = land(1, *bb)
    gg1 = gg0 + fi + bi

    f2, b2 = land_w(1, *bf)
    f2, b2 = f2.astype(BF), b2.astype(BF)
    keep(2, f2)
    keep(4, b2)
    mixed = part + dot_nt(f2[:, :tc], mixall[0, :, pl.ds(2 * tc, tc)]) + dot_nt(b2[:, :tc], mixall[0, :, pl.ds(4 * tc, tc)])
    mixed_h = part_h + dot_nt(f2[:, tc:], mix_h[:, pl.ds(2 * tc, tc)]) + dot_nt(b2[:, tc:], mix_h[:, pl.ds(4 * tc, tc)])
    ext[1, :, pl.ds(0, tc)] = (ext[0, :, pl.ds(0, tc)].astype(F32) + (mixed + mbias[0:1])).astype(BF)
    hid_h = ext[0, :, pl.ds(tc, tc)].astype(F32) + (mixed_h + mbias[0:1])
    ext[1, :, pl.ds(tc, tc)] = jnp.where(lanes_late & down, hid_h, 0.0).astype(BF)

    pre = dot_nt(ext[1], band[1]) + cbias[1:2]
    f = jnp.tanh(pre[:, :tc])
    g = jax.nn.sigmoid(pre[:, tc:])
    filt[1] = f
    gate[1] = g
    gp1 = pre_grad(1, gg1)
    lag_start(0, 1, gp1)
    gated = (f * g).astype(BF)
    hops[1, :, pl.ds(0, tc)] = gated
    launch(2, gated, gated)
    cf = local(gated, gated)
    new = flow[...] + dot(gp1, band[1, :, pl.ds(0, tc)])
    conv1 = conv_fold(1, gp1)

    flow[...] = new + lag_take(0)
    fr0 = flow[...].astype(BF)
    h4, h2 = hop_grad(fr0, 0, 4).astype(BF), hop_grad(fr0, 0, 2).astype(BF)
    launch(4, h4, h2)
    cb_ = local(h4, h2)
    rest1, rest3 = hop_grad(fr0, 0, 1), hop_grad(fr0, 0, 3)

    fo, bo = land(2, *cf)
    fo, bo = fo.astype(BF), bo.astype(BF)
    launch(3, fo, bo)
    hops[1, :, pl.ds(tc, tc)] = fo
    hops[1, :, pl.ds(3 * tc, tc)] = bo
    df = local(fo, bo)
    gg0 = hop_grad(fr0, 0, 0)
    mix0 = mix_fold(fr0, 0)
    part = mix_three(mat_of(1), hop_of(1))

    bi, fi = land(4, *cb_)
    bi = (rest3 + bi).astype(BF)
    fi = (rest1 + fi).astype(BF)
    launch(5, bi, fi)
    db = local(bi, fi)

    f2, b2 = land(3, *df)
    f2, b2 = f2.astype(BF), b2.astype(BF)
    hops[1, :, pl.ds(2 * tc, tc)] = f2
    hops[1, :, pl.ds(4 * tc, tc)] = b2
    mix1 = mix_fold(fr1, 1)
    early = jnp.concatenate(
        [conv1, lanes_of(mix1[:4]), lanes_of(mix0[:4]), lanes_of([mix1[4], mix0[4]])], axis=0
    )
    for p in range(n_graph):
        e_part[p] = early[p * er:(p + 1) * er]

    def scatter(off):
        p = partner(off)
        graph_copy(e_part.at[p], e_buf.at[me], e_ssem.at[p], e_rsem.at[me], p).start()

    peers(n_graph, scatter)
    e_buf[me] = e_part[me]
    mixed = part + dot_nt(f2, mixall[1, :, pl.ds(2 * tc, tc)]) + dot_nt(b2, mixall[1, :, pl.ds(4 * tc, tc)])
    out[...] = (ext[1, :, pl.ds(0, tc)].astype(F32) + (mixed + mbias[1:2])).T.astype(BF)

    bi, fi = land(5, *db)
    gp0 = pre_grad(0, gg0 + fi + bi)
    lag_start(1, 0, gp0)
    l_buf[me] = conv_fold(0, gp0)
    gather_start(l_buf, l_ssem, l_rsem, n_graph, me, graph_copy)
    new = flow[...] + dot(gp0, band[0, :, pl.ds(0, tc)])

    et_buf[z] = gather_sum(e_buf, e_ssem, e_rsem, n_graph, me, graph_copy)
    gather_start(et_buf, et_ssem, et_rsem, n_tm, z, tm_copy)
    gser[...] = (new + lag_take(1)).T.astype(BF)

    lt_buf[z] = gather_sum(l_buf, l_ssem, l_rsem, n_graph, me, graph_copy)
    gather_start(lt_buf, lt_ssem, lt_rsem, n_tm, z, tm_copy)
    eg_buf[me] = gather_sum(et_buf, et_ssem, et_rsem, n_tm, z, tm_copy)
    gather_start(eg_buf, eg_ssem, eg_rsem, n_graph, me, graph_copy)

    def lane_group(x, g):
        return (pltpu.roll(x, tc - g * ch, 1) if g else x)[:, :ch]

    def put_conv(l, x):
        gconv[l, 0] = x[:, :2 * ch]
        gconv[l, 1] = pltpu.roll(x, tc - 2 * ch, 1)[:, :2 * ch]

    put_conv(0, gather_sum(lt_buf, lt_ssem, lt_rsem, n_tm, z, tm_copy) * scale)

    def take_group(off):
        p = partner(off)
        graph_copy(eg_buf.at[p], eg_buf.at[p], eg_ssem.at[p], eg_rsem.at[p], p).wait_recv()

    peers(n_graph, take_group)
    e = jnp.concatenate([eg_buf[p] for p in range(n_graph)], axis=0) * scale
    put_conv(1, e[:ch])
    for k in range(4):
        gmix[1, k] = lane_group(e[ch:2 * ch], k)
        gmix[0, k] = lane_group(e[2 * ch:3 * ch], k)
    gmix[1, 4] = lane_group(e[3 * ch:], 0)
    gmix[0, 4] = lane_group(e[3 * ch:], 1)

    def sent_graph(off):
        p = partner(off)
        for r in range(send.shape[0]):
            graph_copy(send.at[r, p], recv.at[r, me], r_ssem.at[r, p], r_rsem.at[r], p).wait_send()
        for r in range(send_w.shape[0]):
            graph_copy(send_w.at[r, p], recv_w.at[r, me], w_ssem.at[r, p], w_rsem.at[r], p).wait_send()
        graph_copy(e_part.at[p], e_buf.at[me], e_ssem.at[p], e_rsem.at[me], p).wait_send()
        graph_copy(eg_buf.at[me], eg_buf.at[me], eg_ssem.at[p], eg_rsem.at[me], p).wait_send()
        graph_copy(l_buf.at[me], l_buf.at[me], l_ssem.at[p], l_rsem.at[me], p).wait_send()

    peers(n_graph, sent_graph)

    def sent_tm(off):
        p = lax.rem(z + off, n_tm)
        tm_copy(et_buf.at[z], et_buf.at[z], et_ssem.at[p], et_rsem.at[z], p).wait_send()
        tm_copy(lt_buf.at[z], lt_buf.at[z], lt_ssem.at[p], lt_rsem.at[z], p).wait_send()

    peers(n_tm, sent_tm)

    @pl.when(up)
    def _():
        for first in firsts:
            first.wait_send()

    @pl.when(down)
    def _():
        shift_copy(2, pack_s.at[0], pack_r.at[0], -1).wait_send()
        shift_copy(3, pack_s.at[1], pack_r.at[1], -1).wait_send()


def store_kernel(a, b, c, d, ao, bo, co, do):
    ao[...] = a[...]
    bo[...] = b[...]
    co[...] = c[...]
    do[...] = d[...]


def per_device(series, cw, cb, mw, mb, tv, tcol, sidx, smask, cot):
    n_graph = lax.axis_size("graph")
    n_tm = lax.axis_size("tm")
    steps, ch, sensors = series.shape
    tc = steps * ch
    slots = sidx.shape[2]
    halo = n_graph * slots
    wire = BF if slots % 16 == 0 else F32
    narrow, wide = 6, 2
    scale = 1.0 / math.sqrt(float(steps * n_tm * sensors * n_graph))
    vm = pl.BlockSpec(memory_space=pltpu.VMEM)
    hb = pl.BlockSpec(memory_space=pltpu.HBM)
    cwt_shape = (*cw.shape[:2], cw.shape[3], cw.shape[2])
    ins = (
        series.reshape(tc, sensors),
        jnp.swapaxes(cw, 2, 3).reshape(-1, cw.shape[2]),
        cb,
        mw.reshape(-1, ch),
        mb,
        tv.reshape(-1, *tv.shape[2:]),
        tcol,
        sidx[0],
        smask[0],
        cot.reshape(tc, sensors),
    )
    er = 4 * ch // n_graph
    sm = pl.BlockSpec(memory_space=pltpu.SMEM)
    dma = pltpu.SemaphoreType.DMA
    out, gser, gconv, gmix = pl.pallas_call(
        functools.partial(kernel, n_graph, n_tm, steps, scale),
        out_shape=(
            jax.ShapeDtypeStruct((tc, sensors), BF),
            jax.ShapeDtypeStruct((tc, sensors), BF),
            jax.ShapeDtypeStruct(cwt_shape, F32),
            jax.ShapeDtypeStruct(mw.shape, F32),
        ),
        in_specs=[hb] * 6 + [sm] + [hb] * 3,
        out_specs=(vm,) * 4,
        scratch_shapes=[
            pltpu.VMEM((sensors, sensors), BF),
            pltpu.VMEM((sensors, sensors), BF),
            pltpu.VMEM((sensors, halo), BF),
            pltpu.VMEM((halo, sensors), BF),
            pltpu.VMEM((sensors, halo), BF),
            pltpu.VMEM((halo, sensors), BF),
            pltpu.VMEM((GATED_LAYERS, 2 * tc, 2 * tc), BF),
            pltpu.VMEM((2 * tc, tc), BF),
            pltpu.VMEM((GATED_LAYERS, tc, HOPS * tc), BF),
            pltpu.VMEM((tc, HOPS * tc), BF),
            pltpu.VMEM((GATED_LAYERS, sensors, 2 * tc), BF),
            pltpu.VMEM((GATED_LAYERS, sensors, HOPS * tc), BF),
            pltpu.VMEM((sensors, HOPS * tc), BF),
            pltpu.VMEM((GATED_LAYERS, sensors, tc), F32),
            pltpu.VMEM((GATED_LAYERS, sensors, tc), F32),
            pltpu.VMEM((sensors, tc), F32),
            pltpu.VMEM((tc, sensors), BF),
            pltpu.VMEM((2, sensors // 2, tc), BF),
            pltpu.VMEM((2, sensors // 2, tc), BF),
            pltpu.VMEM((narrow, n_graph, 2, slots, tc), wire),
            pltpu.VMEM((narrow, n_graph, 2, slots, tc), wire),
            pltpu.VMEM((wide, n_graph, 3, slots, tc), wire),
            pltpu.VMEM((wide, n_graph, 3, slots, tc), wire),
            pltpu.VMEM((n_graph, er, tc), F32),
            pltpu.VMEM((n_tm, er, tc), F32),
            pltpu.VMEM((n_graph, ch, tc), F32),
            pltpu.VMEM((n_tm, ch, tc), F32),
            pltpu.VMEM((n_graph, er, tc), F32),
            pltpu.VMEM((n_graph, er, tc), F32),
            *[pltpu.VMEM(x.shape, x.dtype) for x in ins[:6] + ins[7:]],
            dma((9,)),
            dma((narrow, n_graph)), dma((narrow,)),
            dma((wide, n_graph)), dma((wide,)),
            dma((4,)), dma((4,)),
            dma((n_graph,)), dma((n_graph,)),
            dma((n_tm,)), dma((n_tm,)),
            dma((n_graph,)), dma((n_graph,)),
            dma((n_tm,)), dma((n_tm,)),
            dma((n_graph,)), dma((n_graph,)),
        ],
        compiler_params=pltpu.CompilerParams(
            collective_id=0, has_side_effects=True, vmem_limit_bytes=63 * 1024 * 1024
        ),
    )(*ins)
    results = (out, gser, gconv, gmix)
    out, gser, gconv, gmix = pl.pallas_call(
        store_kernel,
        out_shape=tuple(jax.ShapeDtypeStruct(x.shape, x.dtype) for x in results),
        in_specs=[vm] * 4,
        out_specs=(vm,) * 4,
    )(*results)
    gconv = jnp.swapaxes(gconv, 2, 3)
    return out.reshape(series.shape), gser.reshape(series.shape), gconv, gmix


def solution(mesh):
    return jax.shard_map(
        per_device,
        mesh=mesh,
        in_specs=(
            P("tm", None, "graph"),
            P(),
            P(),
            P(),
            P(),
            P("graph", None, None, None),
            P("graph", None),
            P("graph", None, None),
            P("graph", None, None),
            P("tm", None, "graph"),
        ),
        out_specs=(P("tm", None, "graph"), P("tm", None, "graph"), P(), P()),
        check_vma=False,
    )
```

```python
import functools
import math

import jax
import jax.numpy as jnp
from jax import lax
from jax.experimental import pallas as pl
from jax.experimental.pallas import tpu as pltpu
from jax.sharding import PartitionSpec as P

GATED_LAYERS = 2
HOPS = 5
BF = jnp.bfloat16
F32 = jnp.float32
MESH = pl.DeviceIdType.MESH


def dot(a, b):
    return lax.dot_general(a, b, (((1,), (0,)), ((), ())), preferred_element_type=F32)


def dot_nt(a, b):
    return lax.dot_general(a, b, (((1,), (1,)), ((), ())), preferred_element_type=F32)


def dot_tn(a, b):
    return lax.dot_general(a, b, (((0,), (0,)), ((), ())), preferred_element_type=F32)


def quot(x, n):
    return x >> (n.bit_length() - 1) if n & (n - 1) == 0 else x // n


def rest_of(x, n):
    return x & (n - 1) if n & (n - 1) == 0 else lax.rem(x, n)


def peers(count, body):
    if count <= 8:
        for off in range(count - 1, 0, -1):
            body(off)
    elif count > 1:
        lax.fori_loop(1, count, lambda off, c: (body(off), c)[1], 0)


def kernel(
    n_graph, n_tm, steps, scale,
    series_h, cw_h, cb_h, mw_h, mb_h, tv_h, tcol_h, sidx_h, smask_h, cot_h,
    out, gser, gconv, gmix,
    wl, wlt, wh, wht, gm, gmt, gwl, gwh, whg, band, band_h, mixall, mix_h, ext, hops, hops_h, filt, gate, flow,
    prev0, pack_s, pack_r, send, recv, send_w, recv_w, e_buf, et_buf, l_buf, lt_buf,
    e_part, eg_buf, m_buf, mt_buf, pair_s, pair_r, fin,
    series, cw, cb, mw, mb, tv, tcol, sidx, smask, cot, in_sem,
    r_ssem, r_rsem, w_ssem, w_rsem, t_ssem, t_rsem, e_ssem, e_rsem, et_ssem, et_rsem,
    l_ssem, l_rsem, lt_ssem, lt_rsem, eg_ssem, eg_rsem, m_ssem, m_rsem, mt_ssem, mt_rsem,
    pair_sem, fin_ssem, fin_rsem,
):
    me = lax.axis_index("graph")
    z = lax.axis_index("tm")
    tc, sensors = series.shape
    ch = tc // steps
    half = tc // 2
    half_s = sensors // 2
    slots = sidx.shape[1]
    halo = n_graph * slots
    tile = tv.shape[-1]
    rblocks, tslots = tcol.shape
    lblocks = sensors // tile
    hblocks = halo // tile
    wire = send.dtype
    direct = fin.shape[0] > 1
    core = lax.rem(me, 2)
    mate = me + 1 - 2 * core

    def partner(off):
        if n_graph & (n_graph - 1) or n_graph > 8:
            return lax.rem(me + off, n_graph)
        p = 0
        bit = 1
        while bit < n_graph:
            p = p + lax.rem(me // bit + off // bit, 2) * bit
            bit *= 2
        return p

    er = e_part.shape[1]

    loads = [
        pltpu.make_async_copy(src, dst, in_sem.at[i])
        for i, (src, dst) in enumerate(
            ((cw_h, cw), (mw_h, mw), (cb_h, cb), (mb_h, mb), (tv_h, tv), (series_h, series),
             (sidx_h, sidx), (smask_h, smask), (cot_h, cot), (tcol_h, tcol))
        )
    ]
    for load in loads:
        load.start()
    barrier = pltpu.get_barrier_semaphore()

    def greet_graph(off):
        pl.semaphore_signal(barrier, inc=1, device_id={"graph": partner(off)}, device_id_type=MESH)

    def greet_tm(off):
        pl.semaphore_signal(barrier, inc=1, device_id={"tm": lax.rem(z + off, n_tm)}, device_id_type=MESH)

    peers(n_graph, greet_graph)
    peers(n_tm, greet_tm)

    def shift_copy(slot, src, dst, by):
        return pltpu.make_async_remote_copy(
            src_ref=src, dst_ref=dst, send_sem=t_ssem.at[slot], recv_sem=t_rsem.at[slot],
            device_id={"tm": lax.rem(z + by + n_tm, n_tm)}, device_id_type=MESH,
        )

    up = z < n_tm - 1
    down = z > 0

    firsts = [
        shift_copy(0, series_h.at[pl.ds(tc - ch, ch)], prev0.at[pl.ds(tc - ch, ch)], 1),
        shift_copy(1, series_h.at[pl.ds(tc - 3 * ch, 2 * ch)], prev0.at[pl.ds(tc - 3 * ch, 2 * ch)], 1),
    ]
    pl.semaphore_wait(barrier, n_graph - 1 + n_tm - 1)

    @pl.when(up)
    def _():
        for first in firsts:
            first.start()

    prev0[pl.ds(0, tc - 3 * ch), :] = jnp.zeros((tc - 3 * ch, sensors), BF)

    row32 = lax.broadcasted_iota(jnp.int32, (ch, tc), 0)
    lane32 = lax.broadcasted_iota(jnp.int32, (ch, tc), 1)
    spread = jnp.where(rest_of(lane32, ch) == row32, 1.0, 0.0)
    spread_b = spread.astype(BF)
    rt = lax.broadcasted_iota(jnp.int32, (tc, tc), 0)
    lt = lax.broadcasted_iota(jnp.int32, (tc, tc), 1)
    rt, lt = quot(rt, ch), quot(lt, ch)
    same = rt == lt
    late = rt >= steps // 2

    def before(d):
        return lt == rt - d

    def before_prev(d):
        return lt == rt - d + steps

    for load in loads[:4]:
        load.wait()
    taps = 2 * GATED_LAYERS
    rs = lax.broadcasted_iota(jnp.int32, (taps * ch, taps * tc), 0)
    ls = lax.broadcasted_iota(jnp.int32, (taps * ch, taps * tc), 1)
    spread_taps = jnp.where(quot(ls, tc) * ch + rest_of(ls, ch) == rs, 1.0, 0.0).astype(BF)
    def after(d):
        return rt == lt - d

    def after_prev(d):
        return rt == lt - d + steps

    cwr = dot_tn(cw[...], spread_taps)
    mwr = dot(mw[...], spread_b)

    def stack(x, base):
        return jnp.concatenate([x[base:base + ch]] * steps, axis=0)

    for l in range(GATED_LAYERS):
        d = l + 1
        for h in range(2):
            w0 = stack(cwr[:, (l * 2) * tc:(l * 2 + 1) * tc], h * ch)
            w1 = stack(cwr[:, (l * 2 + 1) * tc:(l * 2 + 2) * tc], h * ch)
            own = (jnp.where(same, w0, 0.0) + jnp.where(before(d), w1, 0.0)).astype(BF)
            band[l, pl.ds(h * tc, tc), pl.ds(0, tc)] = own
            band[l, pl.ds(h * tc, tc), pl.ds(tc, tc)] = jnp.where(before_prev(d), w1, 0.0).astype(BF)
            if l == 0:
                band_h[pl.ds(h * tc, tc), :] = jnp.concatenate([own[half:], own[half:]], axis=0)
        for k in range(HOPS):
            mk = stack(mwr, (l * HOPS + k) * ch)
            mixall[l, :, pl.ds(k * tc, tc)] = jnp.where(same, mk, 0.0).astype(BF)
            if l == 0:
                at = (rt == lt + steps // 2) if k in (1, 2) else (same & late)
                mix_h[:, pl.ds(k * tc, tc)] = jnp.where(at, mk, 0.0).astype(BF)

    r64 = lax.broadcasted_iota(jnp.int32, (2 * ch, 2 * tc), 0)
    l64 = lax.broadcasted_iota(jnp.int32, (2 * ch, 2 * tc), 1)
    spread2 = jnp.where(rest_of(l64, ch) + quot(l64, tc) * ch == r64, 1.0, 0.0)
    cbias = lax.dot_general(cb[...], spread2, (((1,), (0,)), ((), ())), precision=lax.Precision.HIGHEST, preferred_element_type=F32)
    mbias = lax.dot_general(mb[...], spread, (((1,), (0,)), ((), ())), precision=lax.Precision.HIGHEST, preferred_element_type=F32)

    for load in loads[4:]:
        load.wait()
    for r in range(rblocks):
        tiles = [tv[r * tslots + k].astype(F32) for k in range(tslots)]
        flips = [t.T for t in tiles]
        for c in range(lblocks + hblocks):
            a = jnp.zeros((tile, tile), F32)
            b = jnp.zeros((tile, tile), F32)
            for k in range(tslots):
                on = (tcol[r, k] == c).astype(jnp.int32).astype(F32)
                a = a + tiles[k] * on
                b = b + flips[k] * on
            a = a.astype(BF)
            b = b.astype(BF)
            if c < lblocks:
                wl[pl.ds(r * tile, tile), pl.ds(c * tile, tile)] = a
                wlt[pl.ds(c * tile, tile), pl.ds(r * tile, tile)] = b
            else:
                ch_at = c - lblocks
                wh[pl.ds(r * tile, tile), pl.ds(ch_at * tile, tile)] = a
                wht[pl.ds(ch_at * tile, tile), pl.ds(r * tile, tile)] = b

    key = jnp.where(smask[...] != 0, sidx[...] + 1, 0)
    es = lax.broadcasted_iota(jnp.int32, (slots, halo), 0)
    ej = lax.broadcasted_iota(jnp.int32, (slots, halo), 1)
    pick = jnp.where(rest_of(ej, slots) == es, 1.0, 0.0).astype(BF)
    hi = dot((key >> 5).astype(F32).astype(BF), pick)
    lo = dot((key & 31).astype(F32).astype(BF), pick)
    pr = lax.broadcasted_iota(jnp.int32, (n_graph, halo), 0)
    pj = quot(lax.broadcasted_iota(jnp.int32, (n_graph, halo), 1), slots)
    keys = jnp.sum(jnp.where(pr == pj, hi * 32.0 + lo, 0.0), axis=0, keepdims=True)
    ids = lax.broadcasted_iota(jnp.int32, (sensors, halo), 0).astype(F32) + 1.0
    onehot = jnp.where(ids == keys, 1.0, 0.0)
    gm[...] = onehot.astype(BF)
    gmt[...] = onehot.T.astype(BF)

    def graph_copy(src, dst, ssem, rsem, p):
        return pltpu.make_async_remote_copy(
            src_ref=src, dst_ref=dst, send_sem=ssem, recv_sem=rsem,
            device_id={"graph": p}, device_id_type=MESH,
        )

    def tm_copy(src, dst, ssem, rsem, p):
        return pltpu.make_async_remote_copy(
            src_ref=src, dst_ref=dst, send_sem=ssem, recv_sem=rsem,
            device_id={"tm": p}, device_id_type=MESH,
        )

    lane_low = lax.broadcasted_iota(jnp.int32, (halo, tc), 1) < half

    def ship(blocks, out_buf, in_buf, ssem, rsem, r):
        for i, block in enumerate(blocks):
            out_buf[r, :, i] = block.astype(BF).reshape(n_graph, slots, tc).astype(wire)

        def go(off):
            p = partner(off)
            graph_copy(out_buf.at[r, p], in_buf.at[r, me], ssem.at[r, p], rsem.at[r], p).start()

        peers(n_graph, go)
        in_buf[r, me] = out_buf[r, me]

    def collect(in_buf, ssem, rsem, r, count):
        arrived = in_buf.at[r, pl.ds(0, n_graph - 1)]
        graph_copy(arrived, arrived, ssem.at[r, 0], rsem.at[r], partner(1)).wait_recv()
        return [in_buf[r, :, i].reshape(halo, tc).astype(BF) for i in range(count)]

    def launch(r, pull_in, push_in):
        ship((dot(gmt[...], pull_in), dot(wht[...], push_in)), send, recv, r_ssem, r_rsem, r)

    def launch_w(r, pull_in, push_in):
        ship_w(r, dot(gmt[...], pull_in), dot(wht[...], push_in))

    def ship_w(r, sp, sb):
        packed = jnp.where(lane_low, sp[:, tc:], sb[:, tc:])
        ship((sp[:, :tc], sb[:, :tc], packed), send_w, recv_w, w_ssem, w_rsem, r)

    def local(pull_in, push_in):
        return dot(wl[...], pull_in), dot(wlt[...], push_in)

    def land(r):
        return collect(recv, r_ssem, r_rsem, r, 2)

    def land_w(r):
        rp, rb, both = collect(recv_w, w_ssem, w_rsem, r, 3)
        return jnp.concatenate([rp, both], axis=1), jnp.concatenate([rb, both], axis=1)

    def relay(r, rp, rb, sp, sb):
        ship((sp + dot(gwh[...], rp), sb + dot(whg[...], rb)), send, recv, r_ssem, r_rsem, r)

    def whole(pulled, pushed, rp, rb):
        return pulled + dot(wh[...], rp), pushed + dot(gm[...], rb)

    lane_half = lax.broadcasted_iota(jnp.int32, (half_s, tc), 1) < half

    def pack(x):
        return jnp.where(lane_half, pltpu.roll(x[:half_s], half, 1), x[half_s:]).astype(BF)

    def unpack(p):
        x = p.astype(F32)
        return jnp.concatenate([pltpu.roll(x, half, 1), x], axis=0)

    lane_g = quot(lax.broadcasted_iota(jnp.int32, (ch, tc), 1), ch)

    def fold(x):
        y = x[0:ch]
        for t in range(1, steps):
            y = y + x[t * ch:(t + 1) * ch]
        sh = ch
        while sh < tc:
            y = y + pltpu.roll(y, sh, 1)
            sh *= 2
        return y

    def lanes_of(xs):
        y = jnp.zeros((ch, tc), F32)
        for g, x in enumerate(xs):
            y = jnp.where(lane_g == g, x, y)
        return y

    def gather_start(buf, ssem, rsem, count, here, copy):
        def go(off):
            p = lax.rem(here + off, count)
            copy(buf.at[here], buf.at[here], ssem.at[p], rsem.at[here], p).start()

        peers(count, go)

    def gather_sum(buf, ssem, rsem, count, here, copy):
        def take(off):
            p = lax.rem(here + off, count)
            copy(buf.at[p], buf.at[p], ssem.at[p], rsem.at[p], p).wait_recv()

        peers(count, take)
        total = buf[0]
        for p in range(1, count):
            total = total + buf[p]
        return total

    def hop_grad(fr, l, k):
        return dot(fr, mixall[l, :, pl.ds(k * tc, tc)])

    def mix_fold(l, fr, ks):
        folds = []
        for k in ks:
            hop = hops[l, :, pl.ds(k * tc, tc)]
            folds.append(fold(jnp.where(same, dot(cot[...], hop) if l == 1 else dot_tn(fr, hop), 0.0)))
        return folds

    def conv_fold(l, gp):
        d = l + 1
        if l == 0:
            prod = (dot(series[...], gp), dot(prev0[...], gp))
        else:
            prod = [dot_tn(ext[l, :, pl.ds(i * tc, tc)], gp) for i in range(2)]
        pieces = []
        for tap in range(2):
            for h in range(2):
                own = prod[0][:, h * tc:(h + 1) * tc]
                if tap == 0:
                    x = jnp.where(same, own, 0.0)
                else:
                    x = jnp.where(after(d), own, 0.0) + jnp.where(after_prev(d), prod[1][:, h * tc:(h + 1) * tc], 0.0)
                pieces.append(fold(x))
        return lanes_of(pieces)

    def pre_grad(l, gg):
        f = filt[l]
        g = gate[l]
        return jnp.concatenate([gg * g * (1.0 - f * f), gg * f * g * (1.0 - g)], axis=1).astype(BF)

    def lag_start(i, l, gp):
        pack_s[i] = pack(dot(gp, band[l, :, pl.ds(tc, tc)]))

        @pl.when(down)
        def _():
            shift_copy(2 + i, pack_s.at[i], pack_r.at[i], -1).start()

    lanes_late = lax.broadcasted_iota(jnp.int32, (sensors, tc), 1) >= half

    def lag_take(i):
        @pl.when(up)
        def _():
            shift_copy(2 + i, pack_s.at[i], pack_r.at[i], -1).wait_recv()

        @pl.when(jnp.logical_not(up))
        def _():
            pack_r[i] = jnp.zeros((half_s, tc), BF)

        return jnp.where(lanes_late, unpack(pack_r[i]), 0.0)

    flow[...] = cot[...].astype(F32).T
    fr1 = flow[...].astype(BF)
    h4, h2 = hop_grad(fr1, 1, 4).astype(BF), hop_grad(fr1, 1, 2).astype(BF)
    launch(0, h4, h2)
    gwl[...] = dot(gmt[...], wl[...]).astype(BF)
    gwh[...] = dot(gmt[...], wh[...]).astype(BF)
    whg[...] = dot(wht[...], gm[...]).astype(BF)

    def mid_back(fr, l, pull_in, push_in):
        pulled, pushed = local(pull_in, push_in)
        pulled = pulled + hop_grad(fr, l, 3)
        pushed = pushed + hop_grad(fr, l, 1)
        sp = dot(gwl[...], pull_in) + hop_grad(dot(gmt[...], fr).astype(BF), l, 3)
        return pulled, pushed, sp, dot(wht[...], pushed.astype(BF))

    def mid(pull_in, push_in):
        pulled, pushed = local(pull_in, push_in)
        return pulled, pushed, dot(gwl[...], pull_in), dot(wht[...], pushed.astype(BF))

    ab = mid_back(fr1, 1, h4, h2)

    ext[0, :, pl.ds(0, tc)] = series[...].astype(F32).T.astype(BF)

    @pl.when(down)
    def _():
        for first in firsts:
            first.wait_recv()

    @pl.when(jnp.logical_not(down))
    def _():
        prev0[pl.ds(tc - 3 * ch, 3 * ch), :] = jnp.zeros((3 * ch, sensors), BF)

    prev_t = prev0[...].astype(F32).T
    ext[0, :, pl.ds(tc, tc)] = prev_t.astype(BF)
    pre = dot_nt(ext[0], band[0]) + cbias[0:1]
    f = jnp.tanh(pre[:, :tc])
    g = jax.nn.sigmoid(pre[:, tc:])
    filt[0] = f
    gate[0] = g
    gated = (f * g).astype(BF)
    pre = dot_nt(ext[0, :, pl.ds(tc, tc)], band_h[...]) + cbias[0:1]
    gated_h = (jnp.tanh(pre[:, :tc]) * jax.nn.sigmoid(pre[:, tc:])).astype(BF)
    both = jnp.concatenate([gated, gated_h], axis=1)
    launch_w(0, both, both)

    def keep(k, x):
        hops[0, :, pl.ds(k * tc, tc)] = x[:, :tc]
        hops_h[:, pl.ds(k * tc, tc)] = x[:, tc:]

    keep(0, both)
    af = mid(both, both)

    rp, rb = land(0)
    relay(1, rp, rb, *ab[2:])
    bi, fi = whole(*ab[:2], rp, rb)
    bb = local(bi.astype(BF), fi.astype(BF))
    gg0 = hop_grad(fr1, 1, 0)

    rp, rb = land_w(0)
    ship_w(1, af[2] + dot(gwh[...], rp), af[3] + dot(whg[...], rb))
    fo, bo = whole(*af[:2], rp, rb)
    fo, bo = fo.astype(BF), bo.astype(BF)
    keep(1, fo)
    keep(3, bo)
    bf = local(fo, bo)

    def mix_three(mat, hop):
        m = dot_nt(hop(0, 2), mat(0, 2))
        return m + dot_nt(hop(3, 1), mat(3, 1))

    def mat_of(l):
        return lambda k, n: mixall[l, :, pl.ds(k * tc, n * tc)]

    def hop_of(l):
        return lambda k, n: hops[l, :, pl.ds(k * tc, n * tc)]

    part = mix_three(mat_of(0), hop_of(0))
    part_h = mix_three(
        lambda k, n: mix_h[:, pl.ds(k * tc, n * tc)], lambda k, n: hops_h[:, pl.ds(k * tc, n * tc)]
    )

    bi, fi = whole(*bb, *land(1))
    gg1 = gg0 + fi + bi

    f2, b2 = whole(*bf, *land_w(1))
    f2, b2 = f2.astype(BF), b2.astype(BF)
    keep(2, f2)
    keep(4, b2)
    mixed = part + dot_nt(f2[:, :tc], mixall[0, :, pl.ds(2 * tc, tc)]) + dot_nt(b2[:, :tc], mixall[0, :, pl.ds(4 * tc, tc)])
    mixed_h = part_h + dot_nt(f2[:, tc:], mix_h[:, pl.ds(2 * tc, tc)]) + dot_nt(b2[:, tc:], mix_h[:, pl.ds(4 * tc, tc)])
    ext[1, :, pl.ds(0, tc)] = (ext[0, :, pl.ds(0, tc)].astype(F32) + (mixed + mbias[0:1])).astype(BF)
    hid_h = ext[0, :, pl.ds(tc, tc)].astype(F32) + (mixed_h + mbias[0:1])
    ext[1, :, pl.ds(tc, tc)] = jnp.where(lanes_late & down, hid_h, 0.0).astype(BF)

    pre = dot_nt(ext[1], band[1]) + cbias[1:2]
    f = jnp.tanh(pre[:, :tc])
    g = jax.nn.sigmoid(pre[:, tc:])
    filt[1] = f
    gate[1] = g
    gp1 = pre_grad(1, gg1)
    lag_start(0, 1, gp1)
    gated = (f * g).astype(BF)
    hops[1, :, pl.ds(0, tc)] = gated
    launch(2, gated, gated)
    cf = mid(gated, gated)
    new = flow[...] + dot(gp1, band[1, :, pl.ds(0, tc)])
    conv1 = conv_fold(1, gp1)

    flow[...] = new + lag_take(0)
    fr0 = flow[...].astype(BF)
    h4, h2 = hop_grad(fr0, 0, 4).astype(BF), hop_grad(fr0, 0, 2).astype(BF)
    launch(4, h4, h2)
    cb_ = mid_back(fr0, 0, h4, h2)

    rp, rb = land(2)
    relay(3, rp, rb, *cf[2:])
    fo, bo = whole(*cf[:2], rp, rb)
    fo, bo = fo.astype(BF), bo.astype(BF)
    hops[1, :, pl.ds(tc, tc)] = fo
    hops[1, :, pl.ds(3 * tc, tc)] = bo
    df = local(fo, bo)
    gg0 = hop_grad(fr0, 0, 0)
    mix0 = mix_fold(0, fr0, range(HOPS))
    mix1 = mix_fold(1, fr1, (0, 1, 3))
    early = jnp.concatenate([conv1, lanes_of(mix0[:4]), lanes_of([mix0[4]] + mix1)], axis=0)
    for p in range(n_graph):
        e_part[p] = early[p * er:(p + 1) * er]

    def scatter(off):
        p = partner(off)
        graph_copy(e_part.at[p], e_buf.at[me], e_ssem.at[p], e_rsem.at[me], p).start()

    peers(n_graph, scatter)
    e_buf[me] = e_part[me]
    part = mix_three(mat_of(1), hop_of(1))

    rp, rb = land(4)
    relay(5, rp, rb, *cb_[2:])
    bi, fi = whole(*cb_[:2], rp, rb)
    db = local(bi.astype(BF), fi.astype(BF))

    f2, b2 = whole(*df, *land(3))
    f2, b2 = f2.astype(BF), b2.astype(BF)
    hops[1, :, pl.ds(2 * tc, tc)] = f2
    hops[1, :, pl.ds(4 * tc, tc)] = b2
    a2, a4 = mix_fold(1, fr1, (2, 4))
    hc = ch // 2
    last = jnp.zeros((hc, tc), F32)
    for g, x in enumerate((a2[:hc], a4[:hc], a2[hc:], a4[hc:])):
        last = jnp.where(lane_g[:hc] == g, x, last)
    m_buf[me] = last
    gather_start(m_buf, m_ssem, m_rsem, n_graph, me, graph_copy)
    mixed = part + dot_nt(f2, mixall[1, :, pl.ds(2 * tc, tc)]) + dot_nt(b2, mixall[1, :, pl.ds(4 * tc, tc)])
    out[...] = (ext[1, :, pl.ds(0, tc)].astype(F32) + (mixed + mbias[1:2])).T.astype(BF)

    et_buf[z] = gather_sum(e_buf, e_ssem, e_rsem, n_graph, me, graph_copy)
    gather_start(et_buf, et_ssem, et_rsem, n_tm, z, tm_copy)

    bi, fi = whole(*db, *land(5))
    gp0 = pre_grad(0, gg0 + fi + bi)
    conv0 = conv_fold(0, gp0)
    if direct:
        swap = graph_copy(pair_s, pair_r, pair_sem.at[0], pair_sem.at[1], mate)
        low = core == 0
        pair_s[...] = jnp.where(low, conv0[hc:], conv0[:hc])
        swap.start()
    else:
        l_buf[me] = conv0
        gather_start(l_buf, l_ssem, l_rsem, n_graph, me, graph_copy)
    lag_start(1, 0, gp0)

    def final_copy(goff, toff):
        p = partner(goff) if goff else me
        return pltpu.make_async_remote_copy(
            src_ref=fin.at[z * n_graph + me], dst_ref=fin.at[z * n_graph + me],
            send_sem=fin_ssem.at[toff * n_graph + goff], recv_sem=fin_rsem.at[0],
            device_id={"graph": p, "tm": lax.rem(z + toff, n_tm)}, device_id_type=MESH,
        )

    others = [(g, t) for t in range(n_tm) for g in range(n_graph) if (g, t) != (0, 0)] if direct else []
    if direct:
        swap.wait_recv()
        fin[z * n_graph + me] = (jnp.where(low, conv0[:hc], conv0[hc:]) + pair_r[...]).astype(BF)
        for g, t in reversed(others):
            final_copy(g, t).start()
    mt_buf[z] = gather_sum(m_buf, m_ssem, m_rsem, n_graph, me, graph_copy)
    gather_start(mt_buf, mt_ssem, mt_rsem, n_tm, z, tm_copy)
    eg_buf[me] = gather_sum(et_buf, et_ssem, et_rsem, n_tm, z, tm_copy)
    gather_start(eg_buf, eg_ssem, eg_rsem, n_graph, me, graph_copy)
    if not direct:
        lt_buf[z] = gather_sum(l_buf, l_ssem, l_rsem, n_graph, me, graph_copy)
        gather_start(lt_buf, lt_ssem, lt_rsem, n_tm, z, tm_copy)
    new = flow[...] + dot(gp0, band[0, :, pl.ds(0, tc)])
    gser[...] = (new + lag_take(1)).T.astype(BF)

    def lane_group(x, g):
        return (pltpu.roll(x, tc - g * ch, 1) if g else x)[:, :ch]

    def put_conv(l, x):
        gconv[l, 0] = x[:, :2 * ch]
        gconv[l, 1] = pltpu.roll(x, tc - 2 * ch, 1)[:, :2 * ch]

    m = gather_sum(mt_buf, mt_ssem, mt_rsem, n_tm, z, tm_copy) * scale
    for i, k in enumerate((2, 4)):
        gmix[1, k, pl.ds(0, hc)] = lane_group(m, i)
        gmix[1, k, pl.ds(hc, hc)] = lane_group(m, i + 2)

    def take_group(off):
        p = partner(off)
        graph_copy(eg_buf.at[p], eg_buf.at[p], eg_ssem.at[p], eg_rsem.at[p], p).wait_recv()

    peers(n_graph, take_group)
    e = jnp.concatenate([eg_buf[p] for p in range(n_graph)], axis=0) * scale
    put_conv(1, e[:ch])
    for k in range(4):
        gmix[0, k] = lane_group(e[ch:2 * ch], k)
    gmix[0, 4] = lane_group(e[2 * ch:], 0)
    for i, k in enumerate((0, 1, 3)):
        gmix[1, k] = lane_group(e[2 * ch:], i + 1)
    if direct:
        arrived = fin.at[pl.ds(0, n_graph * n_tm - 1)]
        pltpu.make_async_remote_copy(
            src_ref=arrived, dst_ref=arrived, send_sem=fin_ssem.at[1], recv_sem=fin_rsem.at[0],
            device_id={"graph": mate}, device_id_type=MESH,
        ).wait_recv()
        halves = []
        for c in range(2):
            total = fin[c].astype(F32)
            for p in range(c + 2, n_graph * n_tm, 2):
                total = total + fin[p].astype(F32)
            halves.append(total)
        put_conv(0, jnp.concatenate(halves, axis=0) * scale)
        swap.wait_send()
        for g, t in others:
            final_copy(g, t).wait_send()
    else:
        put_conv(0, gather_sum(lt_buf, lt_ssem, lt_rsem, n_tm, z, tm_copy) * scale)

    def sent_graph(off):
        p = partner(off)
        for r in range(send.shape[0]):
            graph_copy(send.at[r, p], recv.at[r, me], r_ssem.at[r, p], r_rsem.at[r], p).wait_send()
        for r in range(send_w.shape[0]):
            graph_copy(send_w.at[r, p], recv_w.at[r, me], w_ssem.at[r, p], w_rsem.at[r], p).wait_send()
        graph_copy(e_part.at[p], e_buf.at[me], e_ssem.at[p], e_rsem.at[me], p).wait_send()
        graph_copy(eg_buf.at[me], eg_buf.at[me], eg_ssem.at[p], eg_rsem.at[me], p).wait_send()
        graph_copy(m_buf.at[me], m_buf.at[me], m_ssem.at[p], m_rsem.at[me], p).wait_send()
        if not direct:
            graph_copy(l_buf.at[me], l_buf.at[me], l_ssem.at[p], l_rsem.at[me], p).wait_send()

    peers(n_graph, sent_graph)

    def sent_tm(off):
        p = lax.rem(z + off, n_tm)
        tm_copy(et_buf.at[z], et_buf.at[z], et_ssem.at[p], et_rsem.at[z], p).wait_send()
        tm_copy(mt_buf.at[z], mt_buf.at[z], mt_ssem.at[p], mt_rsem.at[z], p).wait_send()
        if not direct:
            tm_copy(lt_buf.at[z], lt_buf.at[z], lt_ssem.at[p], lt_rsem.at[z], p).wait_send()

    peers(n_tm, sent_tm)

    @pl.when(up)
    def _():
        for first in firsts:
            first.wait_send()

    @pl.when(down)
    def _():
        shift_copy(2, pack_s.at[0], pack_r.at[0], -1).wait_send()
        shift_copy(3, pack_s.at[1], pack_r.at[1], -1).wait_send()


def store_kernel(a, b, c, d, ao, bo, co, do, sem):
    copies = [
        pltpu.make_async_copy(src, dst, sem.at[i])
        for i, (src, dst) in enumerate(((a, ao), (b, bo), (c, co), (d, do)))
    ]
    for copy in copies:
        copy.start()
    for copy in copies:
        copy.wait()


def per_device(series, cw, cb, mw, mb, tv, tcol, sidx, smask, cot):
    n_graph = lax.axis_size("graph")
    n_tm = lax.axis_size("tm")
    steps, ch, sensors = series.shape
    tc = steps * ch
    slots = sidx.shape[2]
    halo = n_graph * slots
    wire = BF if slots % 16 == 0 else F32
    narrow, wide = 6, 2
    scale = 1.0 / math.sqrt(float(steps * n_tm * sensors * n_graph))
    vm = pl.BlockSpec(memory_space=pltpu.VMEM)
    hb = pl.BlockSpec(memory_space=pltpu.HBM)
    cwt_shape = (*cw.shape[:2], cw.shape[3], cw.shape[2])
    ins = (
        series.reshape(tc, sensors),
        jnp.swapaxes(cw, 2, 3).reshape(-1, cw.shape[2]),
        cb,
        mw.reshape(-1, ch),
        mb,
        tv.reshape(-1, *tv.shape[2:]),
        tcol,
        sidx[0],
        smask[0],
        cot.reshape(tc, sensors),
    )
    er = 3 * ch // n_graph
    direct = n_graph % 2 == 0 and n_graph * n_tm <= 32 and ch % 32 == 0
    n_all = n_graph * n_tm if direct else 1
    ins = tuple(pltpu.with_memory_space_constraint(x, pltpu.HBM) for x in ins)
    dma = pltpu.SemaphoreType.DMA
    out, gser, gconv, gmix = pl.pallas_call(
        functools.partial(kernel, n_graph, n_tm, steps, scale),
        out_shape=(
            pltpu.VMEM((tc, sensors), BF),
            pltpu.VMEM((tc, sensors), BF),
            pltpu.VMEM(cwt_shape, F32),
            pltpu.VMEM(mw.shape, F32),
        ),
        in_specs=[hb] * 10,
        out_specs=(vm,) * 4,
        scratch_shapes=[
            pltpu.VMEM((sensors, sensors), BF),
            pltpu.VMEM((sensors, sensors), BF),
            pltpu.VMEM((sensors, halo), BF),
            pltpu.VMEM((halo, sensors), BF),
            pltpu.VMEM((sensors, halo), BF),
            pltpu.VMEM((halo, sensors), BF),
            pltpu.VMEM((halo, sensors), BF),
            pltpu.VMEM((halo, halo), BF),
            pltpu.VMEM((halo, halo), BF),
            pltpu.VMEM((GATED_LAYERS, 2 * tc, 2 * tc), BF),
            pltpu.VMEM((2 * tc, tc), BF),
            pltpu.VMEM((GATED_LAYERS, tc, HOPS * tc), BF),
            pltpu.VMEM((tc, HOPS * tc), BF),
            pltpu.VMEM((GATED_LAYERS, sensors, 2 * tc), BF),
            pltpu.VMEM((GATED_LAYERS, sensors, HOPS * tc), BF),
            pltpu.VMEM((sensors, HOPS * tc), BF),
            pltpu.VMEM((GATED_LAYERS, sensors, tc), F32),
            pltpu.VMEM((GATED_LAYERS, sensors, tc), F32),
            pltpu.VMEM((sensors, tc), F32),
            pltpu.VMEM((tc, sensors), BF),
            pltpu.VMEM((2, sensors // 2, tc), BF),
            pltpu.VMEM((2, sensors // 2, tc), BF),
            pltpu.VMEM((narrow, n_graph, 2, slots, tc), wire),
            pltpu.VMEM((narrow, n_graph, 2, slots, tc), wire),
            pltpu.VMEM((wide, n_graph, 3, slots, tc), wire),
            pltpu.VMEM((wide, n_graph, 3, slots, tc), wire),
            pltpu.VMEM((n_graph, er, tc), F32),
            pltpu.VMEM((n_tm, er, tc), F32),
            pltpu.VMEM((n_graph, ch, tc), F32),
            pltpu.VMEM((n_tm, ch, tc), F32),
            pltpu.VMEM((n_graph, er, tc), F32),
            pltpu.VMEM((n_graph, er, tc), F32),
            pltpu.VMEM((n_graph, ch // 2, tc), F32),
            pltpu.VMEM((n_tm, ch // 2, tc), F32),
            pltpu.VMEM((ch // 2, tc), F32),
            pltpu.VMEM((ch // 2, tc), F32),
            pltpu.VMEM((n_all, ch // 2, tc), BF),
            *[(pltpu.SMEM if x.shape == tcol.shape else pltpu.VMEM)(x.shape, x.dtype) for x in ins],
            dma((10,)),
            dma((narrow, n_graph)), dma((narrow,)),
            dma((wide, n_graph)), dma((wide,)),
            dma((4,)), dma((4,)),
            dma((n_graph,)), dma((n_graph,)),
            dma((n_tm,)), dma((n_tm,)),
            dma((n_graph,)), dma((n_graph,)),
            dma((n_tm,)), dma((n_tm,)),
            dma((n_graph,)), dma((n_graph,)),
            dma((n_graph,)), dma((n_graph,)),
            dma((n_tm,)), dma((n_tm,)),
            dma((2,)), dma((n_all,)), dma((1,)),
        ],
        compiler_params=pltpu.CompilerParams(
            collective_id=0, has_side_effects=True, vmem_limit_bytes=48 * 1024 * 1024
        ),
    )(*ins)
    results = tuple(pltpu.with_memory_space_constraint(x, pltpu.VMEM) for x in (out, gser, gconv, gmix))
    out, gser, gconv, gmix = pl.pallas_call(
        store_kernel,
        out_shape=tuple(pltpu.HBM(x.shape, x.dtype) for x in results),
        in_specs=[vm] * 4,
        out_specs=(hb,) * 4,
        scratch_shapes=[dma((4,))],
        compiler_params=pltpu.CompilerParams(vmem_limit_bytes=4 * 1024 * 1024),
    )(*results)
    gconv = jnp.swapaxes(gconv, 2, 3)
    return out.reshape(series.shape), gser.reshape(series.shape), gconv, gmix


def solution(mesh):
    return jax.shard_map(
        per_device,
        mesh=mesh,
        in_specs=(
            P("tm", None, "graph"),
            P(),
            P(),
            P(),
            P(),
            P("graph", None, None, None),
            P("graph", None),
            P("graph", None, None),
            P("graph", None, None),
            P("tm", None, "graph"),
        ),
        out_specs=(P("tm", None, "graph"), P("tm", None, "graph"), P(), P()),
        check_vma=False,
    )
```

```python
import functools
import math

import jax
import jax.numpy as jnp
from jax import lax
from jax.experimental import pallas as pl
from jax.experimental.pallas import tpu as pltpu
from jax.sharding import PartitionSpec as P

GATED_LAYERS = 2
HOPS = 5
BF = jnp.bfloat16
F32 = jnp.float32
MESH = pl.DeviceIdType.MESH


def dot(a, b):
    return lax.dot_general(a, b, (((1,), (0,)), ((), ())), preferred_element_type=F32)


def dot_nt(a, b):
    return lax.dot_general(a, b, (((1,), (1,)), ((), ())), preferred_element_type=F32)


def dot_tn(a, b):
    return lax.dot_general(a, b, (((0,), (0,)), ((), ())), preferred_element_type=F32)


def sigmoid(x):
    return 0.5 + 0.5 * jnp.tanh(0.5 * x)


def quot(x, n):
    return x >> (n.bit_length() - 1) if n & (n - 1) == 0 else x // n


def rest_of(x, n):
    return x & (n - 1) if n & (n - 1) == 0 else lax.rem(x, n)


def peers(count, body):
    if count <= 8:
        for off in range(count - 1, 0, -1):
            body(off)
    elif count > 1:
        lax.fori_loop(1, count, lambda off, c: (body(off), c)[1], 0)


def kernel(
    n_graph, n_tm, steps, scale,
    series_h, cw_h, cb_h, mw_h, mb_h, tv_h, tcol_h, sidx_h, smask_h, cot_h,
    out, gser, gconv, gmix,
    wl, wlt, whgm, wht, gmt, gwl, gwh, whg, band, band_h, mixall, mix_h, ext, hops, hops_h, filt, gate, flow,
    prev0, pack_s, pack_r, send, recv, send_w, recv_w, e_buf, et_buf, l_buf, lt_buf,
    e_part, eg_buf, m_buf, mt_buf, pair_s, pair_r, back_s, back_r, fin,
    series, cw, cb, mw, mb, tv, tcol, sidx, smask, cot, in_sem,
    r_ssem, r_rsem, w_ssem, w_rsem, t_ssem, t_rsem, e_ssem, e_rsem, et_ssem, et_rsem,
    l_ssem, l_rsem, lt_ssem, lt_rsem, eg_ssem, eg_rsem, m_ssem, m_rsem, mt_ssem, mt_rsem,
    pair_sem, fin_ssem, fin_rsem,
):
    me = lax.axis_index("graph")
    z = lax.axis_index("tm")
    tc, sensors = series.shape
    ch = tc // steps
    half = tc // 2
    half_s = sensors // 2
    slots = sidx.shape[1]
    halo = n_graph * slots
    tile = tv.shape[-1]
    rblocks, tslots = tcol.shape
    lblocks = sensors // tile
    hblocks = halo // tile
    wire = send.dtype
    wh = whgm.at[:, pl.ds(0, halo)]
    gm = whgm.at[:, pl.ds(halo, halo)]
    direct = fin.shape[0] > 1
    core = lax.rem(me, 2)
    mate = me + 1 - 2 * core

    def partner(off):
        if n_graph & (n_graph - 1) or n_graph > 8:
            return lax.rem(me + off, n_graph)
        p = 0
        bit = 1
        while bit < n_graph:
            p = p + lax.rem(me // bit + off // bit, 2) * bit
            bit *= 2
        return p

    er = e_part.shape[1]

    loads = [
        pltpu.make_async_copy(src, dst, in_sem.at[i])
        for i, (src, dst) in enumerate(
            ((cw_h, cw), (mw_h, mw), (cb_h, cb), (mb_h, mb), (tv_h, tv), (series_h, series),
             (sidx_h, sidx), (smask_h, smask), (cot_h, cot), (tcol_h, tcol))
        )
    ]
    for load in loads:
        load.start()
    barrier = pltpu.get_barrier_semaphore()

    def greet_graph(off):
        pl.semaphore_signal(barrier, inc=1, device_id={"graph": partner(off)}, device_id_type=MESH)

    def greet_tm(off):
        pl.semaphore_signal(barrier, inc=1, device_id={"tm": lax.rem(z + off, n_tm)}, device_id_type=MESH)

    peers(n_graph, greet_graph)
    peers(n_tm, greet_tm)

    def shift_copy(slot, src, dst, by):
        return pltpu.make_async_remote_copy(
            src_ref=src, dst_ref=dst, send_sem=t_ssem.at[slot], recv_sem=t_rsem.at[slot],
            device_id={"tm": lax.rem(z + by + n_tm, n_tm)}, device_id_type=MESH,
        )

    up = z < n_tm - 1
    down = z > 0

    firsts = [
        shift_copy(0, series_h.at[pl.ds(tc - ch, ch)], prev0.at[pl.ds(tc - ch, ch)], 1),
        shift_copy(1, series_h.at[pl.ds(tc - 3 * ch, 2 * ch)], prev0.at[pl.ds(tc - 3 * ch, 2 * ch)], 1),
    ]
    pl.semaphore_wait(barrier, n_graph - 1 + n_tm - 1)

    @pl.when(up)
    def _():
        for first in firsts:
            first.start()

    prev0[pl.ds(0, tc - 3 * ch), :] = jnp.zeros((tc - 3 * ch, sensors), BF)

    row32 = lax.broadcasted_iota(jnp.int32, (ch, tc), 0)
    lane32 = lax.broadcasted_iota(jnp.int32, (ch, tc), 1)
    spread = jnp.where(rest_of(lane32, ch) == row32, 1.0, 0.0)
    spread_b = spread.astype(BF)
    rt = lax.broadcasted_iota(jnp.int32, (tc, tc), 0)
    lt = lax.broadcasted_iota(jnp.int32, (tc, tc), 1)
    rt, lt = quot(rt, ch), quot(lt, ch)
    same = rt == lt
    late = rt >= steps // 2

    def before(d):
        return lt == rt - d

    def before_prev(d):
        return lt == rt - d + steps

    for load in loads[:4]:
        load.wait()
    taps = 2 * GATED_LAYERS
    rs = lax.broadcasted_iota(jnp.int32, (taps * ch, taps * tc), 0)
    ls = lax.broadcasted_iota(jnp.int32, (taps * ch, taps * tc), 1)
    spread_taps = jnp.where(quot(ls, tc) * ch + rest_of(ls, ch) == rs, 1.0, 0.0).astype(BF)
    def after(d):
        return rt == lt - d

    def after_prev(d):
        return rt == lt - d + steps

    cwr = dot_tn(cw[...], spread_taps)
    mwr = dot(mw[...], spread_b)

    def stack(x, base):
        return jnp.concatenate([x[base:base + ch]] * steps, axis=0)

    for l in range(GATED_LAYERS):
        d = l + 1
        for h in range(2):
            w0 = stack(cwr[:, (l * 2) * tc:(l * 2 + 1) * tc], h * ch)
            w1 = stack(cwr[:, (l * 2 + 1) * tc:(l * 2 + 2) * tc], h * ch)
            own = (jnp.where(same, w0, 0.0) + jnp.where(before(d), w1, 0.0)).astype(BF)
            band[l, pl.ds(h * tc, tc), pl.ds(0, tc)] = own
            band[l, pl.ds(h * tc, tc), pl.ds(tc, tc)] = jnp.where(before_prev(d), w1, 0.0).astype(BF)
            if l == 0:
                band_h[pl.ds(h * tc, tc), :] = jnp.concatenate([own[half:], own[half:]], axis=0)
        for k in range(HOPS):
            mk = stack(mwr, (l * HOPS + k) * ch)
            mixall[l, :, pl.ds(k * tc, tc)] = jnp.where(same, mk, 0.0).astype(BF)
            if l == 0:
                at = (rt == lt + steps // 2) if k in (1, 2) else (same & late)
                mix_h[:, pl.ds(k * tc, tc)] = jnp.where(at, mk, 0.0).astype(BF)

    r64 = lax.broadcasted_iota(jnp.int32, (2 * ch, 2 * tc), 0)
    l64 = lax.broadcasted_iota(jnp.int32, (2 * ch, 2 * tc), 1)
    spread2 = jnp.where(rest_of(l64, ch) + quot(l64, tc) * ch == r64, 1.0, 0.0)
    cbias = lax.dot_general(cb[...], spread2, (((1,), (0,)), ((), ())), precision=lax.Precision.HIGHEST, preferred_element_type=F32)
    mbias = lax.dot_general(mb[...], spread, (((1,), (0,)), ((), ())), precision=lax.Precision.HIGHEST, preferred_element_type=F32)

    for load in loads[4:]:
        load.wait()
    def on(r, k, c):
        return (tcol[r, k] == c).astype(jnp.int32).astype(F32)

    def placed(blocks, r, c):
        y = blocks[0] * on(r, 0, c)
        for k in range(1, tslots):
            y = y + blocks[k] * on(r, k, c)
        return y.astype(BF)

    def flipped(r):
        return [tv[r * tslots + k].astype(F32).T for k in range(tslots)]

    for r in range(rblocks):
        flips = flipped(r)
        for c in range(hblocks):
            wht[pl.ds(c * tile, tile), pl.ds(r * tile, tile)] = placed(flips, r, lblocks + c)

    def build_rest():
        for r in range(rblocks):
            tiles = [tv[r * tslots + k].astype(F32) for k in range(tslots)]
            flips = flipped(r)
            for c in range(lblocks):
                wl[pl.ds(r * tile, tile), pl.ds(c * tile, tile)] = placed(tiles, r, c)
                wlt[pl.ds(c * tile, tile), pl.ds(r * tile, tile)] = placed(flips, r, c)
            for c in range(hblocks):
                wh[pl.ds(r * tile, tile), pl.ds(c * tile, tile)] = placed(tiles, r, lblocks + c)

    key = jnp.where(smask[...] != 0, sidx[...] + 1, 0)
    es = lax.broadcasted_iota(jnp.int32, (slots, halo), 0)
    ej = lax.broadcasted_iota(jnp.int32, (slots, halo), 1)
    pick = jnp.where(rest_of(ej, slots) == es, 1.0, 0.0).astype(BF)
    hi = dot((key >> 5).astype(F32).astype(BF), pick)
    lo = dot((key & 31).astype(F32).astype(BF), pick)
    pr = lax.broadcasted_iota(jnp.int32, (n_graph, halo), 0)
    pj = quot(lax.broadcasted_iota(jnp.int32, (n_graph, halo), 1), slots)
    keys = jnp.sum(jnp.where(pr == pj, hi * 32.0 + lo, 0.0), axis=0, keepdims=True)
    ids = lax.broadcasted_iota(jnp.int32, (sensors, halo), 0).astype(F32) + 1.0
    onehot = jnp.where(ids == keys, 1.0, 0.0)
    gm[...] = onehot.astype(BF)
    gmt[...] = onehot.T.astype(BF)

    def graph_copy(src, dst, ssem, rsem, p):
        return pltpu.make_async_remote_copy(
            src_ref=src, dst_ref=dst, send_sem=ssem, recv_sem=rsem,
            device_id={"graph": p}, device_id_type=MESH,
        )

    def tm_copy(src, dst, ssem, rsem, p):
        return pltpu.make_async_remote_copy(
            src_ref=src, dst_ref=dst, send_sem=ssem, recv_sem=rsem,
            device_id={"tm": p}, device_id_type=MESH,
        )

    lane_low = lax.broadcasted_iota(jnp.int32, (halo, tc), 1) < half

    def ship(blocks, out_buf, in_buf, ssem, rsem, r):
        for i, block in enumerate(blocks):
            out_buf[r, :, i] = block.astype(BF).reshape(n_graph, slots, tc).astype(wire)

        def go(off):
            p = partner(off)
            graph_copy(out_buf.at[r, p], in_buf.at[r, me], ssem.at[r, p], rsem.at[r], p).start()

        peers(n_graph, go)
        in_buf[r, me] = out_buf[r, me]

    def collect(in_buf, ssem, rsem, r, count):
        arrived = in_buf.at[r, pl.ds(0, n_graph - 1)]
        graph_copy(arrived, arrived, ssem.at[r, 0], rsem.at[r], partner(1)).wait_recv()
        return [in_buf[r, :, i].reshape(halo, tc).astype(BF) for i in range(count)]

    def launch(r, pull_in, push_in):
        ship((dot(gmt[...], pull_in), dot(wht[...], push_in)), send, recv, r_ssem, r_rsem, r)

    def launch_w(r, pull_in, push_in):
        ship_w(r, dot(gmt[...], pull_in), dot(wht[...], push_in))

    def ship_w(r, sp, sb):
        packed = jnp.where(lane_low, sp[:, tc:], sb[:, tc:])
        ship((sp[:, :tc], sb[:, :tc], packed), send_w, recv_w, w_ssem, w_rsem, r)

    def local(pull_in, push_in):
        return dot(wl[...], pull_in), dot(wlt[...], push_in)

    def land(r):
        return collect(recv, r_ssem, r_rsem, r, 2)

    def land_w(r):
        rp, rb, both = collect(recv_w, w_ssem, w_rsem, r, 3)
        return jnp.concatenate([rp, both], axis=1), jnp.concatenate([rb, both], axis=1)

    def relay(r, rp, rb, sp, sb):
        ship((sp + dot(gwh[...], rp), sb + dot(whg[...], rb)), send, recv, r_ssem, r_rsem, r)

    def joined(a, b):
        return dot(whgm[...], jnp.concatenate([a, b], axis=0))

    def whole(pulled, pushed, rp, rb):
        return pulled + dot(wh[...], rp), pushed + dot(gm[...], rb)

    lane_half = lax.broadcasted_iota(jnp.int32, (half_s, tc), 1) < half

    def pack(x):
        return jnp.where(lane_half, pltpu.roll(x[:half_s], half, 1), x[half_s:]).astype(BF)

    def unpack(p):
        x = p.astype(F32)
        return jnp.concatenate([pltpu.roll(x, half, 1), x], axis=0)

    lane_g = quot(lax.broadcasted_iota(jnp.int32, (ch, tc), 1), ch)

    def fold(x):
        y = x[0:ch]
        for t in range(1, steps):
            y = y + x[t * ch:(t + 1) * ch]
        sh = ch
        while sh < tc:
            y = y + pltpu.roll(y, sh, 1)
            sh *= 2
        return y

    def lanes_of(xs):
        y = jnp.zeros((ch, tc), F32)
        for g, x in enumerate(xs):
            y = jnp.where(lane_g == g, x, y)
        return y

    def gather_start(buf, ssem, rsem, count, here, copy):
        def go(off):
            p = lax.rem(here + off, count)
            copy(buf.at[here], buf.at[here], ssem.at[p], rsem.at[here], p).start()

        peers(count, go)

    def gather_sum(buf, ssem, rsem, count, here, copy):
        def take(off):
            p = lax.rem(here + off, count)
            copy(buf.at[p], buf.at[p], ssem.at[p], rsem.at[p], p).wait_recv()

        peers(count, take)
        total = buf[0]
        for p in range(1, count):
            total = total + buf[p]
        return total

    def hop_grad(fr, l, k):
        return dot(fr, mixall[l, :, pl.ds(k * tc, tc)])

    def mix_fold(l, fr, ks):
        folds = []
        for k in ks:
            hop = hops[l, :, pl.ds(k * tc, tc)]
            folds.append(fold(jnp.where(same, dot(cot[...], hop) if l == 1 else dot_tn(fr, hop), 0.0)))
        return folds

    def conv_fold(l, gp):
        d = l + 1
        if l == 0:
            prod = (dot(series[...], gp), dot(prev0[...], gp))
        else:
            prod = [dot_tn(ext[l, :, pl.ds(i * tc, tc)], gp) for i in range(2)]
        pieces = []
        for tap in range(2):
            for h in range(2):
                own = prod[0][:, h * tc:(h + 1) * tc]
                if tap == 0:
                    x = jnp.where(same, own, 0.0)
                else:
                    x = jnp.where(after(d), own, 0.0) + jnp.where(after_prev(d), prod[1][:, h * tc:(h + 1) * tc], 0.0)
                pieces.append(fold(x))
        return lanes_of(pieces)

    def pre_grad(l, gg):
        f = filt[l]
        g = gate[l]
        return jnp.concatenate([gg * g * (1.0 - f * f), gg * f * g * (1.0 - g)], axis=1).astype(BF)

    def lag_pack(i, l, gp):
        pack_s[i] = pack(dot(gp, band[l, :, pl.ds(tc, tc)]))

    def lag_start(i):
        @pl.when(down)
        def _():
            shift_copy(2 + i, pack_s.at[i], pack_r.at[i], -1).start()

    lanes_late = lax.broadcasted_iota(jnp.int32, (sensors, tc), 1) >= half

    def lag_take(i):
        @pl.when(up)
        def _():
            shift_copy(2 + i, pack_s.at[i], pack_r.at[i], -1).wait_recv()

        @pl.when(jnp.logical_not(up))
        def _():
            pack_r[i] = jnp.zeros((half_s, tc), BF)

        return jnp.where(lanes_late, unpack(pack_r[i]), 0.0)

    flow[...] = cot[...].astype(F32).T
    fr1 = flow[...].astype(BF)
    h4, h2 = hop_grad(fr1, 1, 4).astype(BF), hop_grad(fr1, 1, 2).astype(BF)
    launch(0, h4, h2)

    def mid_back(fr, l, pull_in, push_in):
        pulled, pushed = local(pull_in, push_in)
        pulled = pulled + hop_grad(fr, l, 3)
        pushed = pushed + hop_grad(fr, l, 1)
        sp = dot(gwl[...], pull_in) + hop_grad(dot(gmt[...], fr).astype(BF), l, 3)
        return pulled, pushed, sp, dot(wht[...], pushed.astype(BF))

    def mid(pull_in, push_in):
        pulled, pushed = local(pull_in, push_in)
        return pulled, pushed, dot(gwl[...], pull_in), dot(wht[...], pushed.astype(BF))

    ext[0, :, pl.ds(0, tc)] = series[...].astype(F32).T.astype(BF)

    @pl.when(down)
    def _():
        for first in firsts:
            first.wait_recv()

    @pl.when(jnp.logical_not(down))
    def _():
        prev0[pl.ds(tc - 3 * ch, 3 * ch), :] = jnp.zeros((3 * ch, sensors), BF)

    prev_t = prev0[...].astype(F32).T
    ext[0, :, pl.ds(tc, tc)] = prev_t.astype(BF)
    pre = dot_nt(ext[0], band[0]) + cbias[0:1]
    f = jnp.tanh(pre[:, :tc])
    g = sigmoid(pre[:, tc:])
    filt[0] = f
    gate[0] = g
    gated = (f * g).astype(BF)
    pre = dot_nt(ext[0, :, pl.ds(tc, tc)], band_h[...]) + cbias[0:1]
    gated_h = (jnp.tanh(pre[:, :tc]) * sigmoid(pre[:, tc:])).astype(BF)
    both = jnp.concatenate([gated, gated_h], axis=1)
    launch_w(0, both, both)

    def keep(k, x):
        hops[0, :, pl.ds(k * tc, tc)] = x[:, :tc]
        hops_h[:, pl.ds(k * tc, tc)] = x[:, tc:]

    keep(0, both)
    build_rest()
    gwl[...] = dot(gmt[...], wl[...]).astype(BF)
    gwh[...] = dot(gmt[...], wh[...]).astype(BF)
    whg[...] = dot(wht[...], gm[...]).astype(BF)
    ab = mid_back(fr1, 1, h4, h2)
    af = mid(both, both)

    rp, rb = land(0)
    relay(1, rp, rb, *ab[2:])
    bi, fi = whole(*ab[:2], rp, rb)
    bb = local(bi.astype(BF), fi.astype(BF))
    gg0 = hop_grad(fr1, 1, 0)

    rp, rb = land_w(0)
    ship_w(1, af[2] + dot(gwh[...], rp), af[3] + dot(whg[...], rb))
    fo, bo = whole(*af[:2], rp, rb)
    fo, bo = fo.astype(BF), bo.astype(BF)
    keep(1, fo)
    keep(3, bo)
    bf = local(fo, bo)

    def mix_three(mat, hop):
        m = dot_nt(hop(0, 2), mat(0, 2))
        return m + dot_nt(hop(3, 1), mat(3, 1))

    def mat_of(l):
        return lambda k, n: mixall[l, :, pl.ds(k * tc, n * tc)]

    def hop_of(l):
        return lambda k, n: hops[l, :, pl.ds(k * tc, n * tc)]

    part = mix_three(mat_of(0), hop_of(0))
    part_h = mix_three(
        lambda k, n: mix_h[:, pl.ds(k * tc, n * tc)], lambda k, n: hops_h[:, pl.ds(k * tc, n * tc)]
    )

    gg1 = gg0 + bb[0] + bb[1]
    gg1 = gg1 + joined(*land(1))

    def two_late(a, b):
        e = dot_nt(a[:, :tc], mixall[0, :, pl.ds(2 * tc, tc)]), dot_nt(b[:, :tc], mixall[0, :, pl.ds(4 * tc, tc)])
        h = dot_nt(a[:, tc:], mix_h[:, pl.ds(2 * tc, tc)]), dot_nt(b[:, tc:], mix_h[:, pl.ds(4 * tc, tc)])
        return [jnp.concatenate([x, y], axis=1) for x, y in zip(e, h)]

    known = two_late(bf[0].astype(BF), bf[1].astype(BF))
    mbias2 = jnp.concatenate([mbias[0:1], mbias[0:1]], axis=1)
    hid = ext[0].astype(F32) + mbias2 + jnp.concatenate([part, part_h], axis=1) + known[0] + known[1]

    rp, rb = land_w(1)
    hid = hid + joined(*[x.astype(BF) for x in two_late(rp, rb)])
    lane2 = lax.broadcasted_iota(jnp.int32, (sensors, 2 * tc), 1)
    ext[1] = jnp.where((lane2 < tc) | ((lane2 >= tc + half) & down), hid, 0.0).astype(BF)

    pre = dot_nt(ext[1], band[1]) + cbias[1:2]
    f = jnp.tanh(pre[:, :tc])
    g = sigmoid(pre[:, tc:])
    filt[1] = f
    gate[1] = g
    gp1 = pre_grad(1, gg1)
    lag_pack(0, 1, gp1)
    lag_start(0)
    gated = (f * g).astype(BF)
    hops[1, :, pl.ds(0, tc)] = gated
    launch(2, gated, gated)
    f2, b2 = whole(bf[0][:, :tc], bf[1][:, :tc], rp[:, :tc], rb[:, :tc])
    hops[0, :, pl.ds(2 * tc, tc)] = f2.astype(BF)
    hops[0, :, pl.ds(4 * tc, tc)] = b2.astype(BF)
    cf = mid(gated, gated)
    new = flow[...] + dot(gp1, band[1, :, pl.ds(0, tc)])
    conv1 = conv_fold(1, gp1)

    flow[...] = new + lag_take(0)
    fr0 = flow[...].astype(BF)
    h4, h2 = hop_grad(fr0, 0, 4).astype(BF), hop_grad(fr0, 0, 2).astype(BF)
    launch(4, h4, h2)
    rp, rb = land(2)
    relay(3, rp, rb, *cf[2:])
    fo, bo = whole(*cf[:2], rp, rb)
    fo, bo = fo.astype(BF), bo.astype(BF)
    hops[1, :, pl.ds(tc, tc)] = fo
    hops[1, :, pl.ds(3 * tc, tc)] = bo
    mix0 = mix_fold(0, fr0, range(HOPS))
    mix1 = mix_fold(1, fr1, (0, 1, 3))
    early = jnp.concatenate([conv1, lanes_of(mix0[:4]), lanes_of([mix0[4]] + mix1)], axis=0)
    for p in range(n_graph):
        e_part[p] = early[p * er:(p + 1) * er]

    def scatter(off):
        p = partner(off)
        graph_copy(e_part.at[p], e_buf.at[me], e_ssem.at[p], e_rsem.at[me], p).start()

    peers(n_graph, scatter)
    e_buf[me] = e_part[me]
    cb_ = mid_back(fr0, 0, h4, h2)
    df = local(fo, bo)
    gg0 = hop_grad(fr0, 0, 0)
    part = mix_three(mat_of(1), hop_of(1))

    rp, rb = land(4)
    relay(5, rp, rb, *cb_[2:])
    bi, fi = whole(*cb_[:2], rp, rb)
    db = local(bi.astype(BF), fi.astype(BF))
    et_buf[z] = gather_sum(e_buf, e_ssem, e_rsem, n_graph, me, graph_copy)
    gather_start(et_buf, et_ssem, et_rsem, n_tm, z, tm_copy)

    f2, b2 = whole(*df, *land(3))
    f2, b2 = f2.astype(BF), b2.astype(BF)
    hops[1, :, pl.ds(2 * tc, tc)] = f2
    hops[1, :, pl.ds(4 * tc, tc)] = b2
    a2, a4 = mix_fold(1, fr1, (2, 4))
    hc = ch // 2
    last = jnp.zeros((hc, tc), F32)
    for g, x in enumerate((a2[:hc], a4[:hc], a2[hc:], a4[hc:])):
        last = jnp.where(lane_g[:hc] == g, x, last)
    m_buf[me] = last
    gather_start(m_buf, m_ssem, m_rsem, n_graph, me, graph_copy)
    mixed = part + dot_nt(f2, mixall[1, :, pl.ds(2 * tc, tc)]) + dot_nt(b2, mixall[1, :, pl.ds(4 * tc, tc)])
    out[...] = (ext[1, :, pl.ds(0, tc)].astype(F32) + (mixed + mbias[1:2])).T.astype(BF)

    gg0 = gg0 + db[0] + db[1]
    gp0 = pre_grad(0, gg0 + joined(*land(5)))
    lag_pack(1, 0, gp0)
    lag_start(1)
    conv0 = conv_fold(0, gp0)
    if direct:
        swap = graph_copy(pair_s, pair_r, pair_sem.at[0], pair_sem.at[1], mate)
        low = core == 0
        pair_s[...] = jnp.where(low, conv0[hc:], conv0[:hc])
        swap.start()
    else:
        l_buf[me] = conv0
        gather_start(l_buf, l_ssem, l_rsem, n_graph, me, graph_copy)

    here = (z * n_graph + me) // 2

    def final_copy(goff, toff):
        p = partner(goff) if goff else me
        return pltpu.make_async_remote_copy(
            src_ref=fin.at[here], dst_ref=fin.at[here],
            send_sem=fin_ssem.at[toff * n_graph + goff], recv_sem=fin_rsem.at[0],
            device_id={"graph": p, "tm": lax.rem(z + toff, n_tm)}, device_id_type=MESH,
        )

    others = [(g, t) for t in range(n_tm) for g in range(0, n_graph, 2) if (g, t) != (0, 0)] if direct else []
    if direct:
        swap.wait_recv()
        fin[here] = (jnp.where(low, conv0[:hc], conv0[hc:]) + pair_r[...]).astype(BF)
        for g, t in reversed(others):
            final_copy(g, t).start()
    mt_buf[z] = gather_sum(m_buf, m_ssem, m_rsem, n_graph, me, graph_copy)
    gather_start(mt_buf, mt_ssem, mt_rsem, n_tm, z, tm_copy)
    eg_buf[me] = gather_sum(et_buf, et_ssem, et_rsem, n_tm, z, tm_copy)
    gather_start(eg_buf, eg_ssem, eg_rsem, n_graph, me, graph_copy)
    if not direct:
        lt_buf[z] = gather_sum(l_buf, l_ssem, l_rsem, n_graph, me, graph_copy)
        gather_start(lt_buf, lt_ssem, lt_rsem, n_tm, z, tm_copy)
    new = flow[...] + dot(gp0, band[0, :, pl.ds(0, tc)])
    gser[...] = (new + lag_take(1)).T.astype(BF)

    def lane_group(x, g):
        return (pltpu.roll(x, tc - g * ch, 1) if g else x)[:, :ch]

    def put_conv(l, x):
        gconv[l, 0] = x[:, :2 * ch]
        gconv[l, 1] = pltpu.roll(x, tc - 2 * ch, 1)[:, :2 * ch]

    m = gather_sum(mt_buf, mt_ssem, mt_rsem, n_tm, z, tm_copy) * scale
    for i, k in enumerate((2, 4)):
        gmix[1, k, pl.ds(0, hc)] = lane_group(m, i)
        gmix[1, k, pl.ds(hc, hc)] = lane_group(m, i + 2)

    def take_group(off):
        p = partner(off)
        graph_copy(eg_buf.at[p], eg_buf.at[p], eg_ssem.at[p], eg_rsem.at[p], p).wait_recv()

    peers(n_graph, take_group)
    e = jnp.concatenate([eg_buf[p] for p in range(n_graph)], axis=0) * scale
    put_conv(1, e[:ch])
    for k in range(4):
        gmix[0, k] = lane_group(e[ch:2 * ch], k)
    gmix[0, 4] = lane_group(e[2 * ch:], 0)
    for i, k in enumerate((0, 1, 3)):
        gmix[1, k] = lane_group(e[2 * ch:], i + 1)
    if direct:
        count = fin.shape[0]
        arrived = fin.at[pl.ds(0, count - 1)]
        pltpu.make_async_remote_copy(
            src_ref=arrived, dst_ref=arrived, send_sem=fin_ssem.at[2], recv_sem=fin_rsem.at[0],
            device_id={"graph": mate}, device_id_type=MESH,
        ).wait_recv()
        total = fin[0].astype(F32)
        for p in range(1, count):
            total = total + fin[p].astype(F32)
        back_s[...] = total
        back = graph_copy(back_s, back_r, pair_sem.at[2], pair_sem.at[3], mate)
        back.start()
        back.wait_recv()
        theirs = back_r[...]
        halves = [jnp.where(low, total, theirs), jnp.where(low, theirs, total)]
        put_conv(0, jnp.concatenate(halves, axis=0) * scale)
        back.wait_send()
        swap.wait_send()
        for g, t in others:
            final_copy(g, t).wait_send()
    else:
        put_conv(0, gather_sum(lt_buf, lt_ssem, lt_rsem, n_tm, z, tm_copy) * scale)

    def sent_graph(off):
        p = partner(off)
        for r in range(send.shape[0]):
            graph_copy(send.at[r, p], recv.at[r, me], r_ssem.at[r, p], r_rsem.at[r], p).wait_send()
        for r in range(send_w.shape[0]):
            graph_copy(send_w.at[r, p], recv_w.at[r, me], w_ssem.at[r, p], w_rsem.at[r], p).wait_send()
        graph_copy(e_part.at[p], e_buf.at[me], e_ssem.at[p], e_rsem.at[me], p).wait_send()
        graph_copy(eg_buf.at[me], eg_buf.at[me], eg_ssem.at[p], eg_rsem.at[me], p).wait_send()
        graph_copy(m_buf.at[me], m_buf.at[me], m_ssem.at[p], m_rsem.at[me], p).wait_send()
        if not direct:
            graph_copy(l_buf.at[me], l_buf.at[me], l_ssem.at[p], l_rsem.at[me], p).wait_send()

    peers(n_graph, sent_graph)

    def sent_tm(off):
        p = lax.rem(z + off, n_tm)
        tm_copy(et_buf.at[z], et_buf.at[z], et_ssem.at[p], et_rsem.at[z], p).wait_send()
        tm_copy(mt_buf.at[z], mt_buf.at[z], mt_ssem.at[p], mt_rsem.at[z], p).wait_send()
        if not direct:
            tm_copy(lt_buf.at[z], lt_buf.at[z], lt_ssem.at[p], lt_rsem.at[z], p).wait_send()

    peers(n_tm, sent_tm)

    @pl.when(up)
    def _():
        for first in firsts:
            first.wait_send()

    @pl.when(down)
    def _():
        shift_copy(2, pack_s.at[0], pack_r.at[0], -1).wait_send()
        shift_copy(3, pack_s.at[1], pack_r.at[1], -1).wait_send()


def store_kernel(a, b, c, d, ao, bo, co, do, sem):
    copies = [
        pltpu.make_async_copy(src, dst, sem.at[i])
        for i, (src, dst) in enumerate(((a, ao), (b, bo), (c, co), (d, do)))
    ]
    for copy in copies:
        copy.start()
    for copy in copies:
        copy.wait()


def per_device(series, cw, cb, mw, mb, tv, tcol, sidx, smask, cot):
    n_graph = lax.axis_size("graph")
    n_tm = lax.axis_size("tm")
    steps, ch, sensors = series.shape
    tc = steps * ch
    slots = sidx.shape[2]
    halo = n_graph * slots
    wire = BF if slots % 16 == 0 else F32
    narrow, wide = 6, 2
    scale = 1.0 / math.sqrt(float(steps * n_tm * sensors * n_graph))
    vm = pl.BlockSpec(memory_space=pltpu.VMEM)
    hb = pl.BlockSpec(memory_space=pltpu.HBM)
    cwt_shape = (*cw.shape[:2], cw.shape[3], cw.shape[2])
    ins = (
        series.reshape(tc, sensors),
        jnp.swapaxes(cw, 2, 3).reshape(-1, cw.shape[2]),
        cb,
        mw.reshape(-1, ch),
        mb,
        tv.reshape(-1, *tv.shape[2:]),
        tcol,
        sidx[0],
        smask[0],
        cot.reshape(tc, sensors),
    )
    er = 3 * ch // n_graph
    direct = n_graph % 2 == 0 and n_graph * n_tm <= 32 and ch % 32 == 0
    n_all = n_graph * n_tm if direct else 1
    ins = tuple(pltpu.with_memory_space_constraint(x, pltpu.HBM) for x in ins)
    dma = pltpu.SemaphoreType.DMA
    out, gser, gconv, gmix = pl.pallas_call(
        functools.partial(kernel, n_graph, n_tm, steps, scale),
        out_shape=(
            pltpu.VMEM((tc, sensors), BF),
            pltpu.VMEM((tc, sensors), BF),
            pltpu.VMEM(cwt_shape, F32),
            pltpu.VMEM(mw.shape, F32),
        ),
        in_specs=[hb] * 10,
        out_specs=(vm,) * 4,
        scratch_shapes=[
            pltpu.VMEM((sensors, sensors), BF),
            pltpu.VMEM((sensors, sensors), BF),
            pltpu.VMEM((sensors, 2 * halo), BF),
            pltpu.VMEM((halo, sensors), BF),
            pltpu.VMEM((halo, sensors), BF),
            pltpu.VMEM((halo, sensors), BF),
            pltpu.VMEM((halo, halo), BF),
            pltpu.VMEM((halo, halo), BF),
            pltpu.VMEM((GATED_LAYERS, 2 * tc, 2 * tc), BF),
            pltpu.VMEM((2 * tc, tc), BF),
            pltpu.VMEM((GATED_LAYERS, tc, HOPS * tc), BF),
            pltpu.VMEM((tc, HOPS * tc), BF),
            pltpu.VMEM((GATED_LAYERS, sensors, 2 * tc), BF),
            pltpu.VMEM((GATED_LAYERS, sensors, HOPS * tc), BF),
            pltpu.VMEM((sensors, HOPS * tc), BF),
            pltpu.VMEM((GATED_LAYERS, sensors, tc), F32),
            pltpu.VMEM((GATED_LAYERS, sensors, tc), F32),
            pltpu.VMEM((sensors, tc), F32),
            pltpu.VMEM((tc, sensors), BF),
            pltpu.VMEM((2, sensors // 2, tc), BF),
            pltpu.VMEM((2, sensors // 2, tc), BF),
            pltpu.VMEM((narrow, n_graph, 2, slots, tc), wire),
            pltpu.VMEM((narrow, n_graph, 2, slots, tc), wire),
            pltpu.VMEM((wide, n_graph, 3, slots, tc), wire),
            pltpu.VMEM((wide, n_graph, 3, slots, tc), wire),
            pltpu.VMEM((n_graph, er, tc), F32),
            pltpu.VMEM((n_tm, er, tc), F32),
            pltpu.VMEM((n_graph, ch, tc), F32),
            pltpu.VMEM((n_tm, ch, tc), F32),
            pltpu.VMEM((n_graph, er, tc), F32),
            pltpu.VMEM((n_graph, er, tc), F32),
            pltpu.VMEM((n_graph, ch // 2, tc), F32),
            pltpu.VMEM((n_tm, ch // 2, tc), F32),
            *[pltpu.VMEM((ch // 2, tc), F32)] * 4,
            pltpu.VMEM((max(n_all // 2, 1), ch // 2, tc), BF),
            *[(pltpu.SMEM if x.shape == tcol.shape else pltpu.VMEM)(x.shape, x.dtype) for x in ins],
            dma((10,)),
            dma((narrow, n_graph)), dma((narrow,)),
            dma((wide, n_graph)), dma((wide,)),
            dma((4,)), dma((4,)),
            dma((n_graph,)), dma((n_graph,)),
            dma((n_tm,)), dma((n_tm,)),
            dma((n_graph,)), dma((n_graph,)),
            dma((n_tm,)), dma((n_tm,)),
            dma((n_graph,)), dma((n_graph,)),
            dma((n_graph,)), dma((n_graph,)),
            dma((n_tm,)), dma((n_tm,)),
            dma((4,)), dma((n_all,)), dma((1,)),
        ],
        compiler_params=pltpu.CompilerParams(
            collective_id=0, has_side_effects=True, vmem_limit_bytes=48 * 1024 * 1024
        ),
    )(*ins)
    results = tuple(pltpu.with_memory_space_constraint(x, pltpu.VMEM) for x in (out, gser, gconv, gmix))
    out, gser, gconv, gmix = pl.pallas_call(
        store_kernel,
        out_shape=tuple(pltpu.HBM(x.shape, x.dtype) for x in results),
        in_specs=[vm] * 4,
        out_specs=(hb,) * 4,
        scratch_shapes=[dma((4,))],
        compiler_params=pltpu.CompilerParams(vmem_limit_bytes=4 * 1024 * 1024),
    )(*results)
    gconv = jnp.swapaxes(gconv, 2, 3)
    return out.reshape(series.shape), gser.reshape(series.shape), gconv, gmix


def solution(mesh):
    return jax.shard_map(
        per_device,
        mesh=mesh,
        in_specs=(
            P("tm", None, "graph"),
            P(),
            P(),
            P(),
            P(),
            P("graph", None, None, None),
            P("graph", None),
            P("graph", None, None),
            P("graph", None, None),
            P("tm", None, "graph"),
        ),
        out_specs=(P("tm", None, "graph"), P("tm", None, "graph"), P(), P()),
        check_vma=False,
    )
```

```python
import functools
import math

import jax
import jax.numpy as jnp
from jax import lax
from jax.experimental import pallas as pl
from jax.experimental.pallas import tpu as pltpu
from jax.sharding import PartitionSpec as P

GATED_LAYERS = 2
HOPS = 5
BF = jnp.bfloat16
F32 = jnp.float32
MESH = pl.DeviceIdType.MESH


def dot(a, b):
    return lax.dot_general(a, b, (((1,), (0,)), ((), ())), preferred_element_type=F32)


def dot_nt(a, b):
    return lax.dot_general(a, b, (((1,), (1,)), ((), ())), preferred_element_type=F32)


def dot_tn(a, b):
    return lax.dot_general(a, b, (((0,), (0,)), ((), ())), preferred_element_type=F32)


def sigmoid(x):
    return 0.5 + 0.5 * jnp.tanh(0.5 * x)


def quot(x, n):
    return x >> (n.bit_length() - 1) if n & (n - 1) == 0 else x // n


def rest_of(x, n):
    return x & (n - 1) if n & (n - 1) == 0 else lax.rem(x, n)


def peers(count, body):
    if count <= 8:
        for off in range(count - 1, 0, -1):
            body(off)
    elif count > 1:
        lax.fori_loop(1, count, lambda off, c: (body(off), c)[1], 0)


def kernel(
    n_graph, n_tm, steps, scale,
    series_h, cw_h, cb_h, mw_h, mb_h, tv_h, tcol_h, sidx_h, smask_h, cot_h,
    out, gser, gconv, gmix,
    wl, wlt, whgm, wht, gmt, gwl, gwh, whg, band, band_h, mixall, mix_h, ext, hops, hops_h, filt, gate, flow,
    prev0, pack_s, pack_r, send, recv, send_h, recv_h, e_buf, et_buf, l_buf, lt_buf,
    e_part, eg_buf, m_buf, mt_buf, pair_s, pair_r, back_s, back_r, fin,
    series, cw, cb, mw, mb, tv, tcol, sidx, smask, cot, in_sem,
    r_ssem, r_rsem, h_ssem, h_rsem, t_ssem, t_rsem, e_ssem, e_rsem, et_ssem, et_rsem,
    l_ssem, l_rsem, lt_ssem, lt_rsem, eg_ssem, eg_rsem, m_ssem, m_rsem, mt_ssem, mt_rsem,
    pair_sem, fin_ssem, fin_rsem,
):
    me = lax.axis_index("graph")
    z = lax.axis_index("tm")
    tc, sensors = series.shape
    ch = tc // steps
    half = tc // 2
    half_s = sensors // 2
    slots = sidx.shape[1]
    halo = n_graph * slots
    tile = tv.shape[-1]
    rblocks, tslots = tcol.shape
    lblocks = sensors // tile
    hblocks = halo // tile
    wire = send.dtype
    wh = whgm.at[:, pl.ds(0, halo)]
    gm = whgm.at[:, pl.ds(halo, halo)]
    direct = fin.shape[0] > 1
    core = lax.rem(me, 2)
    mate = me + 1 - 2 * core

    def partner(off):
        if n_graph & (n_graph - 1) or n_graph > 8:
            return lax.rem(me + off, n_graph)
        p = 0
        bit = 1
        while bit < n_graph:
            p = p + lax.rem(me // bit + off // bit, 2) * bit
            bit *= 2
        return p

    er = e_part.shape[1]

    loads = [
        pltpu.make_async_copy(src, dst, in_sem.at[i])
        for i, (src, dst) in enumerate(
            ((cw_h, cw), (mw_h, mw), (cb_h, cb), (mb_h, mb), (tv_h, tv), (series_h, series),
             (sidx_h, sidx), (smask_h, smask), (cot_h, cot), (tcol_h, tcol))
        )
    ]
    for load in loads:
        load.start()
    barrier = pltpu.get_barrier_semaphore()

    def greet_graph(off):
        pl.semaphore_signal(barrier, inc=1, device_id={"graph": partner(off)}, device_id_type=MESH)

    def greet_tm(off):
        pl.semaphore_signal(barrier, inc=1, device_id={"tm": lax.rem(z + off, n_tm)}, device_id_type=MESH)

    peers(n_graph, greet_graph)
    peers(n_tm, greet_tm)

    def shift_copy(slot, src, dst, by):
        return pltpu.make_async_remote_copy(
            src_ref=src, dst_ref=dst, send_sem=t_ssem.at[slot], recv_sem=t_rsem.at[slot],
            device_id={"tm": lax.rem(z + by + n_tm, n_tm)}, device_id_type=MESH,
        )

    up = z < n_tm - 1
    down = z > 0

    firsts = [
        shift_copy(0, series_h.at[pl.ds(tc - ch, ch)], prev0.at[pl.ds(tc - ch, ch)], 1),
        shift_copy(1, series_h.at[pl.ds(tc - 3 * ch, 2 * ch)], prev0.at[pl.ds(tc - 3 * ch, 2 * ch)], 1),
    ]
    pl.semaphore_wait(barrier, n_graph - 1 + n_tm - 1)

    @pl.when(up)
    def _():
        for first in firsts:
            first.start()

    prev0[pl.ds(0, tc - 3 * ch), :] = jnp.zeros((tc - 3 * ch, sensors), BF)

    row32 = lax.broadcasted_iota(jnp.int32, (ch, tc), 0)
    lane32 = lax.broadcasted_iota(jnp.int32, (ch, tc), 1)
    spread = jnp.where(rest_of(lane32, ch) == row32, 1.0, 0.0)
    spread_b = spread.astype(BF)
    rt = lax.broadcasted_iota(jnp.int32, (tc, tc), 0)
    lt = lax.broadcasted_iota(jnp.int32, (tc, tc), 1)
    rt, lt = quot(rt, ch), quot(lt, ch)
    same = rt == lt
    late = rt >= steps // 2

    def before(d):
        return lt == rt - d

    def before_prev(d):
        return lt == rt - d + steps

    for load in loads[:4]:
        load.wait()
    taps = 2 * GATED_LAYERS
    rs = lax.broadcasted_iota(jnp.int32, (taps * ch, taps * tc), 0)
    ls = lax.broadcasted_iota(jnp.int32, (taps * ch, taps * tc), 1)
    spread_taps = jnp.where(quot(ls, tc) * ch + rest_of(ls, ch) == rs, 1.0, 0.0).astype(BF)
    def after(d):
        return rt == lt - d

    def after_prev(d):
        return rt == lt - d + steps

    cwr = dot_tn(cw[...], spread_taps)
    mwr = dot(mw[...], spread_b)

    def stack(x, base):
        return jnp.concatenate([x[base:base + ch]] * steps, axis=0)

    for l in range(GATED_LAYERS):
        d = l + 1
        for h in range(2):
            w0 = stack(cwr[:, (l * 2) * tc:(l * 2 + 1) * tc], h * ch)
            w1 = stack(cwr[:, (l * 2 + 1) * tc:(l * 2 + 2) * tc], h * ch)
            own = (jnp.where(same, w0, 0.0) + jnp.where(before(d), w1, 0.0)).astype(BF)
            band[l, pl.ds(h * tc, tc), pl.ds(0, tc)] = own
            band[l, pl.ds(h * tc, tc), pl.ds(tc, tc)] = jnp.where(before_prev(d), w1, 0.0).astype(BF)
            if l == 0:
                band_h[pl.ds(h * tc, tc), :] = jnp.concatenate([own[half:], own[half:]], axis=0)
        for k in range(HOPS):
            mk = stack(mwr, (l * HOPS + k) * ch)
            mixall[l, :, pl.ds(k * tc, tc)] = jnp.where(same, mk, 0.0).astype(BF)
            if l == 0:
                at = (rt == lt + steps // 2) if k in (1, 2) else (same & late)
                mix_h[:, pl.ds(k * tc, tc)] = jnp.where(at, mk, 0.0).astype(BF)

    r64 = lax.broadcasted_iota(jnp.int32, (2 * ch, 2 * tc), 0)
    l64 = lax.broadcasted_iota(jnp.int32, (2 * ch, 2 * tc), 1)
    spread2 = jnp.where(rest_of(l64, ch) + quot(l64, tc) * ch == r64, 1.0, 0.0)
    cbias = lax.dot_general(cb[...], spread2, (((1,), (0,)), ((), ())), precision=lax.Precision.HIGHEST, preferred_element_type=F32)
    mbias = lax.dot_general(mb[...], spread, (((1,), (0,)), ((), ())), precision=lax.Precision.HIGHEST, preferred_element_type=F32)

    for load in loads[4:]:
        load.wait()
    def on(r, k, c):
        return (tcol[r, k] == c).astype(jnp.int32).astype(F32)

    def placed(blocks, r, c):
        y = blocks[0] * on(r, 0, c)
        for k in range(1, tslots):
            y = y + blocks[k] * on(r, k, c)
        return y.astype(BF)

    def flipped(r):
        return [tv[r * tslots + k].astype(F32).T for k in range(tslots)]

    for r in range(rblocks):
        flips = flipped(r)
        for c in range(hblocks):
            wht[pl.ds(c * tile, tile), pl.ds(r * tile, tile)] = placed(flips, r, lblocks + c)

    def build_rest():
        for r in range(rblocks):
            tiles = [tv[r * tslots + k].astype(F32) for k in range(tslots)]
            flips = flipped(r)
            for c in range(lblocks):
                wl[pl.ds(r * tile, tile), pl.ds(c * tile, tile)] = placed(tiles, r, c)
                wlt[pl.ds(c * tile, tile), pl.ds(r * tile, tile)] = placed(flips, r, c)
            for c in range(hblocks):
                wh[pl.ds(r * tile, tile), pl.ds(c * tile, tile)] = placed(tiles, r, lblocks + c)

    key = jnp.where(smask[...] != 0, sidx[...] + 1, 0)
    es = lax.broadcasted_iota(jnp.int32, (slots, halo), 0)
    ej = lax.broadcasted_iota(jnp.int32, (slots, halo), 1)
    pick = jnp.where(rest_of(ej, slots) == es, 1.0, 0.0).astype(BF)
    hi = dot((key >> 5).astype(F32).astype(BF), pick)
    lo = dot((key & 31).astype(F32).astype(BF), pick)
    pr = lax.broadcasted_iota(jnp.int32, (n_graph, halo), 0)
    pj = quot(lax.broadcasted_iota(jnp.int32, (n_graph, halo), 1), slots)
    keys = jnp.sum(jnp.where(pr == pj, hi * 32.0 + lo, 0.0), axis=0, keepdims=True)
    ids = lax.broadcasted_iota(jnp.int32, (sensors, halo), 0).astype(F32) + 1.0
    onehot = jnp.where(ids == keys, 1.0, 0.0)
    gm[...] = onehot.astype(BF)
    gmt[...] = onehot.T.astype(BF)

    def graph_copy(src, dst, ssem, rsem, p):
        return pltpu.make_async_remote_copy(
            src_ref=src, dst_ref=dst, send_sem=ssem, recv_sem=rsem,
            device_id={"graph": p}, device_id_type=MESH,
        )

    def tm_copy(src, dst, ssem, rsem, p):
        return pltpu.make_async_remote_copy(
            src_ref=src, dst_ref=dst, send_sem=ssem, recv_sem=rsem,
            device_id={"tm": p}, device_id_type=MESH,
        )

    lane_low = lax.broadcasted_iota(jnp.int32, (halo, tc), 1) < half

    def ship(blocks, out_buf, in_buf, ssem, rsem, r):
        for i, block in enumerate(blocks):
            out_buf[r, :, i] = block.astype(BF).reshape(n_graph, slots, tc).astype(wire)

        def go(off):
            p = partner(off)
            graph_copy(out_buf.at[r, p], in_buf.at[r, me], ssem.at[r, p], rsem.at[r], p).start()

        peers(n_graph, go)
        in_buf[r, me] = out_buf[r, me]

    def collect(in_buf, ssem, rsem, r, count):
        arrived = in_buf.at[r, pl.ds(0, n_graph - 1)]
        graph_copy(arrived, arrived, ssem.at[r, 0], rsem.at[r], partner(1)).wait_recv()
        return [in_buf[r, :, i].reshape(halo, tc).astype(BF) for i in range(count)]

    def launch(r, pull_in, push_in):
        ship((dot(gmt[...], pull_in), dot(wht[...], push_in)), send, recv, r_ssem, r_rsem, r)

    def ship_h(r, sp, sb):
        ship((jnp.where(lane_low, sp, sb),), send_h, recv_h, h_ssem, h_rsem, r)

    def local(pull_in, push_in):
        return dot(wl[...], pull_in), dot(wlt[...], push_in)

    def land(r):
        return collect(recv, r_ssem, r_rsem, r, 2)

    def land_h(r):
        return collect(recv_h, h_ssem, h_rsem, r, 1)[0]

    def beside(rp, rb, both):
        return jnp.concatenate([rp, both], axis=1), jnp.concatenate([rb, both], axis=1)

    def relay(r, rp, rb, sp, sb):
        ship((sp + dot(gwh[...], rp), sb + dot(whg[...], rb)), send, recv, r_ssem, r_rsem, r)

    def joined(a, b):
        return dot(whgm[...], jnp.concatenate([a, b], axis=0))

    def whole(pulled, pushed, rp, rb):
        return pulled + dot(wh[...], rp), pushed + dot(gm[...], rb)

    lane_half = lax.broadcasted_iota(jnp.int32, (half_s, tc), 1) < half

    def pack(x):
        return jnp.where(lane_half, pltpu.roll(x[:half_s], half, 1), x[half_s:]).astype(BF)

    def unpack(p):
        x = p.astype(F32)
        return jnp.concatenate([pltpu.roll(x, half, 1), x], axis=0)

    lane_g = quot(lax.broadcasted_iota(jnp.int32, (ch, tc), 1), ch)

    def fold(x):
        y = x[0:ch]
        for t in range(1, steps):
            y = y + x[t * ch:(t + 1) * ch]
        sh = ch
        while sh < tc:
            y = y + pltpu.roll(y, sh, 1)
            sh *= 2
        return y

    def lanes_of(xs):
        y = jnp.zeros((ch, tc), F32)
        for g, x in enumerate(xs):
            y = jnp.where(lane_g == g, x, y)
        return y

    def gather_start(buf, ssem, rsem, count, here, copy):
        def go(off):
            p = lax.rem(here + off, count)
            copy(buf.at[here], buf.at[here], ssem.at[p], rsem.at[here], p).start()

        peers(count, go)

    def gather_sum(buf, ssem, rsem, count, here, copy):
        def take(off):
            p = lax.rem(here + off, count)
            copy(buf.at[p], buf.at[p], ssem.at[p], rsem.at[p], p).wait_recv()

        peers(count, take)
        total = buf[0]
        for p in range(1, count):
            total = total + buf[p]
        return total

    def hop_grad(fr, l, k):
        return dot(fr, mixall[l, :, pl.ds(k * tc, tc)])

    def mix_fold(l, fr, ks):
        folds = []
        for k in ks:
            hop = hops[l, :, pl.ds(k * tc, tc)]
            folds.append(fold(jnp.where(same, dot(cot[...], hop) if l == 1 else dot_tn(fr, hop), 0.0)))
        return folds

    def conv_fold(l, gp):
        d = l + 1
        if l == 0:
            prod = (dot(series[...], gp), dot(prev0[...], gp))
        else:
            prod = [dot_tn(ext[l, :, pl.ds(i * tc, tc)], gp) for i in range(2)]
        pieces = []
        for tap in range(2):
            for h in range(2):
                own = prod[0][:, h * tc:(h + 1) * tc]
                if tap == 0:
                    x = jnp.where(same, own, 0.0)
                else:
                    x = jnp.where(after(d), own, 0.0) + jnp.where(after_prev(d), prod[1][:, h * tc:(h + 1) * tc], 0.0)
                pieces.append(fold(x))
        return lanes_of(pieces)

    def pre_grad(l, gg):
        f = filt[l]
        g = gate[l]
        return jnp.concatenate([gg * g * (1.0 - f * f), gg * f * g * (1.0 - g)], axis=1).astype(BF)

    def lag_pack(i, l, gp):
        pack_s[i] = pack(dot(gp, band[l, :, pl.ds(tc, tc)]))

    def lag_start(i):
        @pl.when(down)
        def _():
            shift_copy(2 + i, pack_s.at[i], pack_r.at[i], -1).start()

    lanes_late = lax.broadcasted_iota(jnp.int32, (sensors, tc), 1) >= half

    def lag_take(i):
        @pl.when(up)
        def _():
            shift_copy(2 + i, pack_s.at[i], pack_r.at[i], -1).wait_recv()

        @pl.when(jnp.logical_not(up))
        def _():
            pack_r[i] = jnp.zeros((half_s, tc), BF)

        return jnp.where(lanes_late, unpack(pack_r[i]), 0.0)

    flow[...] = cot[...].astype(F32).T
    fr1 = flow[...].astype(BF)
    h4, h2 = hop_grad(fr1, 1, 4).astype(BF), hop_grad(fr1, 1, 2).astype(BF)
    launch(0, h4, h2)

    def mid_back(fr, l, pull_in, push_in):
        pulled, pushed = local(pull_in, push_in)
        pulled = pulled + hop_grad(fr, l, 3)
        pushed = pushed + hop_grad(fr, l, 1)
        sp = dot(gwl[...], pull_in) + hop_grad(dot(gmt[...], fr).astype(BF), l, 3)
        return pulled, pushed, sp, dot(wht[...], pushed.astype(BF))

    def mid(pull_in, push_in):
        pulled, pushed = local(pull_in, push_in)
        return pulled, pushed, dot(gwl[...], pull_in), dot(wht[...], pushed.astype(BF))

    ext[0, :, pl.ds(0, tc)] = series[...].astype(F32).T.astype(BF)
    pre_own = dot_nt(ext[0, :, pl.ds(0, tc)], band[0, :, pl.ds(0, tc)]) + cbias[0:1]

    def halo_take(i, lo, n):
        @pl.when(down)
        def _():
            firsts[i].wait_recv()

        @pl.when(jnp.logical_not(down))
        def _():
            prev0[pl.ds(lo, n), :] = jnp.zeros((n, sensors), BF)

    halo_take(0, tc - ch, ch)
    newest = prev0[pl.ds(tc - ch, ch), :].astype(F32).T.astype(BF)
    pre = pre_own + dot_nt(newest, band[0, :, pl.ds(tc, tc)][:, tc - ch:])
    f = jnp.tanh(pre[:, :tc])
    g = sigmoid(pre[:, tc:])
    gated = (f * g).astype(BF)
    launch(6, gated, gated)
    filt[0] = f
    gate[0] = g

    halo_take(1, tc - 3 * ch, 2 * ch)
    ext[0, :, pl.ds(tc, tc)] = prev0[...].astype(F32).T.astype(BF)
    pre = dot_nt(ext[0, :, pl.ds(tc, tc)], band_h[...]) + cbias[0:1]
    gated_h = (jnp.tanh(pre[:, :tc]) * sigmoid(pre[:, tc:])).astype(BF)
    ship_h(0, dot(gmt[...], gated_h), dot(wht[...], gated_h))
    both = jnp.concatenate([gated, gated_h], axis=1)

    def keep(k, x):
        hops[0, :, pl.ds(k * tc, tc)] = x[:, :tc]
        hops_h[:, pl.ds(k * tc, tc)] = x[:, tc:]

    keep(0, both)
    build_rest()
    gwl[...] = dot(gmt[...], wl[...]).astype(BF)
    gwh[...] = dot(gmt[...], wh[...]).astype(BF)
    whg[...] = dot(wht[...], gm[...]).astype(BF)
    ab = mid_back(fr1, 1, h4, h2)
    af = mid(both, both)

    rp, rb = land(0)
    relay(1, rp, rb, *ab[2:])
    bi, fi = whole(*ab[:2], rp, rb)
    bb = local(bi.astype(BF), fi.astype(BF))
    gg0 = hop_grad(fr1, 1, 0)

    rp, rb = land(6)
    relay(7, rp, rb, af[2][:, :tc], af[3][:, :tc])
    both = land_h(0)
    ship_h(1, af[2][:, tc:] + dot(gwh[...], both), af[3][:, tc:] + dot(whg[...], both))
    rp, rb = beside(rp, rb, both)
    fo, bo = whole(*af[:2], rp, rb)
    fo, bo = fo.astype(BF), bo.astype(BF)
    keep(1, fo)
    keep(3, bo)
    bf = local(fo, bo)

    def mix_three(mat, hop):
        m = dot_nt(hop(0, 2), mat(0, 2))
        return m + dot_nt(hop(3, 1), mat(3, 1))

    def mat_of(l):
        return lambda k, n: mixall[l, :, pl.ds(k * tc, n * tc)]

    def hop_of(l):
        return lambda k, n: hops[l, :, pl.ds(k * tc, n * tc)]

    part = mix_three(mat_of(0), hop_of(0))
    part_h = mix_three(
        lambda k, n: mix_h[:, pl.ds(k * tc, n * tc)], lambda k, n: hops_h[:, pl.ds(k * tc, n * tc)]
    )

    gg1 = gg0 + bb[0] + bb[1]
    gg1 = gg1 + joined(*land(1))

    def two_late(a, b):
        e = dot_nt(a[:, :tc], mixall[0, :, pl.ds(2 * tc, tc)]), dot_nt(b[:, :tc], mixall[0, :, pl.ds(4 * tc, tc)])
        h = dot_nt(a[:, tc:], mix_h[:, pl.ds(2 * tc, tc)]), dot_nt(b[:, tc:], mix_h[:, pl.ds(4 * tc, tc)])
        return [jnp.concatenate([x, y], axis=1) for x, y in zip(e, h)]

    known = two_late(bf[0].astype(BF), bf[1].astype(BF))
    mbias2 = jnp.concatenate([mbias[0:1], mbias[0:1]], axis=1)
    hid = ext[0].astype(F32) + mbias2 + jnp.concatenate([part, part_h], axis=1) + known[0] + known[1]

    rp, rb = beside(*land(7), land_h(1))
    hid = hid + joined(*[x.astype(BF) for x in two_late(rp, rb)])
    lane2 = lax.broadcasted_iota(jnp.int32, (sensors, 2 * tc), 1)
    ext[1] = jnp.where((lane2 < tc) | ((lane2 >= tc + half) & down), hid, 0.0).astype(BF)

    pre = dot_nt(ext[1], band[1]) + cbias[1:2]
    f = jnp.tanh(pre[:, :tc])
    g = sigmoid(pre[:, tc:])
    filt[1] = f
    gate[1] = g
    gp1 = pre_grad(1, gg1)
    lag_pack(0, 1, gp1)
    lag_start(0)
    gated = (f * g).astype(BF)
    hops[1, :, pl.ds(0, tc)] = gated
    launch(2, gated, gated)
    f2, b2 = whole(bf[0][:, :tc], bf[1][:, :tc], rp[:, :tc], rb[:, :tc])
    hops[0, :, pl.ds(2 * tc, tc)] = f2.astype(BF)
    hops[0, :, pl.ds(4 * tc, tc)] = b2.astype(BF)
    cf = mid(gated, gated)
    new = flow[...] + dot(gp1, band[1, :, pl.ds(0, tc)])
    conv1 = conv_fold(1, gp1)

    flow[...] = new + lag_take(0)
    fr0 = flow[...].astype(BF)
    h4, h2 = hop_grad(fr0, 0, 4).astype(BF), hop_grad(fr0, 0, 2).astype(BF)
    launch(4, h4, h2)
    rp, rb = land(2)
    relay(3, rp, rb, *cf[2:])
    fo, bo = whole(*cf[:2], rp, rb)
    fo, bo = fo.astype(BF), bo.astype(BF)
    hops[1, :, pl.ds(tc, tc)] = fo
    hops[1, :, pl.ds(3 * tc, tc)] = bo
    mix0 = mix_fold(0, fr0, range(HOPS))
    mix1 = mix_fold(1, fr1, (0, 1, 3))
    early = jnp.concatenate([conv1, lanes_of(mix0[:4]), lanes_of([mix0[4]] + mix1)], axis=0)
    for p in range(n_graph):
        e_part[p] = early[p * er:(p + 1) * er]

    def scatter(off):
        p = partner(off)
        graph_copy(e_part.at[p], e_buf.at[me], e_ssem.at[p], e_rsem.at[me], p).start()

    peers(n_graph, scatter)
    e_buf[me] = e_part[me]
    cb_ = mid_back(fr0, 0, h4, h2)
    df = local(fo, bo)
    gg0 = hop_grad(fr0, 0, 0)
    part = mix_three(mat_of(1), hop_of(1))

    rp, rb = land(4)
    relay(5, rp, rb, *cb_[2:])
    bi, fi = whole(*cb_[:2], rp, rb)
    db = local(bi.astype(BF), fi.astype(BF))
    et_buf[z] = gather_sum(e_buf, e_ssem, e_rsem, n_graph, me, graph_copy)
    gather_start(et_buf, et_ssem, et_rsem, n_tm, z, tm_copy)

    f2, b2 = whole(*df, *land(3))
    f2, b2 = f2.astype(BF), b2.astype(BF)
    hops[1, :, pl.ds(2 * tc, tc)] = f2
    hops[1, :, pl.ds(4 * tc, tc)] = b2
    a2, a4 = mix_fold(1, fr1, (2, 4))
    hc = ch // 2
    last = jnp.zeros((hc, tc), F32)
    for g, x in enumerate((a2[:hc], a4[:hc], a2[hc:], a4[hc:])):
        last = jnp.where(lane_g[:hc] == g, x, last)
    m_buf[me] = last
    gather_start(m_buf, m_ssem, m_rsem, n_graph, me, graph_copy)
    mixed = part + dot_nt(f2, mixall[1, :, pl.ds(2 * tc, tc)]) + dot_nt(b2, mixall[1, :, pl.ds(4 * tc, tc)])
    out[...] = (ext[1, :, pl.ds(0, tc)].astype(F32) + (mixed + mbias[1:2])).T.astype(BF)

    gg0 = gg0 + db[0] + db[1]
    gp0 = pre_grad(0, gg0 + joined(*land(5)))
    lag_pack(1, 0, gp0)
    lag_start(1)
    conv0 = conv_fold(0, gp0)
    if direct:
        swap = graph_copy(pair_s, pair_r, pair_sem.at[0], pair_sem.at[1], mate)
        low = core == 0
        pair_s[...] = jnp.where(low, conv0[hc:], conv0[:hc])
        swap.start()
    else:
        l_buf[me] = conv0
        gather_start(l_buf, l_ssem, l_rsem, n_graph, me, graph_copy)

    here = (z * n_graph + me) // 2

    def final_copy(goff, toff):
        p = partner(goff) if goff else me
        return pltpu.make_async_remote_copy(
            src_ref=fin.at[here], dst_ref=fin.at[here],
            send_sem=fin_ssem.at[toff * n_graph + goff], recv_sem=fin_rsem.at[0],
            device_id={"graph": p, "tm": lax.rem(z + toff, n_tm)}, device_id_type=MESH,
        )

    others = [(g, t) for t in range(n_tm) for g in range(0, n_graph, 2) if (g, t) != (0, 0)] if direct else []
    if direct:
        swap.wait_recv()
        fin[here] = (jnp.where(low, conv0[:hc], conv0[hc:]) + pair_r[...]).astype(BF)
        for g, t in reversed(others):
            final_copy(g, t).start()
    mt_buf[z] = gather_sum(m_buf, m_ssem, m_rsem, n_graph, me, graph_copy)
    gather_start(mt_buf, mt_ssem, mt_rsem, n_tm, z, tm_copy)
    eg_buf[me] = gather_sum(et_buf, et_ssem, et_rsem, n_tm, z, tm_copy)
    gather_start(eg_buf, eg_ssem, eg_rsem, n_graph, me, graph_copy)
    if not direct:
        lt_buf[z] = gather_sum(l_buf, l_ssem, l_rsem, n_graph, me, graph_copy)
        gather_start(lt_buf, lt_ssem, lt_rsem, n_tm, z, tm_copy)
    new = flow[...] + dot(gp0, band[0, :, pl.ds(0, tc)])
    gser[...] = (new + lag_take(1)).T.astype(BF)

    def lane_group(x, g):
        return (pltpu.roll(x, tc - g * ch, 1) if g else x)[:, :ch]

    def put_conv(l, x):
        gconv[l, 0] = x[:, :2 * ch]
        gconv[l, 1] = pltpu.roll(x, tc - 2 * ch, 1)[:, :2 * ch]

    m = gather_sum(mt_buf, mt_ssem, mt_rsem, n_tm, z, tm_copy) * scale
    for i, k in enumerate((2, 4)):
        gmix[1, k, pl.ds(0, hc)] = lane_group(m, i)
        gmix[1, k, pl.ds(hc, hc)] = lane_group(m, i + 2)

    def take_group(off):
        p = partner(off)
        graph_copy(eg_buf.at[p], eg_buf.at[p], eg_ssem.at[p], eg_rsem.at[p], p).wait_recv()

    peers(n_graph, take_group)
    e = jnp.concatenate([eg_buf[p] for p in range(n_graph)], axis=0) * scale
    put_conv(1, e[:ch])
    for k in range(4):
        gmix[0, k] = lane_group(e[ch:2 * ch], k)
    gmix[0, 4] = lane_group(e[2 * ch:], 0)
    for i, k in enumerate((0, 1, 3)):
        gmix[1, k] = lane_group(e[2 * ch:], i + 1)
    if direct:
        count = fin.shape[0]
        arrived = fin.at[pl.ds(0, count - 1)]
        pltpu.make_async_remote_copy(
            src_ref=arrived, dst_ref=arrived, send_sem=fin_ssem.at[2], recv_sem=fin_rsem.at[0],
            device_id={"graph": mate}, device_id_type=MESH,
        ).wait_recv()
        total = fin[0].astype(F32)
        for p in range(1, count):
            total = total + fin[p].astype(F32)
        back_s[...] = total
        back = graph_copy(back_s, back_r, pair_sem.at[2], pair_sem.at[3], mate)
        back.start()
        back.wait_recv()
        theirs = back_r[...]
        halves = [jnp.where(low, total, theirs), jnp.where(low, theirs, total)]
        put_conv(0, jnp.concatenate(halves, axis=0) * scale)
        back.wait_send()
        swap.wait_send()
        for g, t in others:
            final_copy(g, t).wait_send()
    else:
        put_conv(0, gather_sum(lt_buf, lt_ssem, lt_rsem, n_tm, z, tm_copy) * scale)

    def sent_graph(off):
        p = partner(off)
        for r in range(send.shape[0]):
            graph_copy(send.at[r, p], recv.at[r, me], r_ssem.at[r, p], r_rsem.at[r], p).wait_send()
        for r in range(send_h.shape[0]):
            graph_copy(send_h.at[r, p], recv_h.at[r, me], h_ssem.at[r, p], h_rsem.at[r], p).wait_send()
        graph_copy(e_part.at[p], e_buf.at[me], e_ssem.at[p], e_rsem.at[me], p).wait_send()
        graph_copy(eg_buf.at[me], eg_buf.at[me], eg_ssem.at[p], eg_rsem.at[me], p).wait_send()
        graph_copy(m_buf.at[me], m_buf.at[me], m_ssem.at[p], m_rsem.at[me], p).wait_send()
        if not direct:
            graph_copy(l_buf.at[me], l_buf.at[me], l_ssem.at[p], l_rsem.at[me], p).wait_send()

    peers(n_graph, sent_graph)

    def sent_tm(off):
        p = lax.rem(z + off, n_tm)
        tm_copy(et_buf.at[z], et_buf.at[z], et_ssem.at[p], et_rsem.at[z], p).wait_send()
        tm_copy(mt_buf.at[z], mt_buf.at[z], mt_ssem.at[p], mt_rsem.at[z], p).wait_send()
        if not direct:
            tm_copy(lt_buf.at[z], lt_buf.at[z], lt_ssem.at[p], lt_rsem.at[z], p).wait_send()

    peers(n_tm, sent_tm)

    @pl.when(up)
    def _():
        for first in firsts:
            first.wait_send()

    @pl.when(down)
    def _():
        shift_copy(2, pack_s.at[0], pack_r.at[0], -1).wait_send()
        shift_copy(3, pack_s.at[1], pack_r.at[1], -1).wait_send()


def store_kernel(a, b, c, d, ao, bo, co, do, sem):
    copies = [
        pltpu.make_async_copy(src, dst, sem.at[i])
        for i, (src, dst) in enumerate(((a, ao), (b, bo), (c, co), (d, do)))
    ]
    for copy in copies:
        copy.start()
    for copy in copies:
        copy.wait()


def per_device(series, cw, cb, mw, mb, tv, tcol, sidx, smask, cot):
    n_graph = lax.axis_size("graph")
    n_tm = lax.axis_size("tm")
    steps, ch, sensors = series.shape
    tc = steps * ch
    slots = sidx.shape[2]
    halo = n_graph * slots
    wire = BF if slots % 16 == 0 else F32
    narrow, wide = 8, 2
    scale = 1.0 / math.sqrt(float(steps * n_tm * sensors * n_graph))
    vm = pl.BlockSpec(memory_space=pltpu.VMEM)
    hb = pl.BlockSpec(memory_space=pltpu.HBM)
    cwt_shape = (*cw.shape[:2], cw.shape[3], cw.shape[2])
    ins = (
        series.reshape(tc, sensors),
        jnp.swapaxes(cw, 2, 3).reshape(-1, cw.shape[2]),
        cb,
        mw.reshape(-1, ch),
        mb,
        tv.reshape(-1, *tv.shape[2:]),
        tcol,
        sidx[0],
        smask[0],
        cot.reshape(tc, sensors),
    )
    er = 3 * ch // n_graph
    direct = n_graph % 2 == 0 and n_graph * n_tm <= 32 and ch % 32 == 0
    n_all = n_graph * n_tm if direct else 1
    ins = tuple(pltpu.with_memory_space_constraint(x, pltpu.HBM) for x in ins)
    dma = pltpu.SemaphoreType.DMA
    out, gser, gconv, gmix = pl.pallas_call(
        functools.partial(kernel, n_graph, n_tm, steps, scale),
        out_shape=(
            pltpu.VMEM((tc, sensors), BF),
            pltpu.VMEM((tc, sensors), BF),
            pltpu.VMEM(cwt_shape, F32),
            pltpu.VMEM(mw.shape, F32),
        ),
        in_specs=[hb] * 10,
        out_specs=(vm,) * 4,
        scratch_shapes=[
            pltpu.VMEM((sensors, sensors), BF),
            pltpu.VMEM((sensors, sensors), BF),
            pltpu.VMEM((sensors, 2 * halo), BF),
            pltpu.VMEM((halo, sensors), BF),
            pltpu.VMEM((halo, sensors), BF),
            pltpu.VMEM((halo, sensors), BF),
            pltpu.VMEM((halo, halo), BF),
            pltpu.VMEM((halo, halo), BF),
            pltpu.VMEM((GATED_LAYERS, 2 * tc, 2 * tc), BF),
            pltpu.VMEM((2 * tc, tc), BF),
            pltpu.VMEM((GATED_LAYERS, tc, HOPS * tc), BF),
            pltpu.VMEM((tc, HOPS * tc), BF),
            pltpu.VMEM((GATED_LAYERS, sensors, 2 * tc), BF),
            pltpu.VMEM((GATED_LAYERS, sensors, HOPS * tc), BF),
            pltpu.VMEM((sensors, HOPS * tc), BF),
            pltpu.VMEM((GATED_LAYERS, sensors, tc), F32),
            pltpu.VMEM((GATED_LAYERS, sensors, tc), F32),
            pltpu.VMEM((sensors, tc), F32),
            pltpu.VMEM((tc, sensors), BF),
            pltpu.VMEM((2, sensors // 2, tc), BF),
            pltpu.VMEM((2, sensors // 2, tc), BF),
            pltpu.VMEM((narrow, n_graph, 2, slots, tc), wire),
            pltpu.VMEM((narrow, n_graph, 2, slots, tc), wire),
            pltpu.VMEM((wide, n_graph, 1, slots, tc), wire),
            pltpu.VMEM((wide, n_graph, 1, slots, tc), wire),
            pltpu.VMEM((n_graph, er, tc), F32),
            pltpu.VMEM((n_tm, er, tc), F32),
            pltpu.VMEM((n_graph, ch, tc), F32),
            pltpu.VMEM((n_tm, ch, tc), F32),
            pltpu.VMEM((n_graph, er, tc), F32),
            pltpu.VMEM((n_graph, er, tc), F32),
            pltpu.VMEM((n_graph, ch // 2, tc), F32),
            pltpu.VMEM((n_tm, ch // 2, tc), F32),
            *[pltpu.VMEM((ch // 2, tc), F32)] * 4,
            pltpu.VMEM((max(n_all // 2, 1), ch // 2, tc), BF),
            *[(pltpu.SMEM if x.shape == tcol.shape else pltpu.VMEM)(x.shape, x.dtype) for x in ins],
            dma((10,)),
            dma((narrow, n_graph)), dma((narrow,)),
            dma((wide, n_graph)), dma((wide,)),
            dma((4,)), dma((4,)),
            dma((n_graph,)), dma((n_graph,)),
            dma((n_tm,)), dma((n_tm,)),
            dma((n_graph,)), dma((n_graph,)),
            dma((n_tm,)), dma((n_tm,)),
            dma((n_graph,)), dma((n_graph,)),
            dma((n_graph,)), dma((n_graph,)),
            dma((n_tm,)), dma((n_tm,)),
            dma((4,)), dma((n_all,)), dma((1,)),
        ],
        compiler_params=pltpu.CompilerParams(
            collective_id=0, has_side_effects=True, vmem_limit_bytes=48 * 1024 * 1024
        ),
    )(*ins)
    results = tuple(pltpu.with_memory_space_constraint(x, pltpu.VMEM) for x in (out, gser, gconv, gmix))
    out, gser, gconv, gmix = pl.pallas_call(
        store_kernel,
        out_shape=tuple(pltpu.HBM(x.shape, x.dtype) for x in results),
        in_specs=[vm] * 4,
        out_specs=(hb,) * 4,
        scratch_shapes=[dma((4,))],
        compiler_params=pltpu.CompilerParams(vmem_limit_bytes=4 * 1024 * 1024),
    )(*results)
    gconv = jnp.swapaxes(gconv, 2, 3)
    return out.reshape(series.shape), gser.reshape(series.shape), gconv, gmix


def solution(mesh):
    return jax.shard_map(
        per_device,
        mesh=mesh,
        in_specs=(
            P("tm", None, "graph"),
            P(),
            P(),
            P(),
            P(),
            P("graph", None, None, None),
            P("graph", None),
            P("graph", None, None),
            P("graph", None, None),
            P("tm", None, "graph"),
        ),
        out_specs=(P("tm", None, "graph"), P("tm", None, "graph"), P(), P()),
        check_vma=False,
    )
```

```python
import functools
import math

import jax
import jax.numpy as jnp
from jax import lax
from jax.experimental import pallas as pl
from jax.experimental.pallas import tpu as pltpu
from jax.sharding import PartitionSpec as P

GATED_LAYERS = 2
HOPS = 5
BF = jnp.bfloat16
F32 = jnp.float32
MESH = pl.DeviceIdType.MESH


def dot(a, b):
    return lax.dot_general(a, b, (((1,), (0,)), ((), ())), preferred_element_type=F32)


def dot_nt(a, b):
    return lax.dot_general(a, b, (((1,), (1,)), ((), ())), preferred_element_type=F32)


def dot_tn(a, b):
    return lax.dot_general(a, b, (((0,), (0,)), ((), ())), preferred_element_type=F32)


def sigmoid(x):
    return 0.5 + 0.5 * jnp.tanh(0.5 * x)


def quot(x, n):
    return x >> (n.bit_length() - 1) if n & (n - 1) == 0 else x // n


def rest_of(x, n):
    return x & (n - 1) if n & (n - 1) == 0 else lax.rem(x, n)


def peers(count, body):
    if count <= 8:
        for off in range(count - 1, 0, -1):
            body(off)
    elif count > 1:
        lax.fori_loop(1, count, lambda off, c: (body(off), c)[1], 0)


def kernel(
    n_graph, n_tm, steps, scale,
    series_h, cw_h, cb_h, mw_h, mb_h, tv_h, tcol_h, sidx_h, smask_h, cot_h,
    out, gser, gconv, gmix,
    wl, wlt, whgm, wht, gmt, gwl, gwh, whg, band, band_h, mixall, mix_h, ext, hops, hops_h, filt, gate, flow,
    prev0, pack_s, pack_r, send, recv, send_h, recv_h, e_buf, et_buf, l_buf, lt_buf,
    e_part, eg_buf, m_buf, mt_buf, pair_s, pair_r, back_s, back_r, fin,
    series, cw, cb, mw, mb, tv, tcol, sidx, smask, cot, in_sem,
    r_ssem, r_rsem, h_ssem, h_rsem, t_ssem, t_rsem, e_ssem, e_rsem, et_ssem, et_rsem,
    l_ssem, l_rsem, lt_ssem, lt_rsem, eg_ssem, eg_rsem, m_ssem, m_rsem, mt_ssem, mt_rsem,
    pair_sem, fin_ssem, fin_rsem,
):
    me = lax.axis_index("graph")
    z = lax.axis_index("tm")
    tc, sensors = series.shape
    ch = tc // steps
    half = tc // 2
    half_s = sensors // 2
    slots = sidx.shape[1]
    halo = n_graph * slots
    tile = tv.shape[-1]
    rblocks, tslots = tcol.shape
    lblocks = sensors // tile
    hblocks = halo // tile
    wire = send.dtype
    wh = whgm.at[:, pl.ds(0, halo)]
    gm = whgm.at[:, pl.ds(halo, halo)]
    direct = fin.shape[0] > 1
    core = lax.rem(me, 2)
    mate = me + 1 - 2 * core

    def partner(off):
        if n_graph & (n_graph - 1) or n_graph > 8:
            return lax.rem(me + off, n_graph)
        p = 0
        bit = 1
        while bit < n_graph:
            p = p + lax.rem(me // bit + off // bit, 2) * bit
            bit *= 2
        return p

    er = e_part.shape[1]

    loads = [
        pltpu.make_async_copy(src, dst, in_sem.at[i])
        for i, (src, dst) in enumerate(
            ((cw_h, cw), (mw_h, mw), (cb_h, cb), (mb_h, mb), (tv_h, tv), (series_h, series),
             (sidx_h, sidx), (smask_h, smask), (cot_h, cot), (tcol_h, tcol))
        )
    ]
    for load in loads:
        load.start()
    barrier = pltpu.get_barrier_semaphore()

    def greet_graph(off):
        pl.semaphore_signal(barrier, inc=1, device_id={"graph": partner(off)}, device_id_type=MESH)

    def greet_tm(off):
        pl.semaphore_signal(barrier, inc=1, device_id={"tm": lax.rem(z + off, n_tm)}, device_id_type=MESH)

    peers(n_tm, greet_tm)
    peers(n_graph, greet_graph)

    def shift_copy(slot, src, dst, by):
        return pltpu.make_async_remote_copy(
            src_ref=src, dst_ref=dst, send_sem=t_ssem.at[slot], recv_sem=t_rsem.at[slot],
            device_id={"tm": lax.rem(z + by + n_tm, n_tm)}, device_id_type=MESH,
        )

    up = z < n_tm - 1
    down = z > 0

    firsts = [
        shift_copy(0, series_h.at[pl.ds(tc - ch, ch)], prev0.at[pl.ds(tc - ch, ch)], 1),
        shift_copy(1, series_h.at[pl.ds(tc - 3 * ch, 2 * ch)], prev0.at[pl.ds(tc - 3 * ch, 2 * ch)], 1),
    ]
    pl.semaphore_wait(barrier, n_graph - 1 + n_tm - 1)

    @pl.when(up)
    def _():
        for first in firsts:
            first.start()

    prev0[pl.ds(0, tc - 3 * ch), :] = jnp.zeros((tc - 3 * ch, sensors), BF)

    row32 = lax.broadcasted_iota(jnp.int32, (ch, tc), 0)
    lane32 = lax.broadcasted_iota(jnp.int32, (ch, tc), 1)
    spread = jnp.where(rest_of(lane32, ch) == row32, 1.0, 0.0)
    spread_b = spread.astype(BF)
    rt = lax.broadcasted_iota(jnp.int32, (tc, tc), 0)
    lt = lax.broadcasted_iota(jnp.int32, (tc, tc), 1)
    rt, lt = quot(rt, ch), quot(lt, ch)
    same = rt == lt
    late = rt >= steps // 2

    def before(d):
        return lt == rt - d

    def before_prev(d):
        return lt == rt - d + steps

    for load in loads[:4]:
        load.wait()
    taps = 2 * GATED_LAYERS
    rs = lax.broadcasted_iota(jnp.int32, (taps * ch, taps * tc), 0)
    ls = lax.broadcasted_iota(jnp.int32, (taps * ch, taps * tc), 1)
    spread_taps = jnp.where(quot(ls, tc) * ch + rest_of(ls, ch) == rs, 1.0, 0.0).astype(BF)
    def after(d):
        return rt == lt - d

    def after_prev(d):
        return rt == lt - d + steps

    cwr = dot_tn(cw[...], spread_taps)
    mwr = dot(mw[...], spread_b)

    def stack(x, base):
        return jnp.concatenate([x[base:base + ch]] * steps, axis=0)

    for l in range(GATED_LAYERS):
        d = l + 1
        for h in range(2):
            w0 = stack(cwr[:, (l * 2) * tc:(l * 2 + 1) * tc], h * ch)
            w1 = stack(cwr[:, (l * 2 + 1) * tc:(l * 2 + 2) * tc], h * ch)
            own = (jnp.where(same, w0, 0.0) + jnp.where(before(d), w1, 0.0)).astype(BF)
            band[l, pl.ds(h * tc, tc), pl.ds(0, tc)] = own
            band[l, pl.ds(h * tc, tc), pl.ds(tc, tc)] = jnp.where(before_prev(d), w1, 0.0).astype(BF)
            if l == 0:
                band_h[pl.ds(h * tc, tc), :] = jnp.concatenate([own[half:], own[half:]], axis=0)
        for k in range(HOPS):
            mk = stack(mwr, (l * HOPS + k) * ch)
            mixall[l, :, pl.ds(k * tc, tc)] = jnp.where(same, mk, 0.0).astype(BF)
            if l == 0:
                at = (rt == lt + steps // 2) if k in (1, 2) else (same & late)
                mix_h[:, pl.ds(k * tc, tc)] = jnp.where(at, mk, 0.0).astype(BF)

    r64 = lax.broadcasted_iota(jnp.int32, (2 * ch, 2 * tc), 0)
    l64 = lax.broadcasted_iota(jnp.int32, (2 * ch, 2 * tc), 1)
    spread2 = jnp.where(rest_of(l64, ch) + quot(l64, tc) * ch == r64, 1.0, 0.0)
    cbias = lax.dot_general(cb[...], spread2, (((1,), (0,)), ((), ())), precision=lax.Precision.HIGHEST, preferred_element_type=F32)
    mbias = lax.dot_general(mb[...], spread, (((1,), (0,)), ((), ())), precision=lax.Precision.HIGHEST, preferred_element_type=F32)

    for load in loads[4:]:
        load.wait()
    def on(r, k, c):
        return (tcol[r, k] == c).astype(jnp.int32).astype(F32)

    def placed(blocks, r, c):
        y = blocks[0] * on(r, 0, c)
        for k in range(1, tslots):
            y = y + blocks[k] * on(r, k, c)
        return y.astype(BF)

    def flipped(r):
        return [tv[r * tslots + k].astype(F32).T for k in range(tslots)]

    for r in range(rblocks):
        flips = flipped(r)
        for c in range(hblocks):
            wht[pl.ds(c * tile, tile), pl.ds(r * tile, tile)] = placed(flips, r, lblocks + c)

    def build_rest():
        for r in range(rblocks):
            tiles = [tv[r * tslots + k].astype(F32) for k in range(tslots)]
            flips = flipped(r)
            for c in range(lblocks):
                wl[pl.ds(r * tile, tile), pl.ds(c * tile, tile)] = placed(tiles, r, c)
                wlt[pl.ds(c * tile, tile), pl.ds(r * tile, tile)] = placed(flips, r, c)
            for c in range(hblocks):
                wh[pl.ds(r * tile, tile), pl.ds(c * tile, tile)] = placed(tiles, r, lblocks + c)

    key = jnp.where(smask[...] != 0, sidx[...] + 1, 0)
    es = lax.broadcasted_iota(jnp.int32, (slots, halo), 0)
    ej = lax.broadcasted_iota(jnp.int32, (slots, halo), 1)
    pick = jnp.where(rest_of(ej, slots) == es, 1.0, 0.0).astype(BF)
    hi = dot((key >> 5).astype(F32).astype(BF), pick)
    lo = dot((key & 31).astype(F32).astype(BF), pick)
    pr = lax.broadcasted_iota(jnp.int32, (n_graph, halo), 0)
    pj = quot(lax.broadcasted_iota(jnp.int32, (n_graph, halo), 1), slots)
    keys = jnp.sum(jnp.where(pr == pj, hi * 32.0 + lo, 0.0), axis=0, keepdims=True)
    ids = lax.broadcasted_iota(jnp.int32, (sensors, halo), 0).astype(F32) + 1.0
    onehot = jnp.where(ids == keys, 1.0, 0.0)
    gm[...] = onehot.astype(BF)
    gmt[...] = onehot.T.astype(BF)

    def graph_copy(src, dst, ssem, rsem, p):
        return pltpu.make_async_remote_copy(
            src_ref=src, dst_ref=dst, send_sem=ssem, recv_sem=rsem,
            device_id={"graph": p}, device_id_type=MESH,
        )

    def tm_copy(src, dst, ssem, rsem, p):
        return pltpu.make_async_remote_copy(
            src_ref=src, dst_ref=dst, send_sem=ssem, recv_sem=rsem,
            device_id={"tm": p}, device_id_type=MESH,
        )

    lane_low = lax.broadcasted_iota(jnp.int32, (halo, tc), 1) < half

    def ship(blocks, out_buf, in_buf, ssem, rsem, r):
        for i, block in enumerate(blocks):
            out_buf[r, :, i] = block.astype(BF).reshape(n_graph, slots, tc).astype(wire)

        def go(off):
            p = partner(off)
            graph_copy(out_buf.at[r, p], in_buf.at[r, me], ssem.at[r, p], rsem.at[r], p).start()

        peers(n_graph, go)
        in_buf[r, me] = out_buf[r, me]

    def collect(in_buf, ssem, rsem, r, count):
        arrived = in_buf.at[r, pl.ds(0, n_graph - 1)]
        graph_copy(arrived, arrived, ssem.at[r, 0], rsem.at[r], partner(1)).wait_recv()
        return [in_buf[r, :, i].reshape(halo, tc).astype(BF) for i in range(count)]

    def launch(r, pull_in, push_in):
        ship((dot(gmt[...], pull_in), dot(wht[...], push_in)), send, recv, r_ssem, r_rsem, r)

    def ship_h(r, sp, sb):
        ship((jnp.where(lane_low, sp, sb),), send_h, recv_h, h_ssem, h_rsem, r)

    def local(pull_in, push_in):
        return dot(wl[...], pull_in), dot(wlt[...], push_in)

    def land(r):
        return collect(recv, r_ssem, r_rsem, r, 2)

    def land_h(r):
        return collect(recv_h, h_ssem, h_rsem, r, 1)[0]

    def beside(rp, rb, both):
        return jnp.concatenate([rp, both], axis=1), jnp.concatenate([rb, both], axis=1)

    def relay(r, rp, rb, sp, sb):
        ship((sp + dot(gwh[...], rp), sb + dot(whg[...], rb)), send, recv, r_ssem, r_rsem, r)

    def joined(a, b):
        return dot(whgm[...], jnp.concatenate([a, b], axis=0))

    def whole(pulled, pushed, rp, rb):
        return pulled + dot(wh[...], rp), pushed + dot(gm[...], rb)

    lane_half = lax.broadcasted_iota(jnp.int32, (half_s, tc), 1) < half

    def pack(x):
        return jnp.where(lane_half, pltpu.roll(x[:half_s], half, 1), x[half_s:]).astype(BF)

    def unpack(p):
        x = p.astype(F32)
        return jnp.concatenate([pltpu.roll(x, half, 1), x], axis=0)

    lane_g = quot(lax.broadcasted_iota(jnp.int32, (ch, tc), 1), ch)

    def fold(x):
        y = x[0:ch]
        for t in range(1, steps):
            y = y + x[t * ch:(t + 1) * ch]
        sh = ch
        while sh < tc:
            y = y + pltpu.roll(y, sh, 1)
            sh *= 2
        return y

    def lanes_of(xs):
        y = jnp.zeros((ch, tc), F32)
        for g, x in enumerate(xs):
            y = jnp.where(lane_g == g, x, y)
        return y

    def gather_start(buf, ssem, rsem, count, here, copy):
        def go(off):
            p = lax.rem(here + off, count)
            copy(buf.at[here], buf.at[here], ssem.at[p], rsem.at[here], p).start()

        peers(count, go)

    def gather_sum(buf, ssem, rsem, count, here, copy):
        def take(off):
            p = lax.rem(here + off, count)
            copy(buf.at[p], buf.at[p], ssem.at[p], rsem.at[p], p).wait_recv()

        peers(count, take)
        total = buf[0]
        for p in range(1, count):
            total = total + buf[p]
        return total

    def hop_grad(fr, l, k):
        return dot(fr, mixall[l, :, pl.ds(k * tc, tc)])

    def mix_fold(l, fr, ks):
        folds = []
        for k in ks:
            hop = hops[l, :, pl.ds(k * tc, tc)]
            folds.append(fold(jnp.where(same, dot(cot[...], hop) if l == 1 else dot_tn(fr, hop), 0.0)))
        return folds

    def conv_fold(l, gp):
        d = l + 1
        if l == 0:
            prod = (dot(series[...], gp), dot(prev0[...], gp))
        else:
            prod = [dot_tn(ext[l, :, pl.ds(i * tc, tc)], gp) for i in range(2)]
        pieces = []
        for tap in range(2):
            for h in range(2):
                own = prod[0][:, h * tc:(h + 1) * tc]
                if tap == 0:
                    x = jnp.where(same, own, 0.0)
                else:
                    x = jnp.where(after(d), own, 0.0) + jnp.where(after_prev(d), prod[1][:, h * tc:(h + 1) * tc], 0.0)
                pieces.append(fold(x))
        return lanes_of(pieces)

    def pre_grad(l, gg):
        f = filt[l]
        g = gate[l]
        return jnp.concatenate([gg * g * (1.0 - f * f), gg * f * g * (1.0 - g)], axis=1).astype(BF)

    def lag_pack(i, l, gp):
        pack_s[i] = pack(dot(gp, band[l, :, pl.ds(tc, tc)]))

    def lag_start(i):
        @pl.when(down)
        def _():
            shift_copy(2 + i, pack_s.at[i], pack_r.at[i], -1).start()

    lanes_late = lax.broadcasted_iota(jnp.int32, (sensors, tc), 1) >= half

    def lag_take(i):
        @pl.when(up)
        def _():
            shift_copy(2 + i, pack_s.at[i], pack_r.at[i], -1).wait_recv()

        @pl.when(jnp.logical_not(up))
        def _():
            pack_r[i] = jnp.zeros((half_s, tc), BF)

        return jnp.where(lanes_late, unpack(pack_r[i]), 0.0)

    flow[...] = cot[...].astype(F32).T
    fr1 = flow[...].astype(BF)
    h4, h2 = hop_grad(fr1, 1, 4).astype(BF), hop_grad(fr1, 1, 2).astype(BF)
    launch(0, h4, h2)

    def mid_back(fr, l, pull_in, push_in):
        pulled, pushed = local(pull_in, push_in)
        pulled = pulled + hop_grad(fr, l, 3)
        pushed = pushed + hop_grad(fr, l, 1)
        sp = dot(gwl[...], pull_in) + hop_grad(dot(gmt[...], fr).astype(BF), l, 3)
        return pulled, pushed, sp, dot(wht[...], pushed.astype(BF))

    def mid(pull_in, push_in):
        pulled, pushed = local(pull_in, push_in)
        return pulled, pushed, dot(gwl[...], pull_in), dot(wht[...], pushed.astype(BF))

    ext[0, :, pl.ds(0, tc)] = series[...].astype(F32).T.astype(BF)
    pre_own = dot_nt(ext[0, :, pl.ds(0, tc)], band[0, :, pl.ds(0, tc)]) + cbias[0:1]

    def halo_take(i, lo, n):
        @pl.when(down)
        def _():
            firsts[i].wait_recv()

        @pl.when(jnp.logical_not(down))
        def _():
            prev0[pl.ds(lo, n), :] = jnp.zeros((n, sensors), BF)

    halo_take(0, tc - ch, ch)
    newest = prev0[pl.ds(tc - ch, ch), :].astype(F32).T.astype(BF)
    pre = pre_own + dot_nt(newest, band[0, :, pl.ds(tc, tc)][:, tc - ch:])
    f = jnp.tanh(pre[:, :tc])
    g = sigmoid(pre[:, tc:])
    gated = (f * g).astype(BF)
    launch(6, gated, gated)
    filt[0] = f
    gate[0] = g

    halo_take(1, tc - 3 * ch, 2 * ch)
    ext[0, :, pl.ds(tc, tc)] = prev0[...].astype(F32).T.astype(BF)
    pre = dot_nt(ext[0, :, pl.ds(tc, tc)], band_h[...]) + cbias[0:1]
    gated_h = (jnp.tanh(pre[:, :tc]) * sigmoid(pre[:, tc:])).astype(BF)
    ship_h(0, dot(gmt[...], gated_h), dot(wht[...], gated_h))
    both = jnp.concatenate([gated, gated_h], axis=1)

    def keep(k, x):
        hops[0, :, pl.ds(k * tc, tc)] = x[:, :tc]
        hops_h[:, pl.ds(k * tc, tc)] = x[:, tc:]

    keep(0, both)
    build_rest()
    gwl[...] = dot(gmt[...], wl[...]).astype(BF)
    gwh[...] = dot(gmt[...], wh[...]).astype(BF)
    whg[...] = dot(wht[...], gm[...]).astype(BF)
    ab = mid_back(fr1, 1, h4, h2)
    af = mid(both, both)

    rp0, rb0 = land(0)
    relay(1, rp0, rb0, *ab[2:])

    rp, rb = land(6)
    relay(7, rp, rb, af[2][:, :tc], af[3][:, :tc])
    both = land_h(0)
    ship_h(1, af[2][:, tc:] + dot(gwh[...], both), af[3][:, tc:] + dot(whg[...], both))
    rp, rb = beside(rp, rb, both)
    bi, fi = whole(*ab[:2], rp0, rb0)
    bb = local(bi.astype(BF), fi.astype(BF))
    gg0 = hop_grad(fr1, 1, 0)
    fo, bo = whole(*af[:2], rp, rb)
    fo, bo = fo.astype(BF), bo.astype(BF)
    keep(1, fo)
    keep(3, bo)
    bf = local(fo, bo)

    def mix_three(mat, hop):
        m = dot_nt(hop(0, 2), mat(0, 2))
        return m + dot_nt(hop(3, 1), mat(3, 1))

    def mat_of(l):
        return lambda k, n: mixall[l, :, pl.ds(k * tc, n * tc)]

    def hop_of(l):
        return lambda k, n: hops[l, :, pl.ds(k * tc, n * tc)]

    part = mix_three(mat_of(0), hop_of(0))
    part_h = mix_three(
        lambda k, n: mix_h[:, pl.ds(k * tc, n * tc)], lambda k, n: hops_h[:, pl.ds(k * tc, n * tc)]
    )

    gg1 = gg0 + bb[0] + bb[1]
    gg1 = gg1 + joined(*land(1))

    def two_late(a, b):
        e = dot_nt(a[:, :tc], mixall[0, :, pl.ds(2 * tc, tc)]), dot_nt(b[:, :tc], mixall[0, :, pl.ds(4 * tc, tc)])
        h = dot_nt(a[:, tc:], mix_h[:, pl.ds(2 * tc, tc)]), dot_nt(b[:, tc:], mix_h[:, pl.ds(4 * tc, tc)])
        return [jnp.concatenate([x, y], axis=1) for x, y in zip(e, h)]

    known = two_late(bf[0].astype(BF), bf[1].astype(BF))
    mbias2 = jnp.concatenate([mbias[0:1], mbias[0:1]], axis=1)
    hid = ext[0].astype(F32) + mbias2 + jnp.concatenate([part, part_h], axis=1) + known[0] + known[1]

    rp, rb = beside(*land(7), land_h(1))
    hid = hid + joined(*[x.astype(BF) for x in two_late(rp, rb)])
    lane2 = lax.broadcasted_iota(jnp.int32, (sensors, 2 * tc), 1)
    ext[1] = jnp.where((lane2 < tc) | ((lane2 >= tc + half) & down), hid, 0.0).astype(BF)

    pre = dot_nt(ext[1], band[1]) + cbias[1:2]
    f = jnp.tanh(pre[:, :tc])
    g = sigmoid(pre[:, tc:])
    filt[1] = f
    gate[1] = g
    gp1 = pre_grad(1, gg1)
    lag_pack(0, 1, gp1)
    lag_start(0)
    gated = (f * g).astype(BF)
    hops[1, :, pl.ds(0, tc)] = gated
    launch(2, gated, gated)
    f2, b2 = whole(bf[0][:, :tc], bf[1][:, :tc], rp[:, :tc], rb[:, :tc])
    hops[0, :, pl.ds(2 * tc, tc)] = f2.astype(BF)
    hops[0, :, pl.ds(4 * tc, tc)] = b2.astype(BF)
    cf = mid(gated, gated)
    new = flow[...] + dot(gp1, band[1, :, pl.ds(0, tc)])
    conv1 = conv_fold(1, gp1)

    flow[...] = new + lag_take(0)
    fr0 = flow[...].astype(BF)
    h4, h2 = hop_grad(fr0, 0, 4).astype(BF), hop_grad(fr0, 0, 2).astype(BF)
    launch(4, h4, h2)
    rp, rb = land(2)
    relay(3, rp, rb, *cf[2:])
    fo, bo = whole(*cf[:2], rp, rb)
    fo, bo = fo.astype(BF), bo.astype(BF)
    hops[1, :, pl.ds(tc, tc)] = fo
    hops[1, :, pl.ds(3 * tc, tc)] = bo
    mix0 = mix_fold(0, fr0, range(HOPS))
    mix1 = mix_fold(1, fr1, (0, 1, 3))
    early = jnp.concatenate([conv1, lanes_of(mix0[:4]), lanes_of([mix0[4]] + mix1)], axis=0)
    for p in range(n_graph):
        e_part[p] = early[p * er:(p + 1) * er]

    def scatter(off):
        p = partner(off)
        graph_copy(e_part.at[p], e_buf.at[me], e_ssem.at[p], e_rsem.at[me], p).start()

    peers(n_graph, scatter)
    e_buf[me] = e_part[me]
    cb_ = mid_back(fr0, 0, h4, h2)
    df = local(fo, bo)
    gg0 = hop_grad(fr0, 0, 0)
    part = mix_three(mat_of(1), hop_of(1))

    rp, rb = land(4)
    relay(5, rp, rb, *cb_[2:])
    bi, fi = whole(*cb_[:2], rp, rb)
    db = local(bi.astype(BF), fi.astype(BF))
    et_buf[z] = gather_sum(e_buf, e_ssem, e_rsem, n_graph, me, graph_copy)
    gather_start(et_buf, et_ssem, et_rsem, n_tm, z, tm_copy)

    f2, b2 = whole(*df, *land(3))
    f2, b2 = f2.astype(BF), b2.astype(BF)
    hops[1, :, pl.ds(2 * tc, tc)] = f2
    hops[1, :, pl.ds(4 * tc, tc)] = b2
    a2, a4 = mix_fold(1, fr1, (2, 4))
    hc = ch // 2
    last = jnp.zeros((hc, tc), F32)
    for g, x in enumerate((a2[:hc], a4[:hc], a2[hc:], a4[hc:])):
        last = jnp.where(lane_g[:hc] == g, x, last)
    m_buf[me] = last
    gather_start(m_buf, m_ssem, m_rsem, n_graph, me, graph_copy)
    mixed = part + dot_nt(f2, mixall[1, :, pl.ds(2 * tc, tc)]) + dot_nt(b2, mixall[1, :, pl.ds(4 * tc, tc)])
    out[...] = (ext[1, :, pl.ds(0, tc)].astype(F32) + (mixed + mbias[1:2])).T.astype(BF)

    gg0 = gg0 + db[0] + db[1]
    gp0 = pre_grad(0, gg0 + joined(*land(5)))
    conv0 = conv_fold(0, gp0)
    if direct:
        swap = graph_copy(pair_s, pair_r, pair_sem.at[0], pair_sem.at[1], mate)
        low = core == 0
        pair_s[...] = jnp.where(low, conv0[hc:], conv0[:hc])
        swap.start()
    else:
        l_buf[me] = conv0
        gather_start(l_buf, l_ssem, l_rsem, n_graph, me, graph_copy)

    lag_pack(1, 0, gp0)
    here = (z * n_graph + me) // 2

    def final_copy(goff, toff):
        p = partner(goff) if goff else me
        return pltpu.make_async_remote_copy(
            src_ref=fin.at[here], dst_ref=fin.at[here],
            send_sem=fin_ssem.at[toff * n_graph + goff], recv_sem=fin_rsem.at[0],
            device_id={"graph": p, "tm": lax.rem(z + toff, n_tm)}, device_id_type=MESH,
        )

    others = [(g, t) for t in range(n_tm) for g in range(0, n_graph, 2) if (g, t) != (0, 0)] if direct else []
    if direct:
        swap.wait_recv()
        fin[here] = (jnp.where(low, conv0[:hc], conv0[hc:]) + pair_r[...]).astype(BF)
        for g, t in reversed(others):
            final_copy(g, t).start()
    lag_start(1)
    mt_buf[z] = gather_sum(m_buf, m_ssem, m_rsem, n_graph, me, graph_copy)
    gather_start(mt_buf, mt_ssem, mt_rsem, n_tm, z, tm_copy)
    eg_buf[me] = gather_sum(et_buf, et_ssem, et_rsem, n_tm, z, tm_copy)
    gather_start(eg_buf, eg_ssem, eg_rsem, n_graph, me, graph_copy)
    if not direct:
        lt_buf[z] = gather_sum(l_buf, l_ssem, l_rsem, n_graph, me, graph_copy)
        gather_start(lt_buf, lt_ssem, lt_rsem, n_tm, z, tm_copy)
    new = flow[...] + dot(gp0, band[0, :, pl.ds(0, tc)])
    def lane_group(x, g):
        return (pltpu.roll(x, tc - g * ch, 1) if g else x)[:, :ch]

    def put_conv(l, x):
        gconv[l, 0] = x[:, :2 * ch]
        gconv[l, 1] = pltpu.roll(x, tc - 2 * ch, 1)[:, :2 * ch]

    def sent_early(off):
        p = partner(off)
        for r in range(send.shape[0]):
            graph_copy(send.at[r, p], recv.at[r, me], r_ssem.at[r, p], r_rsem.at[r], p).wait_send()
        for r in range(send_h.shape[0]):
            graph_copy(send_h.at[r, p], recv_h.at[r, me], h_ssem.at[r, p], h_rsem.at[r], p).wait_send()
        graph_copy(e_part.at[p], e_buf.at[me], e_ssem.at[p], e_rsem.at[me], p).wait_send()
        graph_copy(m_buf.at[me], m_buf.at[me], m_ssem.at[p], m_rsem.at[me], p).wait_send()

    peers(n_graph, sent_early)

    if direct:
        count = fin.shape[0]
        arrived = fin.at[pl.ds(0, count - 1)]
        pltpu.make_async_remote_copy(
            src_ref=arrived, dst_ref=arrived, send_sem=fin_ssem.at[2], recv_sem=fin_rsem.at[0],
            device_id={"graph": mate}, device_id_type=MESH,
        ).wait_recv()
        total = fin[0].astype(F32)
        for p in range(1, count):
            total = total + fin[p].astype(F32)
        back_s[...] = total
        back = graph_copy(back_s, back_r, pair_sem.at[2], pair_sem.at[3], mate)
        back.start()
    gser[...] = (new + lag_take(1)).T.astype(BF)
    m = gather_sum(mt_buf, mt_ssem, mt_rsem, n_tm, z, tm_copy) * scale
    for i, k in enumerate((2, 4)):
        gmix[1, k, pl.ds(0, hc)] = lane_group(m, i)
        gmix[1, k, pl.ds(hc, hc)] = lane_group(m, i + 2)

    def take_group(off):
        p = partner(off)
        graph_copy(eg_buf.at[p], eg_buf.at[p], eg_ssem.at[p], eg_rsem.at[p], p).wait_recv()

    peers(n_graph, take_group)
    e = jnp.concatenate([eg_buf[p] for p in range(n_graph)], axis=0) * scale
    put_conv(1, e[:ch])
    for k in range(4):
        gmix[0, k] = lane_group(e[ch:2 * ch], k)
    gmix[0, 4] = lane_group(e[2 * ch:], 0)
    for i, k in enumerate((0, 1, 3)):
        gmix[1, k] = lane_group(e[2 * ch:], i + 1)
    if direct:
        back.wait_recv()
        theirs = back_r[...]
        halves = [jnp.where(low, total, theirs), jnp.where(low, theirs, total)]
        put_conv(0, jnp.concatenate(halves, axis=0) * scale)
        back.wait_send()
        swap.wait_send()
        for g, t in others:
            final_copy(g, t).wait_send()
    else:
        put_conv(0, gather_sum(lt_buf, lt_ssem, lt_rsem, n_tm, z, tm_copy) * scale)

    def sent_graph(off):
        p = partner(off)
        graph_copy(eg_buf.at[me], eg_buf.at[me], eg_ssem.at[p], eg_rsem.at[me], p).wait_send()
        if not direct:
            graph_copy(l_buf.at[me], l_buf.at[me], l_ssem.at[p], l_rsem.at[me], p).wait_send()

    peers(n_graph, sent_graph)

    def sent_tm(off):
        p = lax.rem(z + off, n_tm)
        tm_copy(et_buf.at[z], et_buf.at[z], et_ssem.at[p], et_rsem.at[z], p).wait_send()
        tm_copy(mt_buf.at[z], mt_buf.at[z], mt_ssem.at[p], mt_rsem.at[z], p).wait_send()
        if not direct:
            tm_copy(lt_buf.at[z], lt_buf.at[z], lt_ssem.at[p], lt_rsem.at[z], p).wait_send()

    peers(n_tm, sent_tm)

    @pl.when(up)
    def _():
        for first in firsts:
            first.wait_send()

    @pl.when(down)
    def _():
        shift_copy(2, pack_s.at[0], pack_r.at[0], -1).wait_send()
        shift_copy(3, pack_s.at[1], pack_r.at[1], -1).wait_send()


def store_kernel(a, b, c, d, ao, bo, co, do, sem):
    copies = [
        pltpu.make_async_copy(src, dst, sem.at[i])
        for i, (src, dst) in enumerate(((a, ao), (b, bo), (c, co), (d, do)))
    ]
    for copy in copies:
        copy.start()
    for copy in copies:
        copy.wait()


def per_device(series, cw, cb, mw, mb, tv, tcol, sidx, smask, cot):
    n_graph = lax.axis_size("graph")
    n_tm = lax.axis_size("tm")
    steps, ch, sensors = series.shape
    tc = steps * ch
    slots = sidx.shape[2]
    halo = n_graph * slots
    wire = BF if slots % 16 == 0 else F32
    narrow, wide = 8, 2
    scale = 1.0 / math.sqrt(float(steps * n_tm * sensors * n_graph))
    vm = pl.BlockSpec(memory_space=pltpu.VMEM)
    hb = pl.BlockSpec(memory_space=pltpu.HBM)
    cwt_shape = (*cw.shape[:2], cw.shape[3], cw.shape[2])
    ins = (
        series.reshape(tc, sensors),
        jnp.swapaxes(cw, 2, 3).reshape(-1, cw.shape[2]),
        cb,
        mw.reshape(-1, ch),
        mb,
        tv.reshape(-1, *tv.shape[2:]),
        tcol,
        sidx[0],
        smask[0],
        cot.reshape(tc, sensors),
    )
    er = 3 * ch // n_graph
    direct = n_graph % 2 == 0 and n_graph * n_tm <= 32 and ch % 32 == 0
    n_all = n_graph * n_tm if direct else 1
    ins = tuple(pltpu.with_memory_space_constraint(x, pltpu.HBM) for x in ins)
    dma = pltpu.SemaphoreType.DMA
    out, gser, gconv, gmix = pl.pallas_call(
        functools.partial(kernel, n_graph, n_tm, steps, scale),
        out_shape=(
            pltpu.VMEM((tc, sensors), BF),
            pltpu.VMEM((tc, sensors), BF),
            pltpu.VMEM(cwt_shape, F32),
            pltpu.VMEM(mw.shape, F32),
        ),
        in_specs=[hb] * 10,
        out_specs=(vm,) * 4,
        scratch_shapes=[
            pltpu.VMEM((sensors, sensors), BF),
            pltpu.VMEM((sensors, sensors), BF),
            pltpu.VMEM((sensors, 2 * halo), BF),
            pltpu.VMEM((halo, sensors), BF),
            pltpu.VMEM((halo, sensors), BF),
            pltpu.VMEM((halo, sensors), BF),
            pltpu.VMEM((halo, halo), BF),
            pltpu.VMEM((halo, halo), BF),
            pltpu.VMEM((GATED_LAYERS, 2 * tc, 2 * tc), BF),
            pltpu.VMEM((2 * tc, tc), BF),
            pltpu.VMEM((GATED_LAYERS, tc, HOPS * tc), BF),
            pltpu.VMEM((tc, HOPS * tc), BF),
            pltpu.VMEM((GATED_LAYERS, sensors, 2 * tc), BF),
            pltpu.VMEM((GATED_LAYERS, sensors, HOPS * tc), BF),
            pltpu.VMEM((sensors, HOPS * tc), BF),
            pltpu.VMEM((GATED_LAYERS, sensors, tc), F32),
            pltpu.VMEM((GATED_LAYERS, sensors, tc), F32),
            pltpu.VMEM((sensors, tc), F32),
            pltpu.VMEM((tc, sensors), BF),
            pltpu.VMEM((2, sensors // 2, tc), BF),
            pltpu.VMEM((2, sensors // 2, tc), BF),
            pltpu.VMEM((narrow, n_graph, 2, slots, tc), wire),
            pltpu.VMEM((narrow, n_graph, 2, slots, tc), wire),
            pltpu.VMEM((wide, n_graph, 1, slots, tc), wire),
            pltpu.VMEM((wide, n_graph, 1, slots, tc), wire),
            pltpu.VMEM((n_graph, er, tc), F32),
            pltpu.VMEM((n_tm, er, tc), F32),
            pltpu.VMEM((n_graph, ch, tc), F32),
            pltpu.VMEM((n_tm, ch, tc), F32),
            pltpu.VMEM((n_graph, er, tc), F32),
            pltpu.VMEM((n_graph, er, tc), F32),
            pltpu.VMEM((n_graph, ch // 2, tc), F32),
            pltpu.VMEM((n_tm, ch // 2, tc), F32),
            *[pltpu.VMEM((ch // 2, tc), F32)] * 4,
            pltpu.VMEM((max(n_all // 2, 1), ch // 2, tc), BF),
            *[(pltpu.SMEM if x.shape == tcol.shape else pltpu.VMEM)(x.shape, x.dtype) for x in ins],
            dma((10,)),
            dma((narrow, n_graph)), dma((narrow,)),
            dma((wide, n_graph)), dma((wide,)),
            dma((4,)), dma((4,)),
            dma((n_graph,)), dma((n_graph,)),
            dma((n_tm,)), dma((n_tm,)),
            dma((n_graph,)), dma((n_graph,)),
            dma((n_tm,)), dma((n_tm,)),
            dma((n_graph,)), dma((n_graph,)),
            dma((n_graph,)), dma((n_graph,)),
            dma((n_tm,)), dma((n_tm,)),
            dma((4,)), dma((n_all,)), dma((1,)),
        ],
        compiler_params=pltpu.CompilerParams(
            collective_id=0, has_side_effects=True, vmem_limit_bytes=48 * 1024 * 1024
        ),
    )(*ins)
    results = tuple(pltpu.with_memory_space_constraint(x, pltpu.VMEM) for x in (out, gser, gconv, gmix))
    out, gser, gconv, gmix = pl.pallas_call(
        store_kernel,
        out_shape=tuple(pltpu.HBM(x.shape, x.dtype) for x in results),
        in_specs=[vm] * 4,
        out_specs=(hb,) * 4,
        scratch_shapes=[dma((4,))],
        compiler_params=pltpu.CompilerParams(vmem_limit_bytes=4 * 1024 * 1024),
    )(*results)
    gconv = jnp.swapaxes(gconv, 2, 3)
    return out.reshape(series.shape), gser.reshape(series.shape), gconv, gmix


def solution(mesh):
    return jax.shard_map(
        per_device,
        mesh=mesh,
        in_specs=(
            P("tm", None, "graph"),
            P(),
            P(),
            P(),
            P(),
            P("graph", None, None, None),
            P("graph", None),
            P("graph", None, None),
            P("graph", None, None),
            P("tm", None, "graph"),
        ),
        out_specs=(P("tm", None, "graph"), P("tm", None, "graph"), P(), P()),
        check_vma=False,
    )
```

```python
import functools
import math

import jax
import jax.numpy as jnp
from jax import lax
from jax.experimental import pallas as pl
from jax.experimental.pallas import tpu as pltpu
from jax.sharding import PartitionSpec as P

GATED_LAYERS = 2
HOPS = 5
BF = jnp.bfloat16
F32 = jnp.float32
MESH = pl.DeviceIdType.MESH


def dot(a, b):
    return lax.dot_general(a, b, (((1,), (0,)), ((), ())), preferred_element_type=F32)


def dot_nt(a, b):
    return lax.dot_general(a, b, (((1,), (1,)), ((), ())), preferred_element_type=F32)


def dot_tn(a, b):
    return lax.dot_general(a, b, (((0,), (0,)), ((), ())), preferred_element_type=F32)


def sigmoid(x):
    return 0.5 + 0.5 * jnp.tanh(0.5 * x)


def quot(x, n):
    return x >> (n.bit_length() - 1) if n & (n - 1) == 0 else x // n


def rest_of(x, n):
    return x & (n - 1) if n & (n - 1) == 0 else lax.rem(x, n)


def peers(count, body):
    if count <= 8:
        for off in range(count - 1, 0, -1):
            body(off)
    elif count > 1:
        lax.fori_loop(1, count, lambda off, c: (body(off), c)[1], 0)


def kernel(
    n_graph, n_tm, steps, scale,
    series_h, cw_h, cb_h, mw_h, mb_h, tv_h, tcol_h, sidx_h, smask_h, cot_h,
    out, gser, gconv, gmix,
    wl, wlt, whgm, wht, gmt, gwl, gwh, whg, band, band_h, mixall, mix_h, ext, hops, hops_h, filt, gate, flow,
    prev0, pack_s, pack_r, send, recv, send_h, recv_h, e_buf, et_buf, l_buf, lt_buf,
    e_part, eg_buf, m_buf, mt_buf, pair_s, pair_r, back_s, back_r, fin,
    series, cw, cb, mw, mb, tv, tcol, sidx, smask, cot, in_sem,
    r_ssem, r_rsem, h_ssem, h_rsem, t_ssem, t_rsem, e_ssem, e_rsem, et_ssem, et_rsem,
    l_ssem, l_rsem, lt_ssem, lt_rsem, eg_ssem, eg_rsem, m_ssem, m_rsem, mt_ssem, mt_rsem,
    pair_sem, fin_ssem, fin_rsem,
):
    me = lax.axis_index("graph")
    z = lax.axis_index("tm")
    tc, sensors = series.shape
    ch = tc // steps
    half = tc // 2
    half_s = sensors // 2
    slots = sidx.shape[1]
    halo = n_graph * slots
    tile = tv.shape[-1]
    rblocks, tslots = tcol.shape
    lblocks = sensors // tile
    hblocks = halo // tile
    wire = send.dtype
    wh = whgm.at[:, pl.ds(0, halo)]
    gm = whgm.at[:, pl.ds(halo, halo)]
    direct = fin.shape[0] > 1
    core = lax.rem(me, 2)
    mate = me + 1 - 2 * core

    def partner(off):
        if n_graph & (n_graph - 1) or n_graph > 8:
            return lax.rem(me + off, n_graph)
        p = 0
        bit = 1
        while bit < n_graph:
            p = p + lax.rem(me // bit + off // bit, 2) * bit
            bit *= 2
        return p

    er = e_part.shape[1]

    loads = [
        pltpu.make_async_copy(src, dst, in_sem.at[i])
        for i, (src, dst) in enumerate(
            ((cw_h, cw), (mw_h, mw), (cb_h, cb), (mb_h, mb), (tv_h, tv), (series_h, series),
             (sidx_h, sidx), (smask_h, smask), (cot_h, cot), (tcol_h, tcol))
        )
    ]
    for load in loads:
        load.start()
    barrier = pltpu.get_barrier_semaphore()

    def greet_graph(off):
        pl.semaphore_signal(barrier, inc=1, device_id={"graph": partner(off)}, device_id_type=MESH)

    def greet_tm(off):
        pl.semaphore_signal(barrier, inc=1, device_id={"tm": lax.rem(z + off, n_tm)}, device_id_type=MESH)

    peers(n_tm, greet_tm)
    peers(n_graph, greet_graph)

    def shift_copy(slot, src, dst, by):
        return pltpu.make_async_remote_copy(
            src_ref=src, dst_ref=dst, send_sem=t_ssem.at[slot], recv_sem=t_rsem.at[slot],
            device_id={"tm": lax.rem(z + by + n_tm, n_tm)}, device_id_type=MESH,
        )

    up = z < n_tm - 1
    down = z > 0

    firsts = [
        shift_copy(0, series_h.at[pl.ds(tc - ch, ch)], prev0.at[pl.ds(tc - ch, ch)], 1),
        shift_copy(1, series_h.at[pl.ds(tc - 3 * ch, 2 * ch)], prev0.at[pl.ds(tc - 3 * ch, 2 * ch)], 1),
    ]
    pl.semaphore_wait(barrier, n_graph - 1 + n_tm - 1)

    @pl.when(up)
    def _():
        for first in firsts:
            first.start()

    prev0[pl.ds(0, tc - 3 * ch), :] = jnp.zeros((tc - 3 * ch, sensors), BF)

    row32 = lax.broadcasted_iota(jnp.int32, (ch, tc), 0)
    lane32 = lax.broadcasted_iota(jnp.int32, (ch, tc), 1)
    spread = jnp.where(rest_of(lane32, ch) == row32, 1.0, 0.0)
    spread_b = spread.astype(BF)
    rt = lax.broadcasted_iota(jnp.int32, (tc, tc), 0)
    lt = lax.broadcasted_iota(jnp.int32, (tc, tc), 1)
    rt, lt = quot(rt, ch), quot(lt, ch)
    same = rt == lt
    late = rt >= steps // 2

    def before(d):
        return lt == rt - d

    def before_prev(d):
        return lt == rt - d + steps

    for load in loads[:4]:
        load.wait()
    taps = 2 * GATED_LAYERS
    rs = lax.broadcasted_iota(jnp.int32, (taps * ch, taps * tc), 0)
    ls = lax.broadcasted_iota(jnp.int32, (taps * ch, taps * tc), 1)
    spread_taps = jnp.where(quot(ls, tc) * ch + rest_of(ls, ch) == rs, 1.0, 0.0).astype(BF)
    def after(d):
        return rt == lt - d

    def after_prev(d):
        return rt == lt - d + steps

    cwr = dot_tn(cw[...], spread_taps)
    mwr = dot(mw[...], spread_b)

    def stack(x, base):
        return jnp.concatenate([x[base:base + ch]] * steps, axis=0)

    for l in range(GATED_LAYERS):
        d = l + 1
        for h in range(2):
            w0 = stack(cwr[:, (l * 2) * tc:(l * 2 + 1) * tc], h * ch)
            w1 = stack(cwr[:, (l * 2 + 1) * tc:(l * 2 + 2) * tc], h * ch)
            own = (jnp.where(same, w0, 0.0) + jnp.where(before(d), w1, 0.0)).astype(BF)
            band[l, pl.ds(h * tc, tc), pl.ds(0, tc)] = own
            band[l, pl.ds(h * tc, tc), pl.ds(tc, tc)] = jnp.where(before_prev(d), w1, 0.0).astype(BF)
            if l == 0:
                band_h[pl.ds(h * tc, tc), :] = jnp.concatenate([own[half:], own[half:]], axis=0)
        for k in range(HOPS):
            mk = stack(mwr, (l * HOPS + k) * ch)
            mixall[l, :, pl.ds(k * tc, tc)] = jnp.where(same, mk, 0.0).astype(BF)
            if l == 0:
                at = (rt == lt + steps // 2) if k in (1, 2) else (same & late)
                mix_h[:, pl.ds(k * tc, tc)] = jnp.where(at, mk, 0.0).astype(BF)

    r64 = lax.broadcasted_iota(jnp.int32, (2 * ch, 2 * tc), 0)
    l64 = lax.broadcasted_iota(jnp.int32, (2 * ch, 2 * tc), 1)
    spread2 = jnp.where(rest_of(l64, ch) + quot(l64, tc) * ch == r64, 1.0, 0.0)
    cbias = lax.dot_general(cb[...], spread2, (((1,), (0,)), ((), ())), precision=lax.Precision.HIGHEST, preferred_element_type=F32)
    mbias = lax.dot_general(mb[...], spread, (((1,), (0,)), ((), ())), precision=lax.Precision.HIGHEST, preferred_element_type=F32)

    for load in loads[4:]:
        load.wait()
    def on(r, k, c):
        return (tcol[r, k] == c).astype(jnp.int32).astype(F32)

    def placed(blocks, r, c):
        y = blocks[0] * on(r, 0, c)
        for k in range(1, tslots):
            y = y + blocks[k] * on(r, k, c)
        return y.astype(BF)

    def flipped(r):
        return [tv[r * tslots + k].astype(F32).T for k in range(tslots)]

    for r in range(rblocks):
        flips = flipped(r)
        for c in range(hblocks):
            wht[pl.ds(c * tile, tile), pl.ds(r * tile, tile)] = placed(flips, r, lblocks + c)

    def build_rest():
        for r in range(rblocks):
            tiles = [tv[r * tslots + k].astype(F32) for k in range(tslots)]
            flips = flipped(r)
            for c in range(lblocks):
                wl[pl.ds(r * tile, tile), pl.ds(c * tile, tile)] = placed(tiles, r, c)
                wlt[pl.ds(c * tile, tile), pl.ds(r * tile, tile)] = placed(flips, r, c)
            for c in range(hblocks):
                wh[pl.ds(r * tile, tile), pl.ds(c * tile, tile)] = placed(tiles, r, lblocks + c)

    key = jnp.where(smask[...] != 0, sidx[...] + 1, 0)
    es = lax.broadcasted_iota(jnp.int32, (slots, halo), 0)
    ej = lax.broadcasted_iota(jnp.int32, (slots, halo), 1)
    pick = jnp.where(rest_of(ej, slots) == es, 1.0, 0.0).astype(BF)
    hi = dot((key >> 5).astype(F32).astype(BF), pick)
    lo = dot((key & 31).astype(F32).astype(BF), pick)
    pr = lax.broadcasted_iota(jnp.int32, (n_graph, halo), 0)
    pj = quot(lax.broadcasted_iota(jnp.int32, (n_graph, halo), 1), slots)
    keys = jnp.sum(jnp.where(pr == pj, hi * 32.0 + lo, 0.0), axis=0, keepdims=True)
    ids = lax.broadcasted_iota(jnp.int32, (sensors, halo), 0).astype(F32) + 1.0
    onehot = jnp.where(ids == keys, 1.0, 0.0)
    gm[...] = onehot.astype(BF)
    gmt[...] = onehot.T.astype(BF)

    def graph_copy(src, dst, ssem, rsem, p):
        return pltpu.make_async_remote_copy(
            src_ref=src, dst_ref=dst, send_sem=ssem, recv_sem=rsem,
            device_id={"graph": p}, device_id_type=MESH,
        )

    def tm_copy(src, dst, ssem, rsem, p):
        return pltpu.make_async_remote_copy(
            src_ref=src, dst_ref=dst, send_sem=ssem, recv_sem=rsem,
            device_id={"tm": p}, device_id_type=MESH,
        )

    lane_low = lax.broadcasted_iota(jnp.int32, (halo, tc), 1) < half

    def ship(blocks, out_buf, in_buf, ssem, rsem, r):
        for i, block in enumerate(blocks):
            out_buf[r, :, i] = block.astype(BF).reshape(n_graph, slots, tc).astype(wire)

        def go(off):
            p = partner(off)
            graph_copy(out_buf.at[r, p], in_buf.at[r, me], ssem.at[r, p], rsem.at[r], p).start()

        peers(n_graph, go)
        in_buf[r, me] = out_buf[r, me]

    def collect(in_buf, ssem, rsem, r, count):
        arrived = in_buf.at[r, pl.ds(0, n_graph - 1)]
        graph_copy(arrived, arrived, ssem.at[r, 0], rsem.at[r], partner(1)).wait_recv()
        return [in_buf[r, :, i].reshape(halo, tc).astype(BF) for i in range(count)]

    def launch(r, pull_in, push_in):
        ship((dot(gmt[...], pull_in), dot(wht[...], push_in)), send, recv, r_ssem, r_rsem, r)

    def ship_h(r, sp, sb):
        ship((jnp.where(lane_low, sp, sb),), send_h, recv_h, h_ssem, h_rsem, r)

    def local(pull_in, push_in):
        return dot(wl[...], pull_in), dot(wlt[...], push_in)

    def land(r):
        return collect(recv, r_ssem, r_rsem, r, 2)

    def land_h(r):
        return collect(recv_h, h_ssem, h_rsem, r, 1)[0]

    def beside(rp, rb, both):
        return jnp.concatenate([rp, both], axis=1), jnp.concatenate([rb, both], axis=1)

    def relay(r, rp, rb, sp, sb):
        ship((sp + dot(gwh[...], rp), sb + dot(whg[...], rb)), send, recv, r_ssem, r_rsem, r)

    def joined(a, b):
        return dot(whgm[...], jnp.concatenate([a, b], axis=0))

    def whole(pulled, pushed, rp, rb):
        return pulled + dot(wh[...], rp), pushed + dot(gm[...], rb)

    lane_half = lax.broadcasted_iota(jnp.int32, (half_s, tc), 1) < half

    def pack(x):
        return jnp.where(lane_half, pltpu.roll(x[:half_s], half, 1), x[half_s:]).astype(BF)

    def unpack(p):
        x = p.astype(F32)
        return jnp.concatenate([pltpu.roll(x, half, 1), x], axis=0)

    lane_g = quot(lax.broadcasted_iota(jnp.int32, (ch, tc), 1), ch)

    def fold(x):
        y = x[0:ch]
        for t in range(1, steps):
            y = y + x[t * ch:(t + 1) * ch]
        sh = ch
        while sh < tc:
            y = y + pltpu.roll(y, sh, 1)
            sh *= 2
        return y

    def lanes_of(xs):
        y = jnp.zeros((ch, tc), F32)
        for g, x in enumerate(xs):
            y = jnp.where(lane_g == g, x, y)
        return y

    def gather_start(buf, ssem, rsem, count, here, copy):
        def go(off):
            p = lax.rem(here + off, count)
            copy(buf.at[here], buf.at[here], ssem.at[p], rsem.at[here], p).start()

        peers(count, go)

    def gather_sum(buf, ssem, rsem, count, here, copy):
        def take(off):
            p = lax.rem(here + off, count)
            copy(buf.at[p], buf.at[p], ssem.at[p], rsem.at[p], p).wait_recv()

        peers(count, take)
        total = buf[0].astype(F32)
        for p in range(1, count):
            total = total + buf[p].astype(F32)
        return total

    def hop_grad(fr, l, k):
        return dot(fr, mixall[l, :, pl.ds(k * tc, tc)])

    def mix_fold(l, fr, ks):
        folds = []
        for k in ks:
            hop = hops[l, :, pl.ds(k * tc, tc)]
            folds.append(fold(jnp.where(same, dot(cot[...], hop) if l == 1 else dot_tn(fr, hop), 0.0)))
        return folds

    def conv_fold(l, gp):
        d = l + 1
        if l == 0:
            prod = (dot(series[...], gp), dot(prev0[...], gp))
        else:
            prod = [dot_tn(ext[l, :, pl.ds(i * tc, tc)], gp) for i in range(2)]
        pieces = []
        for tap in range(2):
            for h in range(2):
                own = prod[0][:, h * tc:(h + 1) * tc]
                if tap == 0:
                    x = jnp.where(same, own, 0.0)
                else:
                    x = jnp.where(after(d), own, 0.0) + jnp.where(after_prev(d), prod[1][:, h * tc:(h + 1) * tc], 0.0)
                pieces.append(fold(x))
        return lanes_of(pieces)

    def pre_grad(l, gg):
        f = filt[l]
        g = gate[l]
        return jnp.concatenate([gg * g * (1.0 - f * f), gg * f * g * (1.0 - g)], axis=1).astype(BF)

    def lag_pack(i, l, gp):
        pack_s[i] = pack(dot(gp, band[l, :, pl.ds(tc, tc)]))

    def lag_start(i):
        @pl.when(down)
        def _():
            shift_copy(2 + i, pack_s.at[i], pack_r.at[i], -1).start()

    lanes_late = lax.broadcasted_iota(jnp.int32, (sensors, tc), 1) >= half

    def lag_take(i):
        @pl.when(up)
        def _():
            shift_copy(2 + i, pack_s.at[i], pack_r.at[i], -1).wait_recv()

        @pl.when(jnp.logical_not(up))
        def _():
            pack_r[i] = jnp.zeros((half_s, tc), BF)

        return jnp.where(lanes_late, unpack(pack_r[i]), 0.0)

    flow[...] = cot[...].astype(F32).T
    fr1 = flow[...].astype(BF)
    h4, h2 = hop_grad(fr1, 1, 4).astype(BF), hop_grad(fr1, 1, 2).astype(BF)
    launch(0, h4, h2)

    def mid_back(fr, l, pull_in, push_in):
        pulled, pushed = local(pull_in, push_in)
        pulled = pulled + hop_grad(fr, l, 3)
        pushed = pushed + hop_grad(fr, l, 1)
        sp = dot(gwl[...], pull_in) + hop_grad(dot(gmt[...], fr).astype(BF), l, 3)
        return pulled, pushed, sp, dot(wht[...], pushed.astype(BF))

    def mid(pull_in, push_in):
        pulled, pushed = local(pull_in, push_in)
        return pulled, pushed, dot(gwl[...], pull_in), dot(wht[...], pushed.astype(BF))

    ext[0, :, pl.ds(0, tc)] = series[...].astype(F32).T.astype(BF)
    pre_own = dot_nt(ext[0, :, pl.ds(0, tc)], band[0, :, pl.ds(0, tc)]) + cbias[0:1]

    def halo_take(i, lo, n):
        @pl.when(down)
        def _():
            firsts[i].wait_recv()

        @pl.when(jnp.logical_not(down))
        def _():
            prev0[pl.ds(lo, n), :] = jnp.zeros((n, sensors), BF)

    halo_take(0, tc - ch, ch)
    newest = prev0[pl.ds(tc - ch, ch), :].astype(F32).T.astype(BF)
    pre = pre_own + dot_nt(newest, band[0, :, pl.ds(tc, tc)][:, tc - ch:])
    f = jnp.tanh(pre[:, :tc])
    g = sigmoid(pre[:, tc:])
    gated = (f * g).astype(BF)
    launch(6, gated, gated)
    filt[0] = f
    gate[0] = g

    halo_take(1, tc - 3 * ch, 2 * ch)
    ext[0, :, pl.ds(tc, tc)] = prev0[...].astype(F32).T.astype(BF)
    pre = dot_nt(ext[0, :, pl.ds(tc, tc)], band_h[...]) + cbias[0:1]
    gated_h = (jnp.tanh(pre[:, :tc]) * sigmoid(pre[:, tc:])).astype(BF)
    ship_h(0, dot(gmt[...], gated_h), dot(wht[...], gated_h))
    both = jnp.concatenate([gated, gated_h], axis=1)

    def keep(k, x):
        hops[0, :, pl.ds(k * tc, tc)] = x[:, :tc]
        hops_h[:, pl.ds(k * tc, tc)] = x[:, tc:]

    keep(0, both)
    build_rest()
    gwl[...] = dot(gmt[...], wl[...]).astype(BF)
    gwh[...] = dot(gmt[...], wh[...]).astype(BF)
    whg[...] = dot(wht[...], gm[...]).astype(BF)
    ab = mid_back(fr1, 1, h4, h2)
    af = mid(both, both)

    rp0, rb0 = land(0)
    relay(1, rp0, rb0, *ab[2:])

    rp, rb = land(6)
    relay(7, rp, rb, af[2][:, :tc], af[3][:, :tc])
    both = land_h(0)
    ship_h(1, af[2][:, tc:] + dot(gwh[...], both), af[3][:, tc:] + dot(whg[...], both))
    rp, rb = beside(rp, rb, both)
    bi, fi = whole(*ab[:2], rp0, rb0)
    bb = local(bi.astype(BF), fi.astype(BF))
    gg0 = hop_grad(fr1, 1, 0)
    fo, bo = whole(*af[:2], rp, rb)
    fo, bo = fo.astype(BF), bo.astype(BF)
    keep(1, fo)
    keep(3, bo)
    bf = local(fo, bo)

    def mix_three(mat, hop):
        m = dot_nt(hop(0, 2), mat(0, 2))
        return m + dot_nt(hop(3, 1), mat(3, 1))

    def mat_of(l):
        return lambda k, n: mixall[l, :, pl.ds(k * tc, n * tc)]

    def hop_of(l):
        return lambda k, n: hops[l, :, pl.ds(k * tc, n * tc)]

    part = mix_three(mat_of(0), hop_of(0))
    part_h = mix_three(
        lambda k, n: mix_h[:, pl.ds(k * tc, n * tc)], lambda k, n: hops_h[:, pl.ds(k * tc, n * tc)]
    )

    gg1 = gg0 + bb[0] + bb[1]
    gg1 = gg1 + joined(*land(1))

    def two_late(a, b):
        e = dot_nt(a[:, :tc], mixall[0, :, pl.ds(2 * tc, tc)]), dot_nt(b[:, :tc], mixall[0, :, pl.ds(4 * tc, tc)])
        h = dot_nt(a[:, tc:], mix_h[:, pl.ds(2 * tc, tc)]), dot_nt(b[:, tc:], mix_h[:, pl.ds(4 * tc, tc)])
        return [jnp.concatenate([x, y], axis=1) for x, y in zip(e, h)]

    known = two_late(bf[0].astype(BF), bf[1].astype(BF))
    mbias2 = jnp.concatenate([mbias[0:1], mbias[0:1]], axis=1)
    hid = ext[0].astype(F32) + mbias2 + jnp.concatenate([part, part_h], axis=1) + known[0] + known[1]

    rp, rb = beside(*land(7), land_h(1))
    hid = hid + joined(*[x.astype(BF) for x in two_late(rp, rb)])
    lane2 = lax.broadcasted_iota(jnp.int32, (sensors, 2 * tc), 1)
    ext[1] = jnp.where((lane2 < tc) | ((lane2 >= tc + half) & down), hid, 0.0).astype(BF)

    pre = dot_nt(ext[1], band[1]) + cbias[1:2]
    f = jnp.tanh(pre[:, :tc])
    g = sigmoid(pre[:, tc:])
    filt[1] = f
    gate[1] = g
    gp1 = pre_grad(1, gg1)
    lag_pack(0, 1, gp1)
    lag_start(0)
    gated = (f * g).astype(BF)
    hops[1, :, pl.ds(0, tc)] = gated
    launch(2, gated, gated)
    f2, b2 = whole(bf[0][:, :tc], bf[1][:, :tc], rp[:, :tc], rb[:, :tc])
    hops[0, :, pl.ds(2 * tc, tc)] = f2.astype(BF)
    hops[0, :, pl.ds(4 * tc, tc)] = b2.astype(BF)
    cf = mid(gated, gated)
    new = flow[...] + dot(gp1, band[1, :, pl.ds(0, tc)])
    conv1 = conv_fold(1, gp1)

    flow[...] = new + lag_take(0)
    fr0 = flow[...].astype(BF)
    h4, h2 = hop_grad(fr0, 0, 4).astype(BF), hop_grad(fr0, 0, 2).astype(BF)
    launch(4, h4, h2)
    rp, rb = land(2)
    relay(3, rp, rb, *cf[2:])
    fo, bo = whole(*cf[:2], rp, rb)
    fo, bo = fo.astype(BF), bo.astype(BF)
    hops[1, :, pl.ds(tc, tc)] = fo
    hops[1, :, pl.ds(3 * tc, tc)] = bo
    mix0 = mix_fold(0, fr0, range(HOPS))
    mix1 = mix_fold(1, fr1, (0, 1, 3))
    early = jnp.concatenate([conv1, lanes_of(mix0[:4]), lanes_of([mix0[4]] + mix1)], axis=0)
    for p in range(n_graph):
        e_part[p] = early[p * er:(p + 1) * er]

    def scatter(off):
        p = partner(off)
        graph_copy(e_part.at[p], e_buf.at[me], e_ssem.at[p], e_rsem.at[me], p).start()

    peers(n_graph, scatter)
    e_buf[me] = e_part[me]
    cb_ = mid_back(fr0, 0, h4, h2)
    df = local(fo, bo)
    gg0 = hop_grad(fr0, 0, 0)
    part = mix_three(mat_of(1), hop_of(1))

    rp, rb = land(4)
    relay(5, rp, rb, *cb_[2:])
    bi, fi = whole(*cb_[:2], rp, rb)
    db = local(bi.astype(BF), fi.astype(BF))
    et_buf[z] = gather_sum(e_buf, e_ssem, e_rsem, n_graph, me, graph_copy)
    gather_start(et_buf, et_ssem, et_rsem, n_tm, z, tm_copy)

    f2, b2 = whole(*df, *land(3))
    f2, b2 = f2.astype(BF), b2.astype(BF)
    hops[1, :, pl.ds(2 * tc, tc)] = f2
    hops[1, :, pl.ds(4 * tc, tc)] = b2
    a2, a4 = mix_fold(1, fr1, (2, 4))
    hc = ch // 2
    last = jnp.zeros((hc, tc), F32)
    for g, x in enumerate((a2[:hc], a4[:hc], a2[hc:], a4[hc:])):
        last = jnp.where(lane_g[:hc] == g, x, last)
    m_buf[me] = last.astype(BF)
    gather_start(m_buf, m_ssem, m_rsem, n_graph, me, graph_copy)
    mixed = part + dot_nt(f2, mixall[1, :, pl.ds(2 * tc, tc)]) + dot_nt(b2, mixall[1, :, pl.ds(4 * tc, tc)])
    out[...] = (ext[1, :, pl.ds(0, tc)].astype(F32) + (mixed + mbias[1:2])).T.astype(BF)

    gg0 = gg0 + db[0] + db[1]
    gp0 = pre_grad(0, gg0 + joined(*land(5)))
    conv0 = conv_fold(0, gp0)
    if direct:
        swap = graph_copy(pair_s, pair_r, pair_sem.at[0], pair_sem.at[1], mate)
        low = core == 0
        pair_s[...] = jnp.where(low, conv0[hc:], conv0[:hc])
        swap.start()
    else:
        l_buf[me] = conv0
        gather_start(l_buf, l_ssem, l_rsem, n_graph, me, graph_copy)

    lag_pack(1, 0, gp0)
    here = (z * n_graph + me) // 2

    def final_copy(goff, toff):
        p = partner(goff) if goff else me
        return pltpu.make_async_remote_copy(
            src_ref=fin.at[here], dst_ref=fin.at[here],
            send_sem=fin_ssem.at[toff * n_graph + goff], recv_sem=fin_rsem.at[0],
            device_id={"graph": p, "tm": lax.rem(z + toff, n_tm)}, device_id_type=MESH,
        )

    others = [(g, t) for t in range(n_tm) for g in range(0, n_graph, 2) if (g, t) != (0, 0)] if direct else []
    if direct:
        swap.wait_recv()
        fin[here] = (jnp.where(low, conv0[:hc], conv0[hc:]) + pair_r[...]).astype(BF)
        for g, t in reversed(others):
            final_copy(g, t).start()
    lag_start(1)
    mt_buf[z] = gather_sum(m_buf, m_ssem, m_rsem, n_graph, me, graph_copy).astype(BF)
    gather_start(mt_buf, mt_ssem, mt_rsem, n_tm, z, tm_copy)
    eg_buf[me] = gather_sum(et_buf, et_ssem, et_rsem, n_tm, z, tm_copy)
    gather_start(eg_buf, eg_ssem, eg_rsem, n_graph, me, graph_copy)
    if not direct:
        lt_buf[z] = gather_sum(l_buf, l_ssem, l_rsem, n_graph, me, graph_copy)
        gather_start(lt_buf, lt_ssem, lt_rsem, n_tm, z, tm_copy)
    new = flow[...] + dot(gp0, band[0, :, pl.ds(0, tc)])
    def lane_group(x, g):
        return (pltpu.roll(x, tc - g * ch, 1) if g else x)[:, :ch]

    def put_conv(l, x):
        gconv[l, 0] = x[:, :2 * ch]
        gconv[l, 1] = pltpu.roll(x, tc - 2 * ch, 1)[:, :2 * ch]

    def sent_early(off):
        p = partner(off)
        for r in range(send.shape[0]):
            graph_copy(send.at[r, p], recv.at[r, me], r_ssem.at[r, p], r_rsem.at[r], p).wait_send()
        for r in range(send_h.shape[0]):
            graph_copy(send_h.at[r, p], recv_h.at[r, me], h_ssem.at[r, p], h_rsem.at[r], p).wait_send()
        graph_copy(e_part.at[p], e_buf.at[me], e_ssem.at[p], e_rsem.at[me], p).wait_send()
        graph_copy(m_buf.at[me], m_buf.at[me], m_ssem.at[p], m_rsem.at[me], p).wait_send()

    peers(n_graph, sent_early)

    if direct:
        count = fin.shape[0]
        arrived = fin.at[pl.ds(0, count - 1)]
        pltpu.make_async_remote_copy(
            src_ref=arrived, dst_ref=arrived, send_sem=fin_ssem.at[2], recv_sem=fin_rsem.at[0],
            device_id={"graph": mate}, device_id_type=MESH,
        ).wait_recv()
        total = fin[0].astype(F32)
        for p in range(1, count):
            total = total + fin[p].astype(F32)
        back_s[...] = total
        back = graph_copy(back_s, back_r, pair_sem.at[2], pair_sem.at[3], mate)
        back.start()
    gser[...] = (new + lag_take(1)).T.astype(BF)
    m = gather_sum(mt_buf, mt_ssem, mt_rsem, n_tm, z, tm_copy) * scale
    for i, k in enumerate((2, 4)):
        gmix[1, k, pl.ds(0, hc)] = lane_group(m, i)
        gmix[1, k, pl.ds(hc, hc)] = lane_group(m, i + 2)

    def take_group(off):
        p = partner(off)
        graph_copy(eg_buf.at[p], eg_buf.at[p], eg_ssem.at[p], eg_rsem.at[p], p).wait_recv()

    peers(n_graph, take_group)
    e = jnp.concatenate([eg_buf[p] for p in range(n_graph)], axis=0) * scale
    put_conv(1, e[:ch])
    for k in range(4):
        gmix[0, k] = lane_group(e[ch:2 * ch], k)
    gmix[0, 4] = lane_group(e[2 * ch:], 0)
    for i, k in enumerate((0, 1, 3)):
        gmix[1, k] = lane_group(e[2 * ch:], i + 1)
    if direct:
        back.wait_recv()
        theirs = back_r[...]
        halves = [jnp.where(low, total, theirs), jnp.where(low, theirs, total)]
        put_conv(0, jnp.concatenate(halves, axis=0) * scale)
        back.wait_send()
        swap.wait_send()
        for g, t in others:
            final_copy(g, t).wait_send()
    else:
        put_conv(0, gather_sum(lt_buf, lt_ssem, lt_rsem, n_tm, z, tm_copy) * scale)

    def sent_graph(off):
        p = partner(off)
        graph_copy(eg_buf.at[me], eg_buf.at[me], eg_ssem.at[p], eg_rsem.at[me], p).wait_send()
        if not direct:
            graph_copy(l_buf.at[me], l_buf.at[me], l_ssem.at[p], l_rsem.at[me], p).wait_send()

    peers(n_graph, sent_graph)

    def sent_tm(off):
        p = lax.rem(z + off, n_tm)
        tm_copy(et_buf.at[z], et_buf.at[z], et_ssem.at[p], et_rsem.at[z], p).wait_send()
        tm_copy(mt_buf.at[z], mt_buf.at[z], mt_ssem.at[p], mt_rsem.at[z], p).wait_send()
        if not direct:
            tm_copy(lt_buf.at[z], lt_buf.at[z], lt_ssem.at[p], lt_rsem.at[z], p).wait_send()

    peers(n_tm, sent_tm)

    @pl.when(up)
    def _():
        for first in firsts:
            first.wait_send()

    @pl.when(down)
    def _():
        shift_copy(2, pack_s.at[0], pack_r.at[0], -1).wait_send()
        shift_copy(3, pack_s.at[1], pack_r.at[1], -1).wait_send()


def store_kernel(a, b, c, d, ao, bo, co, do, sem):
    copies = [
        pltpu.make_async_copy(src, dst, sem.at[i])
        for i, (src, dst) in enumerate(((a, ao), (b, bo), (c, co), (d, do)))
    ]
    for copy in copies:
        copy.start()
    for copy in copies:
        copy.wait()


def per_device(series, cw, cb, mw, mb, tv, tcol, sidx, smask, cot):
    n_graph = lax.axis_size("graph")
    n_tm = lax.axis_size("tm")
    steps, ch, sensors = series.shape
    tc = steps * ch
    slots = sidx.shape[2]
    halo = n_graph * slots
    wire = BF if slots % 16 == 0 else F32
    narrow, wide = 8, 2
    scale = 1.0 / math.sqrt(float(steps * n_tm * sensors * n_graph))
    vm = pl.BlockSpec(memory_space=pltpu.VMEM)
    hb = pl.BlockSpec(memory_space=pltpu.HBM)
    cwt_shape = (*cw.shape[:2], cw.shape[3], cw.shape[2])
    ins = (
        series.reshape(tc, sensors),
        jnp.swapaxes(cw, 2, 3).reshape(-1, cw.shape[2]),
        cb,
        mw.reshape(-1, ch),
        mb,
        tv.reshape(-1, *tv.shape[2:]),
        tcol,
        sidx[0],
        smask[0],
        cot.reshape(tc, sensors),
    )
    er = 3 * ch // n_graph
    direct = n_graph % 2 == 0 and n_graph * n_tm <= 32 and ch % 32 == 0
    n_all = n_graph * n_tm if direct else 1
    ins = tuple(pltpu.with_memory_space_constraint(x, pltpu.HBM) for x in ins)
    dma = pltpu.SemaphoreType.DMA
    out, gser, gconv, gmix = pl.pallas_call(
        functools.partial(kernel, n_graph, n_tm, steps, scale),
        out_shape=(
            pltpu.VMEM((tc, sensors), BF),
            pltpu.VMEM((tc, sensors), BF),
            pltpu.VMEM(cwt_shape, F32),
            pltpu.VMEM(mw.shape, F32),
        ),
        in_specs=[hb] * 10,
        out_specs=(vm,) * 4,
        scratch_shapes=[
            pltpu.VMEM((sensors, sensors), BF),
            pltpu.VMEM((sensors, sensors), BF),
            pltpu.VMEM((sensors, 2 * halo), BF),
            pltpu.VMEM((halo, sensors), BF),
            pltpu.VMEM((halo, sensors), BF),
            pltpu.VMEM((halo, sensors), BF),
            pltpu.VMEM((halo, halo), BF),
            pltpu.VMEM((halo, halo), BF),
            pltpu.VMEM((GATED_LAYERS, 2 * tc, 2 * tc), BF),
            pltpu.VMEM((2 * tc, tc), BF),
            pltpu.VMEM((GATED_LAYERS, tc, HOPS * tc), BF),
            pltpu.VMEM((tc, HOPS * tc), BF),
            pltpu.VMEM((GATED_LAYERS, sensors, 2 * tc), BF),
            pltpu.VMEM((GATED_LAYERS, sensors, HOPS * tc), BF),
            pltpu.VMEM((sensors, HOPS * tc), BF),
            pltpu.VMEM((GATED_LAYERS, sensors, tc), F32),
            pltpu.VMEM((GATED_LAYERS, sensors, tc), F32),
            pltpu.VMEM((sensors, tc), F32),
            pltpu.VMEM((tc, sensors), BF),
            pltpu.VMEM((2, sensors // 2, tc), BF),
            pltpu.VMEM((2, sensors // 2, tc), BF),
            pltpu.VMEM((narrow, n_graph, 2, slots, tc), wire),
            pltpu.VMEM((narrow, n_graph, 2, slots, tc), wire),
            pltpu.VMEM((wide, n_graph, 1, slots, tc), wire),
            pltpu.VMEM((wide, n_graph, 1, slots, tc), wire),
            pltpu.VMEM((n_graph, er, tc), F32),
            pltpu.VMEM((n_tm, er, tc), F32),
            pltpu.VMEM((n_graph, ch, tc), F32),
            pltpu.VMEM((n_tm, ch, tc), F32),
            pltpu.VMEM((n_graph, er, tc), F32),
            pltpu.VMEM((n_graph, er, tc), F32),
            pltpu.VMEM((n_graph, ch // 2, tc), BF),
            pltpu.VMEM((n_tm, ch // 2, tc), BF),
            *[pltpu.VMEM((ch // 2, tc), F32)] * 4,
            pltpu.VMEM((max(n_all // 2, 1), ch // 2, tc), BF),
            *[(pltpu.SMEM if x.shape == tcol.shape else pltpu.VMEM)(x.shape, x.dtype) for x in ins],
            dma((10,)),
            dma((narrow, n_graph)), dma((narrow,)),
            dma((wide, n_graph)), dma((wide,)),
            dma((4,)), dma((4,)),
            dma((n_graph,)), dma((n_graph,)),
            dma((n_tm,)), dma((n_tm,)),
            dma((n_graph,)), dma((n_graph,)),
            dma((n_tm,)), dma((n_tm,)),
            dma((n_graph,)), dma((n_graph,)),
            dma((n_graph,)), dma((n_graph,)),
            dma((n_tm,)), dma((n_tm,)),
            dma((4,)), dma((n_all,)), dma((1,)),
        ],
        compiler_params=pltpu.CompilerParams(
            collective_id=0, has_side_effects=True, vmem_limit_bytes=48 * 1024 * 1024
        ),
    )(*ins)
    results = tuple(pltpu.with_memory_space_constraint(x, pltpu.VMEM) for x in (out, gser, gconv, gmix))
    out, gser, gconv, gmix = pl.pallas_call(
        store_kernel,
        out_shape=tuple(pltpu.HBM(x.shape, x.dtype) for x in results),
        in_specs=[vm] * 4,
        out_specs=(hb,) * 4,
        scratch_shapes=[dma((4,))],
        compiler_params=pltpu.CompilerParams(vmem_limit_bytes=4 * 1024 * 1024),
    )(*results)
    gconv = jnp.swapaxes(gconv, 2, 3)
    return out.reshape(series.shape), gser.reshape(series.shape), gconv, gmix


def solution(mesh):
    return jax.shard_map(
        per_device,
        mesh=mesh,
        in_specs=(
            P("tm", None, "graph"),
            P(),
            P(),
            P(),
            P(),
            P("graph", None, None, None),
            P("graph", None),
            P("graph", None, None),
            P("graph", None, None),
            P("tm", None, "graph"),
        ),
        out_specs=(P("tm", None, "graph"), P("tm", None, "graph"), P(), P()),
        check_vma=False,
    )
```

```python
import functools
import math

import jax
import jax.numpy as jnp
from jax import lax
from jax.experimental import pallas as pl
from jax.experimental.pallas import tpu as pltpu
from jax.sharding import PartitionSpec as P

GATED_LAYERS = 2
HOPS = 5
BF = jnp.bfloat16
F32 = jnp.float32
MESH = pl.DeviceIdType.MESH


def dot(a, b):
    return lax.dot_general(a, b, (((1,), (0,)), ((), ())), preferred_element_type=F32)


def dot_nt(a, b):
    return lax.dot_general(a, b, (((1,), (1,)), ((), ())), preferred_element_type=F32)


def dot_tn(a, b):
    return lax.dot_general(a, b, (((0,), (0,)), ((), ())), preferred_element_type=F32)


def sigmoid(x):
    return 0.5 + 0.5 * jnp.tanh(0.5 * x)


def quot(x, n):
    return x >> (n.bit_length() - 1) if n & (n - 1) == 0 else x // n


def rest_of(x, n):
    return x & (n - 1) if n & (n - 1) == 0 else lax.rem(x, n)


def peers(count, body):
    if count <= 8:
        for off in range(count - 1, 0, -1):
            body(off)
    elif count > 1:
        lax.fori_loop(1, count, lambda off, c: (body(off), c)[1], 0)


def kernel(
    n_graph, n_tm, steps, scale,
    series_h, cw_h, cb_h, mw_h, mb_h, tv_h, tcol_h, sidx_h, smask_h, cot_h,
    out, gser, gconv, gmix,
    wl, wlt, whgm, wht, gmt, gwl, gwh, whg, band, band_h, mixall, mix_h, ext, hops, hops_h, filt, gate, flow,
    prev0, pack_s, pack_r, send, recv, send_h, recv_h, e_buf, et_buf, l_buf, lt_buf,
    e_part, eg_buf, m_buf, mt_buf, pair_s, pair_r, back_s, back_r, fin,
    series, cw, cb, mw, mb, tv, tcol, sidx, smask, cot, in_sem,
    r_ssem, r_rsem, h_ssem, h_rsem, t_ssem, t_rsem, e_ssem, e_rsem, et_ssem, et_rsem,
    l_ssem, l_rsem, lt_ssem, lt_rsem, eg_ssem, eg_rsem, m_ssem, m_rsem, mt_ssem, mt_rsem,
    pair_sem, fin_ssem, fin_rsem,
):
    me = lax.axis_index("graph")
    z = lax.axis_index("tm")
    tc, sensors = series.shape
    ch = tc // steps
    half = tc // 2
    half_s = sensors // 2
    slots = sidx.shape[1]
    halo = n_graph * slots
    tile = tv.shape[-1]
    rblocks, tslots = tcol.shape
    lblocks = sensors // tile
    hblocks = halo // tile
    wire = send.dtype
    wh = whgm.at[:, pl.ds(0, halo)]
    gm = whgm.at[:, pl.ds(halo, halo)]
    direct = fin.shape[0] > 1
    core = lax.rem(me, 2)
    mate = me + 1 - 2 * core

    def partner(off):
        if n_graph & (n_graph - 1) or n_graph > 8:
            return lax.rem(me + off, n_graph)
        p = 0
        bit = 1
        while bit < n_graph:
            p = p + lax.rem(me // bit + off // bit, 2) * bit
            bit *= 2
        return p

    er = e_part.shape[1]

    loads = [
        pltpu.make_async_copy(src, dst, in_sem.at[i])
        for i, (src, dst) in enumerate(
            ((cw_h, cw), (mw_h, mw), (cb_h, cb), (mb_h, mb), (tv_h, tv), (series_h, series),
             (sidx_h, sidx), (smask_h, smask), (cot_h, cot), (tcol_h, tcol))
        )
    ]
    for load in loads:
        load.start()
    barrier = pltpu.get_barrier_semaphore()

    def greet_graph(off):
        pl.semaphore_signal(barrier, inc=1, device_id={"graph": partner(off)}, device_id_type=MESH)

    def greet_tm(off):
        pl.semaphore_signal(barrier, inc=1, device_id={"tm": lax.rem(z + off, n_tm)}, device_id_type=MESH)

    peers(n_tm, greet_tm)
    peers(n_graph, greet_graph)

    def shift_copy(slot, src, dst, by):
        return pltpu.make_async_remote_copy(
            src_ref=src, dst_ref=dst, send_sem=t_ssem.at[slot], recv_sem=t_rsem.at[slot],
            device_id={"tm": lax.rem(z + by + n_tm, n_tm)}, device_id_type=MESH,
        )

    up = z < n_tm - 1
    down = z > 0

    firsts = [
        shift_copy(0, series_h.at[pl.ds(tc - ch, ch)], prev0.at[pl.ds(tc - ch, ch)], 1),
        shift_copy(1, series_h.at[pl.ds(tc - 3 * ch, 2 * ch)], prev0.at[pl.ds(tc - 3 * ch, 2 * ch)], 1),
    ]
    pl.semaphore_wait(barrier, n_graph - 1 + n_tm - 1)

    @pl.when(up)
    def _():
        for first in firsts:
            first.start()

    prev0[pl.ds(0, tc - 3 * ch), :] = jnp.zeros((tc - 3 * ch, sensors), BF)

    row32 = lax.broadcasted_iota(jnp.int32, (ch, tc), 0)
    lane32 = lax.broadcasted_iota(jnp.int32, (ch, tc), 1)
    spread = jnp.where(rest_of(lane32, ch) == row32, 1.0, 0.0)
    spread_b = spread.astype(BF)
    rt = lax.broadcasted_iota(jnp.int32, (tc, tc), 0)
    lt = lax.broadcasted_iota(jnp.int32, (tc, tc), 1)
    rt, lt = quot(rt, ch), quot(lt, ch)
    same = rt == lt
    late = rt >= steps // 2

    def before(d):
        return lt == rt - d

    def before_prev(d):
        return lt == rt - d + steps

    for load in loads[:4]:
        load.wait()
    taps = 2 * GATED_LAYERS
    rs = lax.broadcasted_iota(jnp.int32, (taps * ch, taps * tc), 0)
    ls = lax.broadcasted_iota(jnp.int32, (taps * ch, taps * tc), 1)
    spread_taps = jnp.where(quot(ls, tc) * ch + rest_of(ls, ch) == rs, 1.0, 0.0).astype(BF)
    def after(d):
        return rt == lt - d

    def after_prev(d):
        return rt == lt - d + steps

    cwr = dot_tn(cw[...], spread_taps)
    mwr = dot(mw[...], spread_b)

    def stack(x, base):
        return jnp.concatenate([x[base:base + ch]] * steps, axis=0)

    for l in range(GATED_LAYERS):
        d = l + 1
        for h in range(2):
            w0 = stack(cwr[:, (l * 2) * tc:(l * 2 + 1) * tc], h * ch)
            w1 = stack(cwr[:, (l * 2 + 1) * tc:(l * 2 + 2) * tc], h * ch)
            own = (jnp.where(same, w0, 0.0) + jnp.where(before(d), w1, 0.0)).astype(BF)
            band[l, pl.ds(h * tc, tc), pl.ds(0, tc)] = own
            band[l, pl.ds(h * tc, tc), pl.ds(tc, tc)] = jnp.where(before_prev(d), w1, 0.0).astype(BF)
            if l == 0:
                band_h[pl.ds(h * tc, tc), :] = jnp.concatenate([own[half:], own[half:]], axis=0)
        for k in range(HOPS):
            mk = stack(mwr, (l * HOPS + k) * ch)
            mixall[l, :, pl.ds(k * tc, tc)] = jnp.where(same, mk, 0.0).astype(BF)
            if l == 0:
                at = (rt == lt + steps // 2) if k in (1, 2) else (same & late)
                mix_h[:, pl.ds(k * tc, tc)] = jnp.where(at, mk, 0.0).astype(BF)

    r64 = lax.broadcasted_iota(jnp.int32, (2 * ch, 2 * tc), 0)
    l64 = lax.broadcasted_iota(jnp.int32, (2 * ch, 2 * tc), 1)
    spread2 = jnp.where(rest_of(l64, ch) + quot(l64, tc) * ch == r64, 1.0, 0.0)
    cbias = lax.dot_general(cb[...], spread2, (((1,), (0,)), ((), ())), precision=lax.Precision.HIGHEST, preferred_element_type=F32)
    mbias = lax.dot_general(mb[...], spread, (((1,), (0,)), ((), ())), precision=lax.Precision.HIGHEST, preferred_element_type=F32)

    for load in loads[4:]:
        load.wait()
    def on(r, k, c):
        return (tcol[r, k] == c).astype(jnp.int32).astype(F32)

    def placed(blocks, r, c):
        y = blocks[0] * on(r, 0, c)
        for k in range(1, tslots):
            y = y + blocks[k] * on(r, k, c)
        return y.astype(BF)

    def flipped(r):
        return [tv[r * tslots + k].astype(F32).T for k in range(tslots)]

    for r in range(rblocks):
        flips = flipped(r)
        for c in range(hblocks):
            wht[pl.ds(c * tile, tile), pl.ds(r * tile, tile)] = placed(flips, r, lblocks + c)

    def build_rest():
        for r in range(rblocks):
            tiles = [tv[r * tslots + k].astype(F32) for k in range(tslots)]
            flips = flipped(r)
            for c in range(lblocks):
                wl[pl.ds(r * tile, tile), pl.ds(c * tile, tile)] = placed(tiles, r, c)
                wlt[pl.ds(c * tile, tile), pl.ds(r * tile, tile)] = placed(flips, r, c)
            for c in range(hblocks):
                wh[pl.ds(r * tile, tile), pl.ds(c * tile, tile)] = placed(tiles, r, lblocks + c)

    key = jnp.where(smask[...] != 0, sidx[...] + 1, 0)
    es = lax.broadcasted_iota(jnp.int32, (slots, halo), 0)
    ej = lax.broadcasted_iota(jnp.int32, (slots, halo), 1)
    pick = jnp.where(rest_of(ej, slots) == es, 1.0, 0.0).astype(BF)
    hi = dot((key >> 5).astype(F32).astype(BF), pick)
    lo = dot((key & 31).astype(F32).astype(BF), pick)
    pr = lax.broadcasted_iota(jnp.int32, (n_graph, halo), 0)
    pj = quot(lax.broadcasted_iota(jnp.int32, (n_graph, halo), 1), slots)
    keys = jnp.sum(jnp.where(pr == pj, hi * 32.0 + lo, 0.0), axis=0, keepdims=True)
    ids = lax.broadcasted_iota(jnp.int32, (sensors, halo), 0).astype(F32) + 1.0
    onehot = jnp.where(ids == keys, 1.0, 0.0)
    gm[...] = onehot.astype(BF)
    gmt[...] = onehot.T.astype(BF)

    def graph_copy(src, dst, ssem, rsem, p):
        return pltpu.make_async_remote_copy(
            src_ref=src, dst_ref=dst, send_sem=ssem, recv_sem=rsem,
            device_id={"graph": p}, device_id_type=MESH,
        )

    def tm_copy(src, dst, ssem, rsem, p):
        return pltpu.make_async_remote_copy(
            src_ref=src, dst_ref=dst, send_sem=ssem, recv_sem=rsem,
            device_id={"tm": p}, device_id_type=MESH,
        )

    lane_low = lax.broadcasted_iota(jnp.int32, (halo, tc), 1) < half

    def ship(blocks, out_buf, in_buf, ssem, rsem, r):
        for i, block in enumerate(blocks):
            out_buf[r, :, i] = block.astype(BF).reshape(n_graph, slots, tc).astype(wire)

        def go(off):
            p = partner(off)
            graph_copy(out_buf.at[r, p], in_buf.at[r, me], ssem.at[r, p], rsem.at[r], p).start()

        peers(n_graph, go)
        in_buf[r, me] = out_buf[r, me]

    def collect(in_buf, ssem, rsem, r, count):
        arrived = in_buf.at[r, pl.ds(0, n_graph - 1)]
        graph_copy(arrived, arrived, ssem.at[r, 0], rsem.at[r], partner(1)).wait_recv()
        return [in_buf[r, :, i].reshape(halo, tc).astype(BF) for i in range(count)]

    def launch(r, pull_in, push_in):
        ship((dot(gmt[...], pull_in), dot(wht[...], push_in)), send, recv, r_ssem, r_rsem, r)

    def ship_h(r, sp, sb):
        ship((jnp.where(lane_low, sp, sb),), send_h, recv_h, h_ssem, h_rsem, r)

    def local(pull_in, push_in):
        return dot(wl[...], pull_in), dot(wlt[...], push_in)

    def land(r):
        return collect(recv, r_ssem, r_rsem, r, 2)

    def land_h(r):
        return collect(recv_h, h_ssem, h_rsem, r, 1)[0]

    def beside(rp, rb, both):
        return jnp.concatenate([rp, both], axis=1), jnp.concatenate([rb, both], axis=1)

    def relay(r, rp, rb, sp, sb):
        ship((sp + dot(gwh[...], rp), sb + dot(whg[...], rb)), send, recv, r_ssem, r_rsem, r)

    def joined(a, b):
        return dot(whgm[...], jnp.concatenate([a, b], axis=0))

    def whole(pulled, pushed, rp, rb):
        return pulled + dot(wh[...], rp), pushed + dot(gm[...], rb)

    lane_half = lax.broadcasted_iota(jnp.int32, (half_s, tc), 1) < half

    def pack(x):
        return jnp.where(lane_half, pltpu.roll(x[:half_s], half, 1), x[half_s:]).astype(BF)

    def unpack(p):
        x = p.astype(F32)
        return jnp.concatenate([pltpu.roll(x, half, 1), x], axis=0)

    lane_g = quot(lax.broadcasted_iota(jnp.int32, (ch, tc), 1), ch)

    def fold(x):
        y = x[0:ch]
        for t in range(1, steps):
            y = y + x[t * ch:(t + 1) * ch]
        sh = ch
        while sh < tc:
            y = y + pltpu.roll(y, sh, 1)
            sh *= 2
        return y

    def lanes_of(xs):
        y = jnp.zeros((ch, tc), F32)
        for g, x in enumerate(xs):
            y = jnp.where(lane_g == g, x, y)
        return y

    def gather_start(buf, ssem, rsem, count, here, copy):
        def go(off):
            p = lax.rem(here + off, count)
            copy(buf.at[here], buf.at[here], ssem.at[p], rsem.at[here], p).start()

        peers(count, go)

    def gather_sum(buf, ssem, rsem, count, here, copy):
        def take(off):
            p = lax.rem(here + off, count)
            copy(buf.at[p], buf.at[p], ssem.at[p], rsem.at[p], p).wait_recv()

        peers(count, take)
        total = buf[0].astype(F32)
        for p in range(1, count):
            total = total + buf[p].astype(F32)
        return total

    def hop_grad(fr, l, k):
        return dot(fr, mixall[l, :, pl.ds(k * tc, tc)])

    def mix_fold(l, fr, ks):
        folds = []
        for k in ks:
            hop = hops[l, :, pl.ds(k * tc, tc)]
            folds.append(fold(jnp.where(same, dot(cot[...], hop) if l == 1 else dot_tn(fr, hop), 0.0)))
        return folds

    def conv_fold(l, gp):
        d = l + 1
        if l == 0:
            prod = (dot(series[...], gp), dot(prev0[...], gp))
        else:
            prod = [dot_tn(ext[l, :, pl.ds(i * tc, tc)], gp) for i in range(2)]
        pieces = []
        for tap in range(2):
            for h in range(2):
                own = prod[0][:, h * tc:(h + 1) * tc]
                if tap == 0:
                    x = jnp.where(same, own, 0.0)
                else:
                    x = jnp.where(after(d), own, 0.0) + jnp.where(after_prev(d), prod[1][:, h * tc:(h + 1) * tc], 0.0)
                pieces.append(fold(x))
        return lanes_of(pieces)

    def pre_grad(l, gg):
        f = filt[l]
        g = gate[l]
        return jnp.concatenate([gg * g * (1.0 - f * f), gg * f * g * (1.0 - g)], axis=1).astype(BF)

    def lag_pack(i, l, gp):
        pack_s[i] = pack(dot(gp, band[l, :, pl.ds(tc, tc)]))

    def lag_start(i):
        @pl.when(down)
        def _():
            shift_copy(2 + i, pack_s.at[i], pack_r.at[i], -1).start()

    lanes_late = lax.broadcasted_iota(jnp.int32, (sensors, tc), 1) >= half

    def lag_take(i):
        @pl.when(up)
        def _():
            shift_copy(2 + i, pack_s.at[i], pack_r.at[i], -1).wait_recv()

        @pl.when(jnp.logical_not(up))
        def _():
            pack_r[i] = jnp.zeros((half_s, tc), BF)

        return jnp.where(lanes_late, unpack(pack_r[i]), 0.0)

    flow[...] = cot[...].astype(F32).T
    fr1 = flow[...].astype(BF)
    h4, h2 = hop_grad(fr1, 1, 4).astype(BF), hop_grad(fr1, 1, 2).astype(BF)
    launch(0, h4, h2)

    def mid_back(fr, l, pull_in, push_in):
        pulled, pushed = local(pull_in, push_in)
        pulled = pulled + hop_grad(fr, l, 3)
        pushed = pushed + hop_grad(fr, l, 1)
        sp = dot(gwl[...], pull_in) + hop_grad(dot(gmt[...], fr).astype(BF), l, 3)
        return pulled, pushed, sp, dot(wht[...], pushed.astype(BF))

    def mid(pull_in, push_in):
        pulled, pushed = local(pull_in, push_in)
        return pulled, pushed, dot(gwl[...], pull_in), dot(wht[...], pushed.astype(BF))

    ext[0, :, pl.ds(0, tc)] = series[...].astype(F32).T.astype(BF)
    pre_own = dot_nt(ext[0, :, pl.ds(0, tc)], band[0, :, pl.ds(0, tc)]) + cbias[0:1]

    def halo_take(i, lo, n):
        @pl.when(down)
        def _():
            firsts[i].wait_recv()

        @pl.when(jnp.logical_not(down))
        def _():
            prev0[pl.ds(lo, n), :] = jnp.zeros((n, sensors), BF)

    halo_take(0, tc - ch, ch)
    newest = prev0[pl.ds(tc - ch, ch), :].astype(F32).T.astype(BF)
    pre = pre_own + dot_nt(newest, band[0, :, pl.ds(tc, tc)][:, tc - ch:])
    f = jnp.tanh(pre[:, :tc])
    g = sigmoid(pre[:, tc:])
    gated = (f * g).astype(BF)
    launch(6, gated, gated)
    filt[0] = f
    gate[0] = g

    halo_take(1, tc - 3 * ch, 2 * ch)
    ext[0, :, pl.ds(tc, tc)] = prev0[...].astype(F32).T.astype(BF)
    pre = dot_nt(ext[0, :, pl.ds(tc, tc)], band_h[...]) + cbias[0:1]
    gated_h = (jnp.tanh(pre[:, :tc]) * sigmoid(pre[:, tc:])).astype(BF)
    ship_h(0, dot(gmt[...], gated_h), dot(wht[...], gated_h))
    both = jnp.concatenate([gated, gated_h], axis=1)

    def keep(k, x):
        hops[0, :, pl.ds(k * tc, tc)] = x[:, :tc]
        hops_h[:, pl.ds(k * tc, tc)] = x[:, tc:]

    keep(0, both)
    build_rest()
    gwl[...] = dot(gmt[...], wl[...]).astype(BF)
    gwh[...] = dot(gmt[...], wh[...]).astype(BF)
    whg[...] = dot(wht[...], gm[...]).astype(BF)
    ab = mid_back(fr1, 1, h4, h2)
    af = mid(both, both)

    rp0, rb0 = land(0)
    relay(1, rp0, rb0, *ab[2:])

    rp, rb = land(6)
    relay(7, rp, rb, af[2][:, :tc], af[3][:, :tc])
    both = land_h(0)
    ship_h(1, af[2][:, tc:] + dot(gwh[...], both), af[3][:, tc:] + dot(whg[...], both))
    rp, rb = beside(rp, rb, both)
    bi, fi = whole(*ab[:2], rp0, rb0)
    bb = local(bi.astype(BF), fi.astype(BF))
    gg0 = hop_grad(fr1, 1, 0)
    fo, bo = whole(*af[:2], rp, rb)
    fo, bo = fo.astype(BF), bo.astype(BF)
    keep(1, fo)
    keep(3, bo)
    bf = local(fo, bo)

    def mix_three(mat, hop):
        m = dot_nt(hop(0, 2), mat(0, 2))
        return m + dot_nt(hop(3, 1), mat(3, 1))

    def mat_of(l):
        return lambda k, n: mixall[l, :, pl.ds(k * tc, n * tc)]

    def hop_of(l):
        return lambda k, n: hops[l, :, pl.ds(k * tc, n * tc)]

    part = mix_three(mat_of(0), hop_of(0))
    part_h = mix_three(
        lambda k, n: mix_h[:, pl.ds(k * tc, n * tc)], lambda k, n: hops_h[:, pl.ds(k * tc, n * tc)]
    )

    gg1 = gg0 + bb[0] + bb[1]
    gg1 = gg1 + joined(*land(1))

    def two_late(a, b):
        e = dot_nt(a[:, :tc], mixall[0, :, pl.ds(2 * tc, tc)]), dot_nt(b[:, :tc], mixall[0, :, pl.ds(4 * tc, tc)])
        h = dot_nt(a[:, tc:], mix_h[:, pl.ds(2 * tc, tc)]), dot_nt(b[:, tc:], mix_h[:, pl.ds(4 * tc, tc)])
        return [jnp.concatenate([x, y], axis=1) for x, y in zip(e, h)]

    known = two_late(bf[0].astype(BF), bf[1].astype(BF))
    mbias2 = jnp.concatenate([mbias[0:1], mbias[0:1]], axis=1)
    hid = ext[0].astype(F32) + mbias2 + jnp.concatenate([part, part_h], axis=1) + known[0] + known[1]

    rp, rb = beside(*land(7), land_h(1))
    hid = hid + joined(*[x.astype(BF) for x in two_late(rp, rb)])
    lane2 = lax.broadcasted_iota(jnp.int32, (sensors, 2 * tc), 1)
    ext[1] = jnp.where((lane2 < tc) | ((lane2 >= tc + half) & down), hid, 0.0).astype(BF)

    pre = dot_nt(ext[1], band[1]) + cbias[1:2]
    f = jnp.tanh(pre[:, :tc])
    g = sigmoid(pre[:, tc:])
    filt[1] = f
    gate[1] = g
    gp1 = pre_grad(1, gg1)
    lag_pack(0, 1, gp1)
    lag_start(0)
    gated = (f * g).astype(BF)
    hops[1, :, pl.ds(0, tc)] = gated
    launch(2, gated, gated)
    f2, b2 = whole(bf[0][:, :tc], bf[1][:, :tc], rp[:, :tc], rb[:, :tc])
    hops[0, :, pl.ds(2 * tc, tc)] = f2.astype(BF)
    hops[0, :, pl.ds(4 * tc, tc)] = b2.astype(BF)
    cf = mid(gated, gated)
    new = flow[...] + dot(gp1, band[1, :, pl.ds(0, tc)])
    conv1 = conv_fold(1, gp1)

    flow[...] = new + lag_take(0)
    fr0 = flow[...].astype(BF)
    h4, h2 = hop_grad(fr0, 0, 4).astype(BF), hop_grad(fr0, 0, 2).astype(BF)
    launch(4, h4, h2)
    rp, rb = land(2)
    relay(3, rp, rb, *cf[2:])
    fo, bo = whole(*cf[:2], rp, rb)
    fo, bo = fo.astype(BF), bo.astype(BF)
    hops[1, :, pl.ds(tc, tc)] = fo
    hops[1, :, pl.ds(3 * tc, tc)] = bo
    mix0 = mix_fold(0, fr0, range(HOPS))
    mix1 = mix_fold(1, fr1, (0, 1, 3))
    early = jnp.concatenate([conv1, lanes_of(mix0[:4]), lanes_of([mix0[4]] + mix1)], axis=0)
    for p in range(n_graph):
        e_part[p] = early[p * er:(p + 1) * er]

    def scatter(off):
        p = partner(off)
        graph_copy(e_part.at[p], e_buf.at[me], e_ssem.at[p], e_rsem.at[me], p).start()

    peers(n_graph, scatter)
    e_buf[me] = e_part[me]
    cb_ = mid_back(fr0, 0, h4, h2)
    df = local(fo, bo)
    gg0 = hop_grad(fr0, 0, 0)
    part = mix_three(mat_of(1), hop_of(1))

    rp, rb = land(4)
    relay(5, rp, rb, *cb_[2:])
    bi, fi = whole(*cb_[:2], rp, rb)
    db = local(bi.astype(BF), fi.astype(BF))
    et_buf[z] = gather_sum(e_buf, e_ssem, e_rsem, n_graph, me, graph_copy)
    gather_start(et_buf, et_ssem, et_rsem, n_tm, z, tm_copy)

    f2, b2 = whole(*df, *land(3))
    f2, b2 = f2.astype(BF), b2.astype(BF)
    hops[1, :, pl.ds(2 * tc, tc)] = f2
    hops[1, :, pl.ds(4 * tc, tc)] = b2
    a2, a4 = mix_fold(1, fr1, (2, 4))
    hc = ch // 2
    last = jnp.zeros((hc, tc), F32)
    for g, x in enumerate((a2[:hc], a4[:hc], a2[hc:], a4[hc:])):
        last = jnp.where(lane_g[:hc] == g, x, last)
    m_buf[me] = last.astype(BF)
    gather_start(m_buf, m_ssem, m_rsem, n_graph, me, graph_copy)
    mixed = part + dot_nt(f2, mixall[1, :, pl.ds(2 * tc, tc)]) + dot_nt(b2, mixall[1, :, pl.ds(4 * tc, tc)])
    out[...] = (ext[1, :, pl.ds(0, tc)].astype(F32) + (mixed + mbias[1:2])).T.astype(BF)

    gg0 = gg0 + db[0] + db[1]
    gp0 = pre_grad(0, gg0 + joined(*land(5)))
    conv0 = conv_fold(0, gp0)
    if direct:
        swap = graph_copy(pair_s, pair_r, pair_sem.at[0], pair_sem.at[1], mate)
        low = core == 0
        pair_s[...] = jnp.where(low, conv0[hc:], conv0[:hc])
        swap.start()
    else:
        l_buf[me] = conv0
        gather_start(l_buf, l_ssem, l_rsem, n_graph, me, graph_copy)

    lag_pack(1, 0, gp0)
    here = (z * n_graph + me) // 2

    def final_copy(goff, toff):
        p = partner(goff) if goff else me
        return pltpu.make_async_remote_copy(
            src_ref=fin.at[here], dst_ref=fin.at[here],
            send_sem=fin_ssem.at[toff * n_graph + goff], recv_sem=fin_rsem.at[0],
            device_id={"graph": p, "tm": lax.rem(z + toff, n_tm)}, device_id_type=MESH,
        )

    others = [(g, t) for t in range(n_tm) for g in range(0, n_graph, 2) if (g, t) != (0, 0)] if direct else []
    if direct:
        swap.wait_recv()
        fin[here] = (jnp.where(low, conv0[:hc], conv0[hc:]) + pair_r[...]).astype(BF)
        for g, t in others:
            final_copy(g, t).start()
    lag_start(1)
    mt_buf[z] = gather_sum(m_buf, m_ssem, m_rsem, n_graph, me, graph_copy).astype(BF)
    gather_start(mt_buf, mt_ssem, mt_rsem, n_tm, z, tm_copy)
    eg_buf[me] = gather_sum(et_buf, et_ssem, et_rsem, n_tm, z, tm_copy)
    gather_start(eg_buf, eg_ssem, eg_rsem, n_graph, me, graph_copy)
    if not direct:
        lt_buf[z] = gather_sum(l_buf, l_ssem, l_rsem, n_graph, me, graph_copy)
        gather_start(lt_buf, lt_ssem, lt_rsem, n_tm, z, tm_copy)
    new = flow[...] + dot(gp0, band[0, :, pl.ds(0, tc)])
    def lane_group(x, g):
        return (pltpu.roll(x, tc - g * ch, 1) if g else x)[:, :ch]

    def put_conv(l, x):
        gconv[l, 0] = x[:, :2 * ch]
        gconv[l, 1] = pltpu.roll(x, tc - 2 * ch, 1)[:, :2 * ch]

    def sent_early(off):
        p = partner(off)
        for r in range(send.shape[0]):
            graph_copy(send.at[r, p], recv.at[r, me], r_ssem.at[r, p], r_rsem.at[r], p).wait_send()
        for r in range(send_h.shape[0]):
            graph_copy(send_h.at[r, p], recv_h.at[r, me], h_ssem.at[r, p], h_rsem.at[r], p).wait_send()
        graph_copy(e_part.at[p], e_buf.at[me], e_ssem.at[p], e_rsem.at[me], p).wait_send()
        graph_copy(m_buf.at[me], m_buf.at[me], m_ssem.at[p], m_rsem.at[me], p).wait_send()

    peers(n_graph, sent_early)

    if direct:
        count = fin.shape[0]
        arrived = fin.at[pl.ds(0, count - 1)]
        pltpu.make_async_remote_copy(
            src_ref=arrived, dst_ref=arrived, send_sem=fin_ssem.at[2], recv_sem=fin_rsem.at[0],
            device_id={"graph": mate}, device_id_type=MESH,
        ).wait_recv()
        total = fin[0].astype(F32)
        for p in range(1, count):
            total = total + fin[p].astype(F32)
        back_s[...] = total
        back = graph_copy(back_s, back_r, pair_sem.at[2], pair_sem.at[3], mate)
        back.start()
    gser[...] = (new + lag_take(1)).T.astype(BF)
    m = gather_sum(mt_buf, mt_ssem, mt_rsem, n_tm, z, tm_copy) * scale
    for i, k in enumerate((2, 4)):
        gmix[1, k, pl.ds(0, hc)] = lane_group(m, i)
        gmix[1, k, pl.ds(hc, hc)] = lane_group(m, i + 2)

    def take_group(off):
        p = partner(off)
        graph_copy(eg_buf.at[p], eg_buf.at[p], eg_ssem.at[p], eg_rsem.at[p], p).wait_recv()

    peers(n_graph, take_group)
    e = jnp.concatenate([eg_buf[p] for p in range(n_graph)], axis=0) * scale
    put_conv(1, e[:ch])
    for k in range(4):
        gmix[0, k] = lane_group(e[ch:2 * ch], k)
    gmix[0, 4] = lane_group(e[2 * ch:], 0)
    for i, k in enumerate((0, 1, 3)):
        gmix[1, k] = lane_group(e[2 * ch:], i + 1)
    if direct:
        back.wait_recv()
        theirs = back_r[...]
        halves = [jnp.where(low, total, theirs), jnp.where(low, theirs, total)]
        put_conv(0, jnp.concatenate(halves, axis=0) * scale)
        back.wait_send()
        swap.wait_send()
        for g, t in others:
            final_copy(g, t).wait_send()
    else:
        put_conv(0, gather_sum(lt_buf, lt_ssem, lt_rsem, n_tm, z, tm_copy) * scale)

    def sent_graph(off):
        p = partner(off)
        graph_copy(eg_buf.at[me], eg_buf.at[me], eg_ssem.at[p], eg_rsem.at[me], p).wait_send()
        if not direct:
            graph_copy(l_buf.at[me], l_buf.at[me], l_ssem.at[p], l_rsem.at[me], p).wait_send()

    peers(n_graph, sent_graph)

    def sent_tm(off):
        p = lax.rem(z + off, n_tm)
        tm_copy(et_buf.at[z], et_buf.at[z], et_ssem.at[p], et_rsem.at[z], p).wait_send()
        tm_copy(mt_buf.at[z], mt_buf.at[z], mt_ssem.at[p], mt_rsem.at[z], p).wait_send()
        if not direct:
            tm_copy(lt_buf.at[z], lt_buf.at[z], lt_ssem.at[p], lt_rsem.at[z], p).wait_send()

    peers(n_tm, sent_tm)

    @pl.when(up)
    def _():
        for first in firsts:
            first.wait_send()

    @pl.when(down)
    def _():
        shift_copy(2, pack_s.at[0], pack_r.at[0], -1).wait_send()
        shift_copy(3, pack_s.at[1], pack_r.at[1], -1).wait_send()


def store_kernel(a, b, c, d, ao, bo, co, do, sem):
    copies = [
        pltpu.make_async_copy(src, dst, sem.at[i])
        for i, (src, dst) in enumerate(((a, ao), (b, bo), (c, co), (d, do)))
    ]
    for copy in copies:
        copy.start()
    for copy in copies:
        copy.wait()


def per_device(series, cw, cb, mw, mb, tv, tcol, sidx, smask, cot):
    n_graph = lax.axis_size("graph")
    n_tm = lax.axis_size("tm")
    steps, ch, sensors = series.shape
    tc = steps * ch
    slots = sidx.shape[2]
    halo = n_graph * slots
    wire = BF if slots % 16 == 0 else F32
    narrow, wide = 8, 2
    scale = 1.0 / math.sqrt(float(steps * n_tm * sensors * n_graph))
    vm = pl.BlockSpec(memory_space=pltpu.VMEM)
    hb = pl.BlockSpec(memory_space=pltpu.HBM)
    cwt_shape = (*cw.shape[:2], cw.shape[3], cw.shape[2])
    ins = (
        series.reshape(tc, sensors),
        jnp.swapaxes(cw, 2, 3).reshape(-1, cw.shape[2]),
        cb,
        mw.reshape(-1, ch),
        mb,
        tv.reshape(-1, *tv.shape[2:]),
        tcol,
        sidx[0],
        smask[0],
        cot.reshape(tc, sensors),
    )
    er = 3 * ch // n_graph
    direct = n_graph % 2 == 0 and n_graph * n_tm <= 32 and ch % 32 == 0
    n_all = n_graph * n_tm if direct else 1
    ins = tuple(pltpu.with_memory_space_constraint(x, pltpu.HBM) for x in ins)
    dma = pltpu.SemaphoreType.DMA
    out, gser, gconv, gmix = pl.pallas_call(
        functools.partial(kernel, n_graph, n_tm, steps, scale),
        out_shape=(
            pltpu.VMEM((tc, sensors), BF),
            pltpu.VMEM((tc, sensors), BF),
            pltpu.VMEM(cwt_shape, F32),
            pltpu.VMEM(mw.shape, F32),
        ),
        in_specs=[hb] * 10,
        out_specs=(vm,) * 4,
        scratch_shapes=[
            pltpu.VMEM((sensors, sensors), BF),
            pltpu.VMEM((sensors, sensors), BF),
            pltpu.VMEM((sensors, 2 * halo), BF),
            pltpu.VMEM((halo, sensors), BF),
            pltpu.VMEM((halo, sensors), BF),
            pltpu.VMEM((halo, sensors), BF),
            pltpu.VMEM((halo, halo), BF),
            pltpu.VMEM((halo, halo), BF),
            pltpu.VMEM((GATED_LAYERS, 2 * tc, 2 * tc), BF),
            pltpu.VMEM((2 * tc, tc), BF),
            pltpu.VMEM((GATED_LAYERS, tc, HOPS * tc), BF),
            pltpu.VMEM((tc, HOPS * tc), BF),
            pltpu.VMEM((GATED_LAYERS, sensors, 2 * tc), BF),
            pltpu.VMEM((GATED_LAYERS, sensors, HOPS * tc), BF),
            pltpu.VMEM((sensors, HOPS * tc), BF),
            pltpu.VMEM((GATED_LAYERS, sensors, tc), F32),
            pltpu.VMEM((GATED_LAYERS, sensors, tc), F32),
            pltpu.VMEM((sensors, tc), F32),
            pltpu.VMEM((tc, sensors), BF),
            pltpu.VMEM((2, sensors // 2, tc), BF),
            pltpu.VMEM((2, sensors // 2, tc), BF),
            pltpu.VMEM((narrow, n_graph, 2, slots, tc), wire),
            pltpu.VMEM((narrow, n_graph, 2, slots, tc), wire),
            pltpu.VMEM((wide, n_graph, 1, slots, tc), wire),
            pltpu.VMEM((wide, n_graph, 1, slots, tc), wire),
            pltpu.VMEM((n_graph, er, tc), F32),
            pltpu.VMEM((n_tm, er, tc), F32),
            pltpu.VMEM((n_graph, ch, tc), F32),
            pltpu.VMEM((n_tm, ch, tc), F32),
            pltpu.VMEM((n_graph, er, tc), F32),
            pltpu.VMEM((n_graph, er, tc), F32),
            pltpu.VMEM((n_graph, ch // 2, tc), BF),
            pltpu.VMEM((n_tm, ch // 2, tc), BF),
            *[pltpu.VMEM((ch // 2, tc), F32)] * 4,
            pltpu.VMEM((max(n_all // 2, 1), ch // 2, tc), BF),
            *[(pltpu.SMEM if x.shape == tcol.shape else pltpu.VMEM)(x.shape, x.dtype) for x in ins],
            dma((10,)),
            dma((narrow, n_graph)), dma((narrow,)),
            dma((wide, n_graph)), dma((wide,)),
            dma((4,)), dma((4,)),
            dma((n_graph,)), dma((n_graph,)),
            dma((n_tm,)), dma((n_tm,)),
            dma((n_graph,)), dma((n_graph,)),
            dma((n_tm,)), dma((n_tm,)),
            dma((n_graph,)), dma((n_graph,)),
            dma((n_graph,)), dma((n_graph,)),
            dma((n_tm,)), dma((n_tm,)),
            dma((4,)), dma((n_all,)), dma((1,)),
        ],
        compiler_params=pltpu.CompilerParams(
            collective_id=0, has_side_effects=True, vmem_limit_bytes=48 * 1024 * 1024
        ),
    )(*ins)
    results = tuple(pltpu.with_memory_space_constraint(x, pltpu.VMEM) for x in (out, gser, gconv, gmix))
    out, gser, gconv, gmix = pl.pallas_call(
        store_kernel,
        out_shape=tuple(pltpu.HBM(x.shape, x.dtype) for x in results),
        in_specs=[vm] * 4,
        out_specs=(hb,) * 4,
        scratch_shapes=[dma((4,))],
        compiler_params=pltpu.CompilerParams(vmem_limit_bytes=4 * 1024 * 1024),
    )(*results)
    gconv = jnp.swapaxes(gconv, 2, 3)
    return out.reshape(series.shape), gser.reshape(series.shape), gconv, gmix


def solution(mesh):
    return jax.shard_map(
        per_device,
        mesh=mesh,
        in_specs=(
            P("tm", None, "graph"),
            P(),
            P(),
            P(),
            P(),
            P("graph", None, None, None),
            P("graph", None),
            P("graph", None, None),
            P("graph", None, None),
            P("tm", None, "graph"),
        ),
        out_specs=(P("tm", None, "graph"), P("tm", None, "graph"), P(), P()),
        check_vma=False,
    )
```
